512 devices in a mesh: gx: 32 (over y, x), gy: 16 (over z, core).
Axes of the slice: x: 4, y: 8, z: 8, core: 2. Of those that a mesh axis runs over, the one named last changes fastest.
Arguments:
- right_side: float32 [128, 128, 512], P('gx', 'gy'), may hold values from -18 to 18
- labels: int32 [128, 128, 512], P('gx', 'gy'), may hold values from 0 to 2
- conduct_table: float32 [3], replicated, may hold values from 0.2 to 5
Outputs:
- correction: float32 [128, 128, 512], P('gx', 'gy')
The draws below stay inside these ranges and needn't reach their ends.
All inputs are finite; a program needn't handle non-finite values.
Results may differ from the reference program's by a relative error of at most 0.0003.
Values sent between devices are 32-bit elements; how exact they have to be, the bound alone decides.
No kernel may reach another device: no remote copies, remote signals or barrier semaphores. Data moves between devices by JAX's collectives and lax.ppermute only.
A program may use at most 128 MiB of HBM per device.

```python
import math
import jax
import jax.numpy as jnp

NZ = 512
SWEEPS = 8
NX = 128
NY = 128


def draw_right_side(key, part):
    shape = (NX, NY, NZ)
    return jnp.clip(3.0 * jax.random.normal(key, shape, jnp.float32), -18.0, 18.0)


def set_ends(result, own_key, smallest, top_value):
    longest = result.shape.index(max(result.shape))
    spots = []
    for shift in (0, 1):
        where = [jax.random.randint(jax.random.fold_in(own_key, axis), (), 0, length) for axis, length in enumerate(result.shape)]
        where[longest] = (where[longest] + shift) % result.shape[longest]
        spots.append(tuple(where))
    return result.at[spots[0]].set(smallest).at[spots[1]].set(top_value)


def setup_inputs(seed: int = 0) -> dict:
    key_of = jax.random.split(jax.random.key(seed), 4)
    right_side = draw_right_side(jax.random.fold_in(key_of[3], 71), 0)
    labels = set_ends(jax.random.randint(key_of[1], (NX, NY, NZ), 0, 3), jax.random.fold_in(key_of[1], 1), 0, 2).astype(jnp.int32)
    conduct_table = jnp.clip(jnp.exp(jax.random.uniform(key_of[2], (3,), jnp.float32, math.log(0.2), math.log(5.0))), 0.2, 5.0)
    return {"right_side": right_side, "labels": labels, "conduct_table": conduct_table}


OMEGA = 0.8


def lookup(labels, table):
    return jnp.where(labels == 0, table[0], jnp.where(labels == 1, table[1], table[2]))


def face_couplings(padded):
    own = padded[1:-1, 1:-1, 1:-1]
    own = jnp.where(own > 0.0, own, 1.0)

    def across(beside):
        beside = jnp.where(beside > 0.0, beside, own)
        return 2.0 * (own * beside) / (own + beside)

    return jnp.stack([across(padded[:-2, 1:-1, 1:-1]), across(padded[2:, 1:-1, 1:-1]),
                      across(padded[1:-1, :-2, 1:-1]), across(padded[1:-1, 2:, 1:-1]),
                      across(padded[1:-1, 1:-1, :-2]), across(padded[1:-1, 1:-1, 2:])])


def coupled(couplings, padded):
    total = couplings[0] * padded[:-2, 1:-1, 1:-1] + couplings[1] * padded[2:, 1:-1, 1:-1]
    total = total + couplings[2] * padded[1:-1, :-2, 1:-1] + couplings[3] * padded[1:-1, 2:, 1:-1]
    total = total + couplings[4] * padded[1:-1, 1:-1, :-2] + couplings[5] * padded[1:-1, 1:-1, 2:]
    return total


def relax(couplings, diagonal, source, field, padded):
    image = diagonal * field - coupled(couplings, padded)
    return field + OMEGA * (source - image) / diagonal


def residual_of(couplings, diagonal, source, field, padded):
    return source - (diagonal * field - coupled(couplings, padded))


def coarsen_couplings(couplings):
    extent = couplings.shape
    blocks = couplings.reshape(6, extent[1] // 2, 2, extent[2] // 2, 2, extent[3] // 2, 2)
    lower_one = jnp.sum(blocks[0][:, 0], axis=(2, 4))
    upper_one = jnp.sum(blocks[1][:, 1], axis=(2, 4))
    lower_two = jnp.sum(blocks[2][:, :, :, 0], axis=(1, 4))
    upper_two = jnp.sum(blocks[3][:, :, :, 1], axis=(1, 4))
    lower_three = jnp.sum(blocks[4][..., 0], axis=(1, 3))
    upper_three = jnp.sum(blocks[5][..., 1], axis=(1, 3))
    return jnp.stack([lower_one, upper_one, lower_two, upper_two, lower_three, upper_three])


def restrict(field):
    extent = field.shape
    return jnp.sum(field.reshape(extent[0] // 2, 2, extent[1] // 2, 2, extent[2] // 2, 2), axis=(1, 3, 5))


def prolong(field):
    extent = field.shape
    spread = jnp.broadcast_to(field[:, None, :, None, :, None], (extent[0], 2, extent[1], 2, extent[2], 2))
    return spread.reshape(2 * extent[0], 2 * extent[1], 2 * extent[2])


def smooth(couplings, diagonal, source, field, count):
    for repeat in range(count):
        field = relax(couplings, diagonal, source, field, jnp.pad(field, 1))
    return field


def reference(right_side, labels, conduct_table):
    conduct = lookup(labels, conduct_table)
    fine_couplings = face_couplings(jnp.pad(conduct, 1))
    fine_diagonal = jnp.sum(fine_couplings, axis=0)
    fine_iterate = smooth(fine_couplings, fine_diagonal, right_side, jnp.zeros_like(right_side), 2)
    fine_residual = residual_of(fine_couplings, fine_diagonal, right_side, fine_iterate, jnp.pad(fine_iterate, 1))
    middle_source = restrict(fine_residual)
    middle_couplings = coarsen_couplings(fine_couplings)
    middle_diagonal = jnp.sum(middle_couplings, axis=0)
    middle_iterate = smooth(middle_couplings, middle_diagonal, middle_source, jnp.zeros_like(middle_source), 2)
    middle_residual = residual_of(middle_couplings, middle_diagonal, middle_source, middle_iterate, jnp.pad(middle_iterate, 1))
    coarse_source = restrict(middle_residual)
    coarse_couplings = coarsen_couplings(middle_couplings)
    coarse_diagonal = jnp.sum(coarse_couplings, axis=0)
    coarse_iterate = smooth(coarse_couplings, coarse_diagonal, coarse_source, jnp.zeros_like(coarse_source), SWEEPS)
    middle_iterate = middle_iterate + prolong(coarse_iterate)
    middle_iterate = smooth(middle_couplings, middle_diagonal, middle_source, middle_iterate, 1)
    fine_iterate = fine_iterate + prolong(middle_iterate)
    return smooth(fine_couplings, fine_diagonal, right_side, fine_iterate, 1)
```

```python
import jax
import jax.numpy as jnp
from jax import lax
from jax.experimental import pallas as pl
from jax.experimental.pallas import tpu as pltpu
from jax.sharding import PartitionSpec as P

F32 = jnp.float32
LANES = 128
ROWS = 24
REACH = 7
PLANES = 4 + 2 * REACH
WINDOW = 8
KEEP = 0.2
OMEGA = 0.8


def iota(shape, dim):
    return lax.broadcasted_iota(jnp.int32, shape, dim)


def pick(values, index):
    return jnp.take_along_axis(values, index, axis=1)


def lane_roll(value, shift):
    return pltpu.roll(value, shift % LANES, value.ndim - 1)


def row_roll(value, shift):
    return pltpu.roll(value, shift % value.shape[-2], value.ndim - 2)


def split_kernel(labels_ref, source_ref, out_ref):
    lane = iota((8, LANES), 1)
    for plane in range(4):
        labels = labels_ref[plane]
        code = jnp.where(labels == 0, 8.0, jnp.where(labels == 1, 9.0, 11.0)).astype(F32)
        source = source_ref[plane]
        for which, values in enumerate((code, source)):
            parts = [values[:, LANES * j : LANES * (j + 1)] for j in range(4)]
            for residue in range(4):
                index = 4 * (lane % 32) + residue
                moved = [pick(part, index) for part in parts]
                low = jnp.where(lane < 32, moved[0], moved[1])
                high = jnp.where(lane < 96, moved[2], moved[3])
                out_ref[plane, which, residue] = jnp.where(lane < 64, low, high)


def join_kernel(low_ref, own_ref, high_ref, all_ref, up_ref, down_ref):
    for plane in range(4):
        for which in range(2):
            for residue in range(4):
                for part, ref in enumerate((low_ref, own_ref, high_ref)):
                    rows = pl.ds(8 * part, 8)
                    value = ref[plane, which, residue]
                    all_ref[plane, which, residue, rows] = value
                    if plane > 0:
                        up_ref[plane - 1, which, residue, rows] = value
                    if plane < 3:
                        down_ref[plane, which, residue, rows] = value


def fine_sum(fx_up, fx_low, fy, fz, v_up, v_low, v):
    lane = iota((ROWS, LANES), 1)
    total = fx_up * v_up + fx_low * v_low
    total = total + fy * row_roll(v, -1) + row_roll(fy * v, 1)
    zv = fz * v
    last = jnp.where(lane == LANES - 1, 0.0, lane_roll(v[0], -1))
    first = jnp.where(lane == 0, 0.0, lane_roll(zv[3], 1))
    lower = [first, fz[0] * v[0], fz[1] * v[1], fz[2] * v[2]]
    upper = [fz[0] * v[1], fz[1] * v[2], fz[2] * v[3], fz[3] * last]
    return total + jnp.stack([lower[r] + upper[r] for r in range(4)])


def middle_sum(fx_up, fx_low, fy, fz, v_up, v_low, v):
    lane = iota((ROWS, LANES), 1)
    total = fx_up * v_up + fx_low * v_low
    total = total + fy * row_roll(v, -2) + row_roll(fy * v, 2)
    last = jnp.where(lane == LANES - 1, 0.0, lane_roll(v[0], -1))
    first = jnp.where(lane == 0, 0.0, lane_roll(fz[1] * v[1], 1))
    return total + jnp.stack([first + fz[0] * v[1], fz[0] * v[0] + fz[1] * last])


def both_rows(value, bit):
    row = iota(value.shape, value.ndim - 2)
    return value + jnp.where((row & bit) == 0, row_roll(value, -bit), row_roll(value, bit))


def upper_row(value, bit):
    row = iota(value.shape, value.ndim - 2)
    return jnp.where((row & bit) != 0, value, row_roll(value, -bit))


def pair_table(table_ref):
    lane = iota((8, LANES), 1)

    def at(*keys):
        hit = lane == keys[0]
        for key in keys[1:]:
            hit = hit | (lane == key)
        return hit

    one = jnp.where(at(8, 16, 17, 19), table_ref[0], jnp.where(at(9, 18, 20), table_ref[1], jnp.where(at(11, 22), table_ref[2], 1.0)))
    two = jnp.where(at(8, 16), table_ref[0], jnp.where(at(9, 17, 18), table_ref[1], jnp.where(at(11, 19, 20, 22), table_ref[2], 1.0)))
    return 2.0 * (one * two) / (one + two)


def up_kernel(
    spot_ref, table_ref, low2_ref, low1_ref, own_ref, high1_ref, high2_ref,
    chunk_ref, ends_ref, fx_out, fy_out, fz_out, w_out, s_out, v_out,
    fxm_out, fym_out, fzm_out, wm_out, sm_out, vm_out, root_out,
    code, source, fx, fy, fz, zlow, diag, weight, first, second,
    fxm, fym, fzm, zlowm, diagm, weightm, sourcem, firstm, secondm,
):
    x0 = 4 * spot_ref[0]
    y0 = 8 * spot_ref[1]
    nx = 4 * spot_ref[2]
    ny = 8 * spot_ref[3]
    table = pair_table(table_ref)
    at = 0
    for ref in (low2_ref, low1_ref, own_ref, high1_ref, high2_ref):
        for plane in range(ref.shape[0]):
            code[at] = ref[plane, 0].astype(jnp.int32)
            source[at] = ref[plane, 1]
            at += 1

    row = iota((ROWS, LANES), 0)
    lane = iota((ROWS, LANES), 1)
    y = y0 - 8 + row
    rowmask = jnp.where((y >= 0) & (y < ny), 1.0, 0.0)

    def planemask(x):
        return jnp.where((x >= 0) & (x < nx), 1.0, 0.0).astype(F32)

    def look(key):
        flat = key.reshape(-1, LANES)
        parts = [pick(table, flat[8 * k : 8 * k + 8]) for k in range(flat.shape[0] // 8)]
        return jnp.concatenate(parts, axis=0).reshape(key.shape)

    def faces(p, carry):
        here = code[p]
        fx[p] = look(here + code[p + 1])
        fy[p] = look(here + row_roll(here, -1))
        beyond = jnp.where(lane == LANES - 1, 0, lane_roll(here[0], -1))
        after = jnp.stack([here[1], here[2], here[3], beyond])
        fz_here = look(here + after)
        fz[p] = fz_here
        zlow[p] = jnp.where(lane == 0, look(here[0]), lane_roll(fz_here[3], 1))
        return carry

    lax.fori_loop(0, PLANES - 1, faces, 0)

    def start(p, carry):
        fy_here = fy[p]
        fz_here = fz[p]
        lower = jnp.stack([zlow[p], fz_here[0], fz_here[1], fz_here[2]])
        total = fx[p] + fx[p - 1] + fy_here + row_roll(fy_here, 1) + fz_here + lower
        diag[p] = total
        w = (OMEGA * planemask(x0 - REACH + p) * rowmask) / total
        weight[p] = w
        first[p] = w * source[p]
        return carry

    lax.fori_loop(1, PLANES - 1, start, 0)

    def sweep(p, carry):
        v = first[p]
        image = fine_sum(fx[p], fx[p - 1], fy[p], fz[p], first[p + 1], first[p - 1], v)
        second[p] = KEEP * v + weight[p] * (source[p] + image)
        return carry

    lax.fori_loop(2, PLANES - 2, sweep, 0)

    def halves(value):
        return jnp.stack([value[0] + value[1], value[2] + value[3]])

    def residual(p):
        v = second[p]
        image = fine_sum(fx[p], fx[p - 1], fy[p], fz[p], second[p + 1], second[p - 1], v)
        return source[p] - diag[p] * v + image

    def coarse_face(k, carry):
        fxm[k] = both_rows(halves(fx[2 + 2 * k]), 1)
        return carry

    lax.fori_loop(0, 7, coarse_face, 0)

    def middle(k, carry):
        pa = 1 + 2 * k
        pb = 2 + 2 * k
        sm = both_rows(halves(residual(pa) + residual(pb)), 1)
        fym_here = upper_row(halves(fy[pa] + fy[pb]), 1)
        fz_two = fz[pa] + fz[pb]
        fzm_here = both_rows(jnp.stack([fz_two[1], fz_two[3]]), 1)
        zlow_here = both_rows(zlow[pa] + zlow[pb], 1)
        lower = jnp.stack([zlow_here, fzm_here[0]])
        total = fxm[k] + fxm[k - 1] + fym_here + row_roll(fym_here, 2) + fzm_here + lower
        w = (OMEGA * planemask(x0 - REACH + pa) * rowmask) / total
        fym[k] = fym_here
        fzm[k] = fzm_here
        zlowm[k] = zlow_here
        diagm[k] = total
        weightm[k] = w
        sourcem[k] = sm
        firstm[k] = w * sm
        return carry

    lax.fori_loop(1, 7, middle, 0)

    def middle_sweep(k, carry):
        v = firstm[k]
        image = middle_sum(fxm[k], fxm[k - 1], fym[k], fzm[k], firstm[k + 1], firstm[k - 1], v)
        secondm[k] = KEEP * v + weightm[k] * (sourcem[k] + image)
        return carry

    lax.fori_loop(2, 6, middle_sweep, 0)

    coarse_source = jnp.zeros((ROWS, LANES), F32)
    for k in (3, 4):
        v = secondm[k]
        image = middle_sum(fxm[k], fxm[k - 1], fym[k], fzm[k], secondm[k + 1], secondm[k - 1], v)
        left = sourcem[k] - diagm[k] * v + image
        coarse_source = coarse_source + left[0] + left[1]
    coarse_source = both_rows(coarse_source, 2)

    def xface(big):
        value = fxm[2 * big + 4]
        return both_rows(value[0] + value[1], 2)

    xfaces = {big: xface(big) for big in (-2, -1, 0, 1)}
    roots = {}
    keep = None
    for big in (-1, 0, 1):
        ka = 2 * big + 3
        ysum = fym[ka] + fym[ka + 1]
        yface = upper_row(ysum[0] + ysum[1], 2)
        zsum = fzm[ka] + fzm[ka + 1]
        zface = both_rows(zsum[1], 2)
        zbelow = both_rows(zlowm[ka] + zlowm[ka + 1], 2)
        total = xfaces[big] + xfaces[big - 1] + yface + row_roll(yface, 4) + zface + zbelow
        root = lax.rsqrt(total) * (planemask(x0 + 4 * big) * rowmask)
        roots[big] = root
        root_out[big + 1] = root
        if big == 0:
            keep = (yface, zface)
    root = roots[0]
    cx = OMEGA * xfaces[0] * root * roots[1]
    cy = OMEGA * keep[0] * root * row_roll(root, -4)
    cz = OMEGA * keep[1] * root * jnp.where(lane == LANES - 1, 0.0, lane_roll(root, -1))
    lines = []
    for value in (OMEGA * root * coarse_source, cx, cy, cz):
        lines.append(value[8:9])
        lines.append(value[12:13])
    for at_row in (10, 12):
        for k in (3, 4):
            for half in range(2):
                lines.append(secondm[k, half, at_row : at_row + 1])
    chunk = jnp.concatenate(lines, axis=0)
    for peer in range(chunk_ref.shape[0]):
        chunk_ref[peer] = chunk
    for k in (3, 4):
        mids = [secondm[k, half, 8 + 2 * m : 9 + 2 * m] for half in range(2) for m in range(4)]
        ends_ref[k - 3] = jnp.concatenate(mids, axis=0)

    own_rows = pl.ds(8, 8)
    for k in range(5):
        fx_out[k] = fx[REACH - 1 + k, :, own_rows]
        fxm_out[k] = fxm[1 + k]
    for k in range(4):
        p = REACH + k
        fy_out[k] = fy[p]
        fz_out[k] = fz[p, :, own_rows]
        w_out[k] = weight[p, :, own_rows]
        s_out[k] = source[p, :, own_rows]
        fym_out[k] = fym[2 + k]
        fzm_out[k] = fzm[2 + k]
        wm_out[k] = weightm[2 + k]
        sm_out[k] = sourcem[2 + k]
        vm_out[k] = secondm[2 + k]
    for k in range(6):
        v_out[k] = second[REACH - 1 + k]


def window_kernel(spot_ref, got_ref, ends_ref, out_ref, chunk):
    mine = spot_ref[1]
    count = got_ref.shape[0]
    for step in range(9):
        block = mine + (step - 4)
        inside = jnp.where((block >= 0) & (block < count), 1.0, 0.0).astype(F32)
        value = got_ref[jnp.clip(block, 0, count - 1), pl.ds(0, 8)] * inside
        for which in range(4):
            chunk[pl.ds(18 * which + 2 * step, 2)] = value[2 * which : 2 * which + 2]
    body = chunk[...]
    low = ends_ref[0]
    high = ends_ref[1]
    for peer in range(out_ref.shape[0]):
        out_ref[peer, pl.ds(0, 72)] = body
        above = (spot_ref[0] < peer).astype(F32)
        out_ref[peer, pl.ds(72, 8)] = low * above + high * (1.0 - above)


def down_kernel(
    spot_ref, planes_ref, rows_ref, fx, fy, fz, w, s, v2,
    fxm, fym, fzm, wm, sm, vm, root,
    out_ref,
    parts, state, field, third, total,
):
    mine_x = spot_ref[0]
    mine_y = spot_ref[1]
    count_x = planes_ref.shape[0]
    count_y = rows_ref.shape[0]
    width = 2 * WINDOW + 1
    lane = iota((ROWS, LANES), 1)
    row = iota((ROWS, LANES), 0)

    def load(step, carry):
        plane = mine_x + (step - WINDOW)
        inside = jnp.where((plane >= 0) & (plane < count_x), 1.0, 0.0).astype(F32)
        spot = jnp.clip(plane, 0, count_x - 1)
        for which in range(4):
            value = planes_ref[spot, pl.ds(18 * which, ROWS)] if which < 3 else jnp.concatenate(
                [planes_ref[spot, pl.ds(54, 18)], jnp.zeros((ROWS - 18, LANES), F32)], axis=0)
            value = jnp.where(row < 18, value * inside, 0.0)
            parts[which, step] = value
            if which == 0:
                state[0, step] = value
        return carry

    lax.fori_loop(0, width, load, 0)

    for turn in range(1, WINDOW):
        old = (turn - 1) % 2
        new = turn % 2

        def sweep(step, carry):
            v = state[old, step]
            cy = parts[2, step]
            cz = parts[3, step]
            value = KEEP * v + parts[0, step]
            value = value + parts[1, step] * state[old, step + 1] + parts[1, step - 1] * state[old, step - 1]
            value = value + cy * row_roll(v, -1) + row_roll(cy * v, 1)
            value = value + cz * lane_roll(v, -1) + lane_roll(cz * v, 1)
            state[new, step] = value
            return carry

        lax.fori_loop(turn, width - turn, sweep, 0)

    last = (WINDOW - 1) % 2
    spread = []
    for big in range(3):
        value = state[last, WINDOW - 1 + big]
        picked = jnp.zeros((ROWS, LANES), F32)
        for k in range(4):
            line = jnp.broadcast_to(value[7 + k : 8 + k], (ROWS, LANES))
            picked = jnp.where((row >= 4 + 4 * k) & (row < 8 + 4 * k), line, picked)
        spread.append(picked * root[big])

    def line_block(ref, spot, inside, base):
        halves = []
        for half in range(2):
            rows = []
            for m in range(4):
                line = ref[spot, pl.ds(base + 4 * half + m, 1)] * inside
                rows += [line, line]
            pad = jnp.zeros((8, LANES), F32)
            halves.append(jnp.concatenate([pad] + [jnp.concatenate(rows, axis=0)] + [pad], axis=0))
        return jnp.stack(halves)

    below = jnp.where(mine_x > 0, 1.0, 0.0).astype(F32)
    above = jnp.where(mine_x < count_x - 1, 1.0, 0.0).astype(F32)
    field[0] = line_block(planes_ref, jnp.maximum(mine_x - 1, 0), below, 72) + spread[0]
    field[5] = line_block(planes_ref, jnp.minimum(mine_x + 1, count_x - 1), above, 72) + spread[2]
    field[1] = vm[0] + spread[0]
    field[4] = vm[3] + spread[2]
    left = jnp.where(mine_y > 0, 1.0, 0.0).astype(F32)
    right = jnp.where(mine_y < count_y - 1, 1.0, 0.0).astype(F32)
    left_spot = jnp.maximum(mine_y - 1, 0)
    right_spot = jnp.minimum(mine_y + 1, count_y - 1)
    for k in range(2):
        halves = []
        for half in range(2):
            value = vm[1 + k, half]
            lower = rows_ref[left_spot, pl.ds(12 + 2 * k + half, 1)] * left
            upper = rows_ref[right_spot, pl.ds(8 + 2 * k + half, 1)] * right
            value = jnp.where((row >= 4) & (row < 6), jnp.broadcast_to(lower, (ROWS, LANES)), value)
            value = jnp.where((row >= 18) & (row < 20), jnp.broadcast_to(upper, (ROWS, LANES)), value)
            halves.append(value)
        field[2 + k] = jnp.stack(halves) + spread[1]

    for k in range(4):
        v = field[k + 1]
        image = middle_sum(fxm[k + 1], fxm[k], fym[k], fzm[k], field[k + 2], field[k], v)
        third[k] = KEEP * v + wm[k] * (sm[k] + image)

    for p in range(6):
        mid = third[(p + 1) // 2]
        total[p] = v2[p] + jnp.stack([mid[0], mid[0], mid[1], mid[1]])

    lane8 = iota((8, LANES), 1)
    for p in range(4):
        up = total[p + 2, :, pl.ds(8, 8)]
        low = total[p, :, pl.ds(8, 8)]
        v = total[p + 1, :, pl.ds(8, 8)]
        image = fx[p + 1] * up + fx[p] * low
        image = image + fy[p, :, pl.ds(8, 8)] * total[p + 1, :, pl.ds(9, 8)]
        image = image + fy[p, :, pl.ds(7, 8)] * total[p + 1, :, pl.ds(7, 8)]
        zc = fz[p]
        end = jnp.where(lane8 == LANES - 1, 0.0, lane_roll(v[0], -1))
        begin = jnp.where(lane8 == 0, 0.0, lane_roll(zc[3] * v[3], 1))
        below_z = [begin, zc[0] * v[0], zc[1] * v[1], zc[2] * v[2]]
        above_z = [zc[0] * v[1], zc[1] * v[2], zc[2] * v[3], zc[3] * end]
        done = []
        for r in range(4):
            done.append(KEEP * v[r] + w[p, r] * (s[p, r] + image[r] + below_z[r] + above_z[r]))
        for j in range(4):
            index = 32 * j + lane8 // 4
            moved = [pick(done[r], index) for r in range(4)]
            odd = lane8 % 4
            low_pair = jnp.where(odd == 0, moved[0], moved[1])
            high_pair = jnp.where(odd == 2, moved[2], moved[3])
            out_ref[p, :, LANES * j : LANES * (j + 1)] = jnp.where(odd < 2, low_pair, high_pair)


VMEM = pl.BlockSpec(memory_space=pltpu.VMEM)
SMEM = pl.BlockSpec(memory_space=pltpu.SMEM)
PARAMS = pltpu.CompilerParams(vmem_limit_bytes=48 * 1024 * 1024)


def call(kernel, specs, outs, scratch, *args):
    return pl.pallas_call(
        kernel,
        in_specs=specs,
        out_specs=[VMEM] * len(outs),
        out_shape=[jax.ShapeDtypeStruct(shape, F32) for shape in outs],
        scratch_shapes=scratch,
        compiler_params=PARAMS,
    )(*args)


def shifted(value, axis, step):
    count = lax.axis_size(axis)
    if step > 0:
        pairs = [(i, i + step) for i in range(count - step)]
    else:
        pairs = [(i - step, i) for i in range(count + step)]
    return lax.ppermute(value, axis, pairs)


def shards(right_side, labels, conduct_table):
    nx = lax.axis_size("gx")
    ny = lax.axis_size("gy")
    spot = jnp.stack([lax.axis_index("gx"), lax.axis_index("gy"), jnp.int32(nx), jnp.int32(ny)]).astype(jnp.int32)
    (own,) = call(split_kernel, [VMEM] * 2, [(4, 2, 4, 8, LANES)], [], labels, right_side)
    low = shifted(own, "gy", 1)
    high = shifted(own, "gy", -1)
    wide, up, down = call(
        join_kernel,
        [VMEM] * 3,
        [(4, 2, 4, ROWS, LANES), (3, 2, 4, ROWS, LANES), (3, 2, 4, ROWS, LANES)],
        [],
        low, own, high,
    )
    low1 = shifted(wide, "gx", 1)
    high1 = shifted(wide, "gx", -1)
    low2 = shifted(up, "gx", 2)
    high2 = shifted(down, "gx", -2)

    fine = (4, ROWS, LANES)
    mid = (2, ROWS, LANES)
    tile = (4, 8, LANES)

    def room(*shape):
        return pltpu.VMEM(shape, F32)

    outs = call(
        up_kernel,
        [SMEM, SMEM] + [VMEM] * 5,
        [
            (ny, 16, LANES), (2, 8, LANES),
            (5,) + tile, (4,) + fine, (4,) + tile, (4,) + tile, (4,) + tile, (6,) + fine,
            (5,) + mid, (4,) + mid, (4,) + mid, (4,) + mid, (4,) + mid, (4,) + mid,
            (3, ROWS, LANES),
        ],
        [pltpu.VMEM((PLANES,) + fine, jnp.int32), room(PLANES, *fine)]
        + [room(PLANES, *fine)] * 3
        + [room(PLANES, ROWS, LANES)]
        + [room(PLANES, *fine)] * 4
        + [room(8, *mid)] * 3
        + [room(8, ROWS, LANES)]
        + [room(8, *mid)] * 5,
        spot, conduct_table, low2, low1, wide, high1, high2,
    )
    chunk, ends = outs[:2]
    rows = lax.all_to_all(chunk, "gy", 0, 0, tiled=True)
    (planes,) = call(window_kernel, [SMEM, VMEM, VMEM], [(nx, 80, LANES)], [room(72, LANES)], spot, rows, ends)
    planes = lax.all_to_all(planes, "gx", 0, 0, tiled=True)
    width = 2 * WINDOW + 1
    (correction,) = call(
        down_kernel,
        [SMEM] + [VMEM] * 15,
        [(4, 8, 4 * LANES)],
        [room(4, width, ROWS, LANES), room(2, width, ROWS, LANES), room(6, *mid), room(4, *mid), room(6, *fine)],
        spot, planes, rows, *outs[2:],
    )
    return correction


def solution(mesh):
    in_specs = (P("gx", "gy", None), P("gx", "gy", None), P())
    out_specs = P("gx", "gy", None)
    return jax.shard_map(shards, mesh=mesh, in_specs=in_specs, out_specs=out_specs, check_vma=False)
```

```python
import jax
import jax.numpy as jnp
from jax import lax
from jax.experimental import pallas as pl
from jax.experimental.pallas import tpu as pltpu
from jax.sharding import Mesh
from jax.sharding import PartitionSpec as P

F32 = jnp.float32
LANES = 128
ROWS = 24
REACH = 7
PLANES = 4 + 2 * REACH
WINDOW = 8
KEEP = 0.2
OMEGA = 0.8


def iota(shape, dim):
    return lax.broadcasted_iota(jnp.int32, shape, dim)


def pick(values, index):
    return jnp.take_along_axis(values, index, axis=1)


def lane_roll(value, shift):
    return pltpu.roll(value, shift % LANES, value.ndim - 1)


def row_roll(value, shift):
    return pltpu.roll(value, shift % value.shape[-2], value.ndim - 2)


def split_kernel(table_hbm, labels_hbm, source_hbm, out_ref, pairs_ref, table_ref, labels_ref, source_ref, done):
    copies = [
        pltpu.make_async_copy(src, dst, done.at[k])
        for k, (src, dst) in enumerate(
            ((table_hbm, table_ref), (labels_hbm, labels_ref), (source_hbm, source_ref)))
    ]
    for copy in copies:
        copy.start()
    for copy in copies:
        copy.wait()
    pairs_ref[...] = pair_table(table_ref)
    lane = iota((8, LANES), 1)
    for plane in range(4):
        labels = labels_ref[plane]
        code = jnp.where(labels == 0, 8.0, jnp.where(labels == 1, 9.0, 11.0)).astype(F32)
        source = source_ref[plane]
        for which, values in enumerate((code, source)):
            parts = [values[:, LANES * j : LANES * (j + 1)] for j in range(4)]
            for residue in range(4):
                index = 4 * (lane % 32) + residue
                moved = [pick(part, index) for part in parts]
                low = jnp.where(lane < 32, moved[0], moved[1])
                high = jnp.where(lane < 96, moved[2], moved[3])
                out_ref[plane, which, residue] = jnp.where(lane < 64, low, high)


def join_kernel(low_ref, own_ref, high_ref, all_ref, up_ref, down_ref):
    for plane in range(4):
        for which in range(2):
            for residue in range(4):
                for part, ref in enumerate((low_ref, own_ref, high_ref)):
                    rows = pl.ds(8 * part, 8)
                    value = ref[plane, which, residue]
                    all_ref[plane, which, residue, rows] = value
                    near = {0: (slice(4, 8), 0), 1: (slice(0, 8), 4), 2: (slice(0, 4), 12)}[part]
                    size = near[0].stop - near[0].start
                    if plane > which:
                        at = plane - 1 if which == 0 else plane + 1
                        up_ref[at, residue, pl.ds(near[1], size)] = value[near[0]]
                    if plane < 3 - which:
                        at = plane if which == 0 else plane + 3
                        down_ref[at, residue, pl.ds(near[1], size)] = value[near[0]]


def fine_sum(fx_up, fx_low, fy, fz, v_up, v_low, v):
    lane = iota((ROWS, LANES), 1)
    total = fx_up * v_up + fx_low * v_low
    total = total + fy * row_roll(v, -1) + row_roll(fy * v, 1)
    zv = fz * v
    last = jnp.where(lane == LANES - 1, 0.0, lane_roll(v[0], -1))
    first = jnp.where(lane == 0, 0.0, lane_roll(zv[3], 1))
    lower = [first, fz[0] * v[0], fz[1] * v[1], fz[2] * v[2]]
    upper = [fz[0] * v[1], fz[1] * v[2], fz[2] * v[3], fz[3] * last]
    return total + jnp.stack([lower[r] + upper[r] for r in range(4)])


def middle_sum(fx_up, fx_low, fy, fz, v_up, v_low, v):
    lane = iota((ROWS, LANES), 1)
    total = fx_up * v_up + fx_low * v_low
    total = total + fy * row_roll(v, -2) + row_roll(fy * v, 2)
    last = jnp.where(lane == LANES - 1, 0.0, lane_roll(v[0], -1))
    first = jnp.where(lane == 0, 0.0, lane_roll(fz[1] * v[1], 1))
    return total + jnp.stack([first + fz[0] * v[1], fz[0] * v[0] + fz[1] * last])


def both_rows(value, bit):
    row = iota(value.shape, value.ndim - 2)
    return value + jnp.where((row & bit) == 0, row_roll(value, -bit), row_roll(value, bit))


def upper_row(value, bit):
    row = iota(value.shape, value.ndim - 2)
    return jnp.where((row & bit) != 0, value, row_roll(value, -bit))


def pair_table(table_ref):
    lane = iota((8, LANES), 1)

    def at(*keys):
        hit = lane == keys[0]
        for key in keys[1:]:
            hit = hit | (lane == key)
        return hit

    one = jnp.where(at(8, 16, 17, 19), table_ref[0], jnp.where(at(9, 18, 20), table_ref[1], jnp.where(at(11, 22), table_ref[2], 1.0)))
    two = jnp.where(at(8, 16), table_ref[0], jnp.where(at(9, 17, 18), table_ref[1], jnp.where(at(11, 19, 20, 22), table_ref[2], 1.0)))
    return 2.0 * (one * two) / (one + two)


def up_kernel(
    spot_ref, pairs_ref, low2_ref, low1_ref, own_ref, high1_ref, high2_ref,
    chunk_ref, ends_ref, fx_out, fy_out, fz_out, w_out, s_out, v_out,
    fxm_out, fym_out, fzm_out, wm_out, sm_out, vm_out, root_out,
    code, source, fx, fy, fz, zlow, diag, weight, first, second,
    fxm, fym, fzm, zlowm, diagm, weightm, sourcem, firstm, secondm,
):
    x0 = 4 * spot_ref[0]
    y0 = 8 * spot_ref[1]
    nx = 4 * spot_ref[2]
    ny = 8 * spot_ref[3]
    table = pairs_ref[...]
    at = 3
    for ref in (low1_ref, own_ref, high1_ref):
        for plane in range(4):
            code[at] = ref[plane, 0].astype(jnp.int32)
            source[at] = ref[plane, 1]
            at += 1
    blank = jnp.zeros((4, 4, LANES), F32)

    def far(value):
        return jnp.concatenate([blank, value, blank], axis=1)

    for k in range(3):
        code[k] = far(low2_ref[k]).astype(jnp.int32)
        code[PLANES - 3 + k] = far(high2_ref[k]).astype(jnp.int32)
    for k in range(2):
        source[1 + k] = far(low2_ref[3 + k])
        source[PLANES - 3 + k] = far(high2_ref[3 + k])

    row = iota((ROWS, LANES), 0)
    lane = iota((ROWS, LANES), 1)
    y = y0 - 8 + row
    rowmask = jnp.where((y >= 0) & (y < ny), 1.0, 0.0)

    def planemask(x):
        return jnp.where((x >= 0) & (x < nx), 1.0, 0.0).astype(F32)

    def look(key):
        flat = key.reshape(-1, LANES)
        parts = [pick(table, flat[8 * k : 8 * k + 8]) for k in range(flat.shape[0] // 8)]
        return jnp.concatenate(parts, axis=0).reshape(key.shape)

    def faces(p, carry):
        here = code[p]
        fx[p] = look(here + code[p + 1])
        fy[p] = look(here + row_roll(here, -1))
        beyond = jnp.where(lane == LANES - 1, 0, lane_roll(here[0], -1))
        after = jnp.stack([here[1], here[2], here[3], beyond])
        fz_here = look(here + after)
        fz[p] = fz_here
        zlow[p] = jnp.where(lane == 0, look(here[0]), lane_roll(fz_here[3], 1))
        return carry

    lax.fori_loop(0, PLANES - 1, faces, 0, unroll=True)

    def start(p, carry):
        fy_here = fy[p]
        fz_here = fz[p]
        lower = jnp.stack([zlow[p], fz_here[0], fz_here[1], fz_here[2]])
        total = fx[p] + fx[p - 1] + fy_here + row_roll(fy_here, 1) + fz_here + lower
        diag[p] = total
        w = (OMEGA * planemask(x0 - REACH + p) * rowmask) / total
        weight[p] = w
        first[p] = w * source[p]
        return carry

    lax.fori_loop(1, PLANES - 1, start, 0, unroll=True)

    def sweep(p, carry):
        v = first[p]
        image = fine_sum(fx[p], fx[p - 1], fy[p], fz[p], first[p + 1], first[p - 1], v)
        second[p] = KEEP * v + weight[p] * (source[p] + image)
        return carry

    lax.fori_loop(2, PLANES - 2, sweep, 0, unroll=True)

    def halves(value):
        return jnp.stack([value[0] + value[1], value[2] + value[3]])

    def residual(p):
        v = second[p]
        image = fine_sum(fx[p], fx[p - 1], fy[p], fz[p], second[p + 1], second[p - 1], v)
        return source[p] - diag[p] * v + image

    def coarse_face(k, carry):
        fxm[k] = both_rows(halves(fx[2 + 2 * k]), 1)
        return carry

    lax.fori_loop(0, 7, coarse_face, 0, unroll=True)

    def middle(k, carry):
        pa = 1 + 2 * k
        pb = 2 + 2 * k
        sm = both_rows(halves(residual(pa) + residual(pb)), 1)
        fym_here = upper_row(halves(fy[pa] + fy[pb]), 1)
        fz_two = fz[pa] + fz[pb]
        fzm_here = both_rows(jnp.stack([fz_two[1], fz_two[3]]), 1)
        zlow_here = both_rows(zlow[pa] + zlow[pb], 1)
        lower = jnp.stack([zlow_here, fzm_here[0]])
        total = fxm[k] + fxm[k - 1] + fym_here + row_roll(fym_here, 2) + fzm_here + lower
        w = (OMEGA * planemask(x0 - REACH + pa) * rowmask) / total
        fym[k] = fym_here
        fzm[k] = fzm_here
        zlowm[k] = zlow_here
        diagm[k] = total
        weightm[k] = w
        sourcem[k] = sm
        firstm[k] = w * sm
        return carry

    lax.fori_loop(1, 7, middle, 0, unroll=True)

    def middle_sweep(k, carry):
        v = firstm[k]
        image = middle_sum(fxm[k], fxm[k - 1], fym[k], fzm[k], firstm[k + 1], firstm[k - 1], v)
        secondm[k] = KEEP * v + weightm[k] * (sourcem[k] + image)
        return carry

    lax.fori_loop(2, 6, middle_sweep, 0, unroll=True)

    coarse_source = jnp.zeros((ROWS, LANES), F32)
    for k in (3, 4):
        v = secondm[k]
        image = middle_sum(fxm[k], fxm[k - 1], fym[k], fzm[k], secondm[k + 1], secondm[k - 1], v)
        left = sourcem[k] - diagm[k] * v + image
        coarse_source = coarse_source + left[0] + left[1]
    coarse_source = both_rows(coarse_source, 2)

    def xface(big):
        value = fxm[2 * big + 4]
        return both_rows(value[0] + value[1], 2)

    xfaces = {big: xface(big) for big in (-2, -1, 0, 1)}
    roots = {}
    keep = None
    for big in (-1, 0, 1):
        ka = 2 * big + 3
        ysum = fym[ka] + fym[ka + 1]
        yface = upper_row(ysum[0] + ysum[1], 2)
        zsum = fzm[ka] + fzm[ka + 1]
        zface = both_rows(zsum[1], 2)
        zbelow = both_rows(zlowm[ka] + zlowm[ka + 1], 2)
        total = xfaces[big] + xfaces[big - 1] + yface + row_roll(yface, 4) + zface + zbelow
        root = lax.rsqrt(total) * (planemask(x0 + 4 * big) * rowmask)
        roots[big] = root
        root_out[big + 1] = root
        if big == 0:
            keep = (yface, zface)
    root = roots[0]
    cx = OMEGA * xfaces[0] * root * roots[1]
    cy = OMEGA * keep[0] * root * row_roll(root, -4)
    cz = OMEGA * keep[1] * root * jnp.where(lane == LANES - 1, 0.0, lane_roll(root, -1))
    lines = []
    for value in (OMEGA * root * coarse_source, cx, cy, cz):
        lines.append(value[8:9])
        lines.append(value[12:13])
    for at_row in (10, 12):
        for k in (3, 4):
            for half in range(2):
                lines.append(secondm[k, half, at_row : at_row + 1])
    chunk = jnp.concatenate(lines, axis=0)
    for peer in range(chunk_ref.shape[0]):
        chunk_ref[peer] = chunk
    for k in (3, 4):
        mids = [secondm[k, half, 8 + 2 * m : 9 + 2 * m] for half in range(2) for m in range(4)]
        ends_ref[k - 3] = jnp.concatenate(mids, axis=0)

    own_rows = pl.ds(8, 8)
    for k in range(5):
        fx_out[k] = fx[REACH - 1 + k, :, own_rows]
        fxm_out[k] = fxm[1 + k]
    for k in range(4):
        p = REACH + k
        fy_out[k] = fy[p]
        fz_out[k] = fz[p, :, own_rows]
        w_out[k] = weight[p, :, own_rows]
        s_out[k] = source[p, :, own_rows]
        fym_out[k] = fym[2 + k]
        fzm_out[k] = fzm[2 + k]
        wm_out[k] = weightm[2 + k]
        sm_out[k] = sourcem[2 + k]
        vm_out[k] = secondm[2 + k]
    for k in range(6):
        v_out[k] = second[REACH - 1 + k]


def window_kernel(spot_ref, got_ref, ends_ref, out_ref, chunk):
    mine = spot_ref[1]
    count = got_ref.shape[0]
    for step in range(9):
        block = mine + (step - 4)
        inside = jnp.where((block >= 0) & (block < count), 1.0, 0.0).astype(F32)
        value = got_ref[jnp.clip(block, 0, count - 1), pl.ds(0, 8)] * inside
        for which in range(4):
            chunk[pl.ds(18 * which + 2 * step, 2)] = value[2 * which : 2 * which + 2]
    body = chunk[...]
    low = ends_ref[0]
    high = ends_ref[1]
    place = spot_ref[4]
    size = out_ref.shape[0]
    for peer in range(size):
        out_ref[peer, pl.ds(0, 72)] = body
        ahead = (lax.rem(peer - place + size, size) == 1).astype(F32)
        out_ref[peer, pl.ds(72, 8)] = low * ahead + high * (1.0 - ahead)


def down_kernel(
    spot_ref, low2_ref, low1_ref, mid_ref, high1_ref, high2_ref, rows_ref, fx, fy, fz, w, s, v2,
    fxm, fym, fzm, wm, sm, vm, root,
    out_ref,
    parts, state, ends, field, third, total,
):
    mine_y = spot_ref[1]
    place = spot_ref[4]
    count_y = rows_ref.shape[0]
    width = 2 * WINDOW + 1
    lane = iota((ROWS, LANES), 1)
    row = iota((ROWS, LANES), 0)

    at = 0
    for ref in (low2_ref, low1_ref, mid_ref, high1_ref, high2_ref):
        for plane in range(ref.shape[0]):
            for which in range(4):
                value = jnp.where(row < 18, ref[plane, pl.ds(18 * which, ROWS)], 0.0)
                parts[which, at] = value
                if which == 0:
                    state[0, at] = value
            ends[at] = ref[plane, pl.ds(72, 8)]
            at += 1

    for turn in range(1, WINDOW):
        old = (turn - 1) % 2
        new = turn % 2
        for step in range(turn, width - turn):
            here = place + step
            v = state[old, here]
            cy = parts[2, here]
            cz = parts[3, here]
            value = KEEP * v + parts[0, here]
            value = value + parts[1, here] * state[old, here + 1] + parts[1, here - 1] * state[old, here - 1]
            value = value + cy * row_roll(v, -1) + row_roll(cy * v, 1)
            value = value + cz * lane_roll(v, -1) + lane_roll(cz * v, 1)
            state[new, here] = value

    last = (WINDOW - 1) % 2
    spread = []
    for big in range(3):
        value = state[last, place + WINDOW - 1 + big]
        picked = jnp.zeros((ROWS, LANES), F32)
        for k in range(4):
            line = jnp.broadcast_to(value[7 + k : 8 + k], (ROWS, LANES))
            picked = jnp.where((row >= 4 + 4 * k) & (row < 8 + 4 * k), line, picked)
        spread.append(picked * root[big])

    def line_block(at):
        halves = []
        for half in range(2):
            rows = []
            for m in range(4):
                line = ends[at, pl.ds(4 * half + m, 1)]
                rows += [line, line]
            pad = jnp.zeros((8, LANES), F32)
            halves.append(jnp.concatenate([pad] + [jnp.concatenate(rows, axis=0)] + [pad], axis=0))
        return jnp.stack(halves)

    field[0] = line_block(place + WINDOW - 1) + spread[0]
    field[5] = line_block(place + WINDOW + 1) + spread[2]
    field[1] = vm[0] + spread[0]
    field[4] = vm[3] + spread[2]
    left = jnp.where(mine_y > 0, 1.0, 0.0).astype(F32)
    right = jnp.where(mine_y < count_y - 1, 1.0, 0.0).astype(F32)
    left_spot = jnp.maximum(mine_y - 1, 0)
    right_spot = jnp.minimum(mine_y + 1, count_y - 1)
    for k in range(2):
        halves = []
        for half in range(2):
            value = vm[1 + k, half]
            lower = rows_ref[left_spot, pl.ds(12 + 2 * k + half, 1)] * left
            upper = rows_ref[right_spot, pl.ds(8 + 2 * k + half, 1)] * right
            value = jnp.where((row >= 4) & (row < 6), jnp.broadcast_to(lower, (ROWS, LANES)), value)
            value = jnp.where((row >= 18) & (row < 20), jnp.broadcast_to(upper, (ROWS, LANES)), value)
            halves.append(value)
        field[2 + k] = jnp.stack(halves) + spread[1]

    for k in range(4):
        v = field[k + 1]
        image = middle_sum(fxm[k + 1], fxm[k], fym[k], fzm[k], field[k + 2], field[k], v)
        third[k] = KEEP * v + wm[k] * (sm[k] + image)

    for p in range(6):
        mid = third[(p + 1) // 2]
        total[p] = v2[p] + jnp.stack([mid[0], mid[0], mid[1], mid[1]])

    lane8 = iota((8, LANES), 1)
    for p in range(4):
        up = total[p + 2, :, pl.ds(8, 8)]
        low = total[p, :, pl.ds(8, 8)]
        v = total[p + 1, :, pl.ds(8, 8)]
        image = fx[p + 1] * up + fx[p] * low
        image = image + fy[p, :, pl.ds(8, 8)] * total[p + 1, :, pl.ds(9, 8)]
        image = image + fy[p, :, pl.ds(7, 8)] * total[p + 1, :, pl.ds(7, 8)]
        zc = fz[p]
        end = jnp.where(lane8 == LANES - 1, 0.0, lane_roll(v[0], -1))
        begin = jnp.where(lane8 == 0, 0.0, lane_roll(zc[3] * v[3], 1))
        below_z = [begin, zc[0] * v[0], zc[1] * v[1], zc[2] * v[2]]
        above_z = [zc[0] * v[1], zc[1] * v[2], zc[2] * v[3], zc[3] * end]
        done = []
        for r in range(4):
            done.append(KEEP * v[r] + w[p, r] * (s[p, r] + image[r] + below_z[r] + above_z[r]))
        for j in range(4):
            index = 32 * j + lane8 // 4
            moved = [pick(done[r], index) for r in range(4)]
            odd = lane8 % 4
            low_pair = jnp.where(odd == 0, moved[0], moved[1])
            high_pair = jnp.where(odd == 2, moved[2], moved[3])
            out_ref[p, :, LANES * j : LANES * (j + 1)] = jnp.where(odd < 2, low_pair, high_pair)


VMEM = pl.BlockSpec(memory_space=pltpu.VMEM)
SMEM = pl.BlockSpec(memory_space=pltpu.SMEM)
HBM = pl.BlockSpec(memory_space=pltpu.HBM)
PARAMS = pltpu.CompilerParams(vmem_limit_bytes=48 * 1024 * 1024)
GX = ("ya", "xa")
GY = ("za", "ca")


def call(kernel, specs, outs, scratch, *args):
    return pl.pallas_call(
        kernel,
        in_specs=specs,
        out_specs=[VMEM] * len(outs),
        out_shape=[jax.ShapeDtypeStruct(shape, F32) for shape in outs],
        scratch_shapes=scratch,
        compiler_params=PARAMS,
    )(*args)


def shifted(value, axis, step):
    count = lax.axis_size(axis)
    if step > 0:
        pairs = [(i, i + step) for i in range(count - step)]
    else:
        pairs = [(i - step, i) for i in range(count + step)]
    return lax.ppermute(value, axis, pairs)


def shards(right_side, labels, conduct_table):
    nx = lax.axis_size(GX)
    ny = lax.axis_size(GY)
    block = lax.axis_size("xa")
    numbers = [lax.axis_index(GX), lax.axis_index(GY), jnp.int32(nx), jnp.int32(ny), lax.axis_index("xa")]
    spot = jnp.stack(numbers).astype(jnp.int32)

    fine = (4, ROWS, LANES)
    mid = (2, ROWS, LANES)
    tile = (4, 8, LANES)

    def room(*shape):
        return pltpu.VMEM(shape, F32)

    own, pairs = call(
        split_kernel, [HBM] * 3, [(4, 2, 4, 8, LANES), (8, LANES)],
        [
            pltpu.SMEM(conduct_table.shape, F32), pltpu.VMEM(labels.shape, jnp.int32), room(*right_side.shape),
            pltpu.SemaphoreType.DMA((3,)),
        ],
        conduct_table, labels, right_side,
    )
    low = shifted(own, GY, 1)
    high = shifted(own, GY, -1)
    wide, up, down = call(
        join_kernel, [VMEM] * 3, [(4, 2) + fine, (5, 4, 16, LANES), (5, 4, 16, LANES)], [], low, own, high
    )
    low1 = shifted(wide, GX, 1)
    high1 = shifted(wide, GX, -1)
    low2 = shifted(up, GX, 2)
    high2 = shifted(down, GX, -2)

    outs = call(
        up_kernel,
        [SMEM] + [VMEM] * 6,
        [
            (ny, 16, LANES), (2, 8, LANES),
            (5,) + tile, (4,) + fine, (4,) + tile, (4,) + tile, (4,) + tile, (6,) + fine,
            (5,) + mid, (4,) + mid, (4,) + mid, (4,) + mid, (4,) + mid, (4,) + mid,
            (3, ROWS, LANES),
        ],
        [pltpu.VMEM((PLANES,) + fine, jnp.int32), room(PLANES, *fine)]
        + [room(PLANES, *fine)] * 3
        + [room(PLANES, ROWS, LANES)]
        + [room(PLANES, *fine)] * 4
        + [room(8, *mid)] * 3
        + [room(8, ROWS, LANES)]
        + [room(8, *mid)] * 5,
        spot, pairs, low2, low1, wide, high1, high2,
    )
    chunk, ends = outs[:2]
    rows = lax.all_to_all(chunk, GY, 0, 0, tiled=True)
    (planes,) = call(window_kernel, [SMEM, VMEM, VMEM], [(block, 80, LANES)], [room(72, LANES)], spot, rows, ends)
    planes = lax.all_to_all(planes, "xa", 0, 0, tiled=True)
    blocks = [shifted(planes, "ya", 2), shifted(planes, "ya", 1), planes, shifted(planes, "ya", -1), shifted(planes, "ya", -2)]
    (correction,) = call(
        down_kernel,
        [SMEM] + [VMEM] * 19,
        [(4, 8, 4 * LANES)],
        [
            room(4, 5 * block, ROWS, LANES), room(2, 5 * block, ROWS, LANES), room(5 * block, 8, LANES),
            room(6, *mid), room(4, *mid), room(6, *fine),
        ],
        spot, *blocks, rows, *outs[2:],
    )
    return correction


def solution(mesh):
    mesh = Mesh(mesh.devices.reshape(-1, 4, mesh.devices.shape[1] // 2, 2), GX + GY)
    spec = P(GX, GY, None)
    return jax.shard_map(shards, mesh=mesh, in_specs=(spec, spec, P()), out_specs=spec, check_vma=False)
```

```python
import jax
import jax.numpy as jnp
from jax import lax
from jax.experimental import pallas as pl
from jax.experimental.pallas import tpu as pltpu
from jax.sharding import Mesh
from jax.sharding import PartitionSpec as P

F32 = jnp.float32
LANES = 128
ROWS = 24
REACH = 7
PLANES = 4 + 2 * REACH
WINDOW = 8
KEEP = 0.2
OMEGA = 0.8


def iota(shape, dim):
    return lax.broadcasted_iota(jnp.int32, shape, dim)


def pick(values, index):
    return jnp.take_along_axis(values, index, axis=1)


def lane_roll(value, shift):
    return pltpu.roll(value, shift % LANES, value.ndim - 1)


def row_roll(value, shift):
    return pltpu.roll(value, shift % value.shape[-2], value.ndim - 2)


def split_kernel(table_hbm, labels_hbm, source_hbm, out_ref, pairs_ref, table_ref, labels_ref, source_ref, done):
    copies = [
        pltpu.make_async_copy(src, dst, done.at[k])
        for k, (src, dst) in enumerate(
            ((table_hbm, table_ref), (labels_hbm, labels_ref), (source_hbm, source_ref)))
    ]
    for copy in copies:
        copy.start()
    for copy in copies:
        copy.wait()
    pairs_ref[...] = pair_table(table_ref)
    lane = iota((8, LANES), 1)
    for plane in range(4):
        labels = labels_ref[plane]
        code = jnp.where(labels == 0, 8.0, jnp.where(labels == 1, 9.0, 11.0)).astype(F32)
        source = source_ref[plane]
        for which, values in enumerate((code, source)):
            parts = [values[:, LANES * j : LANES * (j + 1)] for j in range(4)]
            for residue in range(4):
                index = 4 * (lane % 32) + residue
                moved = [pick(part, index) for part in parts]
                low = jnp.where(lane < 32, moved[0], moved[1])
                high = jnp.where(lane < 96, moved[2], moved[3])
                out_ref[plane, which, residue] = jnp.where(lane < 64, low, high)


def layout(first, last):
    spots = []
    offset = 0
    for which in range(2):
        for distance in range(first, last + 1 - which * (last == REACH)):
            reach = REACH - which - distance
            spots.append((which, distance, 8 - reach, 8 + 2 * reach, offset))
            offset += 8 + 2 * reach
    return spots, offset


NEAR, NEAR_ROWS = layout(1, 4)
FAR, FAR_ROWS = layout(5, REACH)


def join_kernel(low_ref, own_ref, high_ref, all_ref, up1_ref, down1_ref, up2_ref, down2_ref):
    for plane in range(4):
        for which in range(2):
            for residue in range(4):
                for part, ref in enumerate((low_ref, own_ref, high_ref)):
                    all_ref[plane, which, residue, pl.ds(8 * part, 8)] = ref[plane, which, residue]
    for spots, start, up_ref, down_ref in ((NEAR, 1, up1_ref, down1_ref), (FAR, 5, up2_ref, down2_ref)):
        for which, distance, row, rows, offset in spots:
            ahead = distance - start
            for residue in range(4):
                out = pl.ds(offset, rows)
                down_ref[residue, out] = all_ref[ahead, which, residue, pl.ds(row, rows)]
                up_ref[residue, out] = all_ref[3 - ahead, which, residue, pl.ds(row, rows)]


def fine_sum(fx_up, fx_low, fy, fz, v_up, v_low, v):
    lane = iota((ROWS, LANES), 1)
    total = fx_up * v_up + fx_low * v_low
    total = total + fy * row_roll(v, -1) + row_roll(fy * v, 1)
    zv = fz * v
    last = jnp.where(lane == LANES - 1, 0.0, lane_roll(v[0], -1))
    first = jnp.where(lane == 0, 0.0, lane_roll(zv[3], 1))
    lower = [first, fz[0] * v[0], fz[1] * v[1], fz[2] * v[2]]
    upper = [fz[0] * v[1], fz[1] * v[2], fz[2] * v[3], fz[3] * last]
    return total + jnp.stack([lower[r] + upper[r] for r in range(4)])


def middle_sum(fx_up, fx_low, fy, fz, v_up, v_low, v):
    lane = iota((ROWS, LANES), 1)
    total = fx_up * v_up + fx_low * v_low
    total = total + fy * row_roll(v, -2) + row_roll(fy * v, 2)
    last = jnp.where(lane == LANES - 1, 0.0, lane_roll(v[0], -1))
    first = jnp.where(lane == 0, 0.0, lane_roll(fz[1] * v[1], 1))
    return total + jnp.stack([first + fz[0] * v[1], fz[0] * v[0] + fz[1] * last])


def both_rows(value, bit):
    row = iota(value.shape, value.ndim - 2)
    return value + jnp.where((row & bit) == 0, row_roll(value, -bit), row_roll(value, bit))


def upper_row(value, bit):
    row = iota(value.shape, value.ndim - 2)
    return jnp.where((row & bit) != 0, value, row_roll(value, -bit))


def pair_table(table_ref):
    lane = iota((8, LANES), 1)

    def at(*keys):
        hit = lane == keys[0]
        for key in keys[1:]:
            hit = hit | (lane == key)
        return hit

    one = jnp.where(at(8, 16, 17, 19), table_ref[0], jnp.where(at(9, 18, 20), table_ref[1], jnp.where(at(11, 22), table_ref[2], 1.0)))
    two = jnp.where(at(8, 16), table_ref[0], jnp.where(at(9, 17, 18), table_ref[1], jnp.where(at(11, 19, 20, 22), table_ref[2], 1.0)))
    return 2.0 * (one * two) / (one + two)


def up_kernel(
    spot_ref, pairs_ref, low2_ref, low1_ref, own_ref, high1_ref, high2_ref,
    chunk_ref, ends_ref, fx_out, fy_out, fz_out, w_out, s_out, v_out,
    fxm_out, fym_out, fzm_out, wm_out, sm_out, vm_out, root_out,
    code, source, fx, fy, fz, zlow, diag, weight, first, second,
    fxm, fym, fzm, zlowm, diagm, weightm, sourcem, firstm, secondm,
):
    x0 = 4 * spot_ref[0]
    y0 = 8 * spot_ref[1]
    nx = 4 * spot_ref[2]
    ny = 8 * spot_ref[3]
    table = pairs_ref[...]
    blank = jnp.zeros((4, ROWS, LANES), F32)
    for k in range(4):
        code[REACH + k] = own_ref[k, 0].astype(jnp.int32)
        source[REACH + k] = own_ref[k, 1]
    for distance in range(1, REACH + 1):
        for p in (REACH - distance, REACH + 3 + distance):
            code[p] = blank.astype(jnp.int32)
            source[p] = blank
    for spots, low_ref, high_ref in ((NEAR, low1_ref, high1_ref), (FAR, low2_ref, high2_ref)):
        for which, distance, row, rows, offset in spots:
            for p, ref in ((REACH - distance, low_ref), (REACH + 3 + distance, high_ref)):
                for residue in range(4):
                    value = ref[residue, pl.ds(offset, rows)]
                    if which == 0:
                        code[p, residue, pl.ds(row, rows)] = value.astype(jnp.int32)
                    else:
                        source[p, residue, pl.ds(row, rows)] = value

    row = iota((ROWS, LANES), 0)
    lane = iota((ROWS, LANES), 1)
    y = y0 - 8 + row
    rowmask = jnp.where((y >= 0) & (y < ny), 1.0, 0.0)

    def planemask(x):
        return jnp.where((x >= 0) & (x < nx), 1.0, 0.0).astype(F32)

    def look(key):
        flat = key.reshape(-1, LANES)
        parts = [pick(table, flat[8 * k : 8 * k + 8]) for k in range(flat.shape[0] // 8)]
        return jnp.concatenate(parts, axis=0).reshape(key.shape)

    def faces(p, carry):
        here = code[p]
        fx[p] = look(here + code[p + 1])
        fy[p] = look(here + row_roll(here, -1))
        beyond = jnp.where(lane == LANES - 1, 0, lane_roll(here[0], -1))
        after = jnp.stack([here[1], here[2], here[3], beyond])
        fz_here = look(here + after)
        fz[p] = fz_here
        zlow[p] = jnp.where(lane == 0, look(here[0]), lane_roll(fz_here[3], 1))
        return carry

    lax.fori_loop(0, PLANES - 1, faces, 0, unroll=True)

    def start(p, carry):
        fy_here = fy[p]
        fz_here = fz[p]
        lower = jnp.stack([zlow[p], fz_here[0], fz_here[1], fz_here[2]])
        total = fx[p] + fx[p - 1] + fy_here + row_roll(fy_here, 1) + fz_here + lower
        diag[p] = total
        w = (OMEGA * planemask(x0 - REACH + p) * rowmask) / total
        weight[p] = w
        first[p] = w * source[p]
        return carry

    lax.fori_loop(1, PLANES - 1, start, 0, unroll=True)

    def sweep(p, carry):
        v = first[p]
        image = fine_sum(fx[p], fx[p - 1], fy[p], fz[p], first[p + 1], first[p - 1], v)
        second[p] = KEEP * v + weight[p] * (source[p] + image)
        return carry

    lax.fori_loop(2, PLANES - 2, sweep, 0, unroll=True)

    def halves(value):
        return jnp.stack([value[0] + value[1], value[2] + value[3]])

    def residual(p):
        v = second[p]
        image = fine_sum(fx[p], fx[p - 1], fy[p], fz[p], second[p + 1], second[p - 1], v)
        return source[p] - diag[p] * v + image

    def coarse_face(k, carry):
        fxm[k] = both_rows(halves(fx[2 + 2 * k]), 1)
        return carry

    lax.fori_loop(0, 7, coarse_face, 0, unroll=True)

    def middle(k, carry):
        pa = 1 + 2 * k
        pb = 2 + 2 * k
        sm = both_rows(halves(residual(pa) + residual(pb)), 1)
        fym_here = upper_row(halves(fy[pa] + fy[pb]), 1)
        fz_two = fz[pa] + fz[pb]
        fzm_here = both_rows(jnp.stack([fz_two[1], fz_two[3]]), 1)
        zlow_here = both_rows(zlow[pa] + zlow[pb], 1)
        lower = jnp.stack([zlow_here, fzm_here[0]])
        total = fxm[k] + fxm[k - 1] + fym_here + row_roll(fym_here, 2) + fzm_here + lower
        w = (OMEGA * planemask(x0 - REACH + pa) * rowmask) / total
        fym[k] = fym_here
        fzm[k] = fzm_here
        zlowm[k] = zlow_here
        diagm[k] = total
        weightm[k] = w
        sourcem[k] = sm
        firstm[k] = w * sm
        return carry

    lax.fori_loop(1, 7, middle, 0, unroll=True)

    def middle_sweep(k, carry):
        v = firstm[k]
        image = middle_sum(fxm[k], fxm[k - 1], fym[k], fzm[k], firstm[k + 1], firstm[k - 1], v)
        secondm[k] = KEEP * v + weightm[k] * (sourcem[k] + image)
        return carry

    lax.fori_loop(2, 6, middle_sweep, 0, unroll=True)

    coarse_source = jnp.zeros((ROWS, LANES), F32)
    for k in (3, 4):
        v = secondm[k]
        image = middle_sum(fxm[k], fxm[k - 1], fym[k], fzm[k], secondm[k + 1], secondm[k - 1], v)
        left = sourcem[k] - diagm[k] * v + image
        coarse_source = coarse_source + left[0] + left[1]
    coarse_source = both_rows(coarse_source, 2)

    def xface(big):
        value = fxm[2 * big + 4]
        return both_rows(value[0] + value[1], 2)

    xfaces = {big: xface(big) for big in (-2, -1, 0, 1)}
    roots = {}
    keep = None
    for big in (-1, 0, 1):
        ka = 2 * big + 3
        ysum = fym[ka] + fym[ka + 1]
        yface = upper_row(ysum[0] + ysum[1], 2)
        zsum = fzm[ka] + fzm[ka + 1]
        zface = both_rows(zsum[1], 2)
        zbelow = both_rows(zlowm[ka] + zlowm[ka + 1], 2)
        total = xfaces[big] + xfaces[big - 1] + yface + row_roll(yface, 4) + zface + zbelow
        root = lax.rsqrt(total) * (planemask(x0 + 4 * big) * rowmask)
        roots[big] = root
        root_out[big + 1] = root
        if big == 0:
            keep = (yface, zface)
    root = roots[0]
    cx = OMEGA * xfaces[0] * root * roots[1]
    cy = OMEGA * keep[0] * root * row_roll(root, -4)
    cz = OMEGA * keep[1] * root * jnp.where(lane == LANES - 1, 0.0, lane_roll(root, -1))
    lines = []
    for value in (OMEGA * root * coarse_source, cx, cy, cz):
        lines.append(value[8:9])
        lines.append(value[12:13])
    for at_row in (10, 12):
        for k in (3, 4):
            for half in range(2):
                lines.append(secondm[k, half, at_row : at_row + 1])
    chunk = jnp.concatenate(lines, axis=0)
    for peer in range(chunk_ref.shape[0]):
        chunk_ref[peer] = chunk
    for k, other in ((3, 4), (4, 3)):
        lines = [secondm[k, half, 8 + 2 * m : 9 + 2 * m] for half in range(2) for m in range(4)]
        lines += [secondm[other, half, at_row : at_row + 1] for at_row in (6, 16) for half in range(2)]
        lines += [root[at_row : at_row + 1] for at_row in (4, 16)]
        lines += [jnp.zeros((2, LANES), F32)]
        ends_ref[k - 3] = jnp.concatenate(lines, axis=0)

    own_rows = pl.ds(8, 8)
    for k in range(5):
        fx_out[k] = fx[REACH - 1 + k, :, own_rows]
        fxm_out[k] = fxm[1 + k]
    for k in range(4):
        p = REACH + k
        fy_out[k] = fy[p]
        fz_out[k] = fz[p, :, own_rows]
        w_out[k] = weight[p, :, own_rows]
        s_out[k] = source[p, :, own_rows]
        fym_out[k] = fym[2 + k]
        fzm_out[k] = fzm[2 + k]
        wm_out[k] = weightm[2 + k]
        sm_out[k] = sourcem[2 + k]
        vm_out[k] = secondm[2 + k]
    for k in range(6):
        v_out[k] = second[REACH - 1 + k]


def window_kernel(spot_ref, got_ref, ends_ref, out_ref, chunk):
    mine = spot_ref[1]
    count = got_ref.shape[0]
    for step in range(9):
        block = mine + (step - 4)
        inside = jnp.where((block >= 0) & (block < count), 1.0, 0.0).astype(F32)
        value = got_ref[jnp.clip(block, 0, count - 1), pl.ds(0, 8)] * inside
        for which in range(4):
            chunk[pl.ds(18 * which + 2 * step, 2)] = value[2 * which : 2 * which + 2]
    body = chunk[...]
    low = ends_ref[0]
    high = ends_ref[1]
    place = spot_ref[4]
    size = out_ref.shape[0]
    for peer in range(size):
        out_ref[peer, pl.ds(0, 72)] = body
        ahead = (lax.rem(peer - place + size, size) == 1).astype(F32)
        out_ref[peer, pl.ds(72, 16)] = low * ahead + high * (1.0 - ahead)


def down_kernel(
    spot_ref, low2_ref, low1_ref, mid_ref, high1_ref, high2_ref, rows_ref, fx, fy, fz, w, s, v2,
    fxm, fym, fzm, wm, sm, vm, root,
    out_ref,
    parts, state, ends, field, third, total,
):
    mine_y = spot_ref[1]
    place = spot_ref[4]
    count_y = rows_ref.shape[0]
    width = 2 * WINDOW + 1
    lane = iota((ROWS, LANES), 1)
    row = iota((ROWS, LANES), 0)

    at = 0
    for ref in (low2_ref, low1_ref, mid_ref, high1_ref, high2_ref):
        for plane in range(ref.shape[0]):
            for which in range(4):
                value = jnp.where(row < 18, ref[plane, pl.ds(18 * which, ROWS)], 0.0)
                parts[which, at] = value
                if which == 0:
                    state[0, at] = value
            ends[at] = ref[plane, pl.ds(72, 16)]
            at += 1

    for turn in range(1, WINDOW):
        old = (turn - 1) % 2
        new = turn % 2
        for step in range(turn, width - turn):
            here = place + step
            v = state[old, here]
            cy = parts[2, here]
            cz = parts[3, here]
            value = KEEP * v + parts[0, here]
            value = value + parts[1, here] * state[old, here + 1] + parts[1, here - 1] * state[old, here - 1]
            value = value + cy * row_roll(v, -1) + row_roll(cy * v, 1)
            value = value + cz * lane_roll(v, -1) + lane_roll(cz * v, 1)
            state[new, here] = value

    def swap_rows(value, line, first, stop):
        return jnp.where((row >= first) & (row < stop), jnp.broadcast_to(line, (ROWS, LANES)), value)

    def corners(value, at):
        halves = []
        for half in range(2):
            part = swap_rows(value[half], ends[at, pl.ds(8 + half, 1)], 6, 8)
            halves.append(swap_rows(part, ends[at, pl.ds(10 + half, 1)], 16, 18))
        return jnp.stack(halves)

    last = (WINDOW - 1) % 2
    spread = []
    for big in range(3):
        value = state[last, place + WINDOW - 1 + big]
        picked = jnp.zeros((ROWS, LANES), F32)
        for k in range(4):
            line = jnp.broadcast_to(value[7 + k : 8 + k], (ROWS, LANES))
            picked = jnp.where((row >= 4 + 4 * k) & (row < 8 + 4 * k), line, picked)
        scale = root[big]
        if big != 1:
            beside = place + WINDOW - 1 + big
            scale = swap_rows(scale, ends[beside, pl.ds(12, 1)], 4, 8)
            scale = swap_rows(scale, ends[beside, pl.ds(13, 1)], 16, 20)
        spread.append(picked * scale)

    def line_block(at):
        halves = []
        for half in range(2):
            rows = []
            for m in range(4):
                line = ends[at, pl.ds(4 * half + m, 1)]
                rows += [line, line]
            pad = jnp.zeros((8, LANES), F32)
            halves.append(jnp.concatenate([pad] + [jnp.concatenate(rows, axis=0)] + [pad], axis=0))
        return jnp.stack(halves)

    field[0] = line_block(place + WINDOW - 1) + spread[0]
    field[5] = line_block(place + WINDOW + 1) + spread[2]
    field[1] = corners(vm[0], place + WINDOW - 1) + spread[0]
    field[4] = corners(vm[3], place + WINDOW + 1) + spread[2]
    left = jnp.where(mine_y > 0, 1.0, 0.0).astype(F32)
    right = jnp.where(mine_y < count_y - 1, 1.0, 0.0).astype(F32)
    left_spot = jnp.maximum(mine_y - 1, 0)
    right_spot = jnp.minimum(mine_y + 1, count_y - 1)
    for k in range(2):
        halves = []
        for half in range(2):
            value = vm[1 + k, half]
            lower = rows_ref[left_spot, pl.ds(12 + 2 * k + half, 1)] * left
            upper = rows_ref[right_spot, pl.ds(8 + 2 * k + half, 1)] * right
            halves.append(swap_rows(swap_rows(value, lower, 4, 6), upper, 18, 20))
        field[2 + k] = jnp.stack(halves) + spread[1]

    for k in range(4):
        v = field[k + 1]
        image = middle_sum(fxm[k + 1], fxm[k], fym[k], fzm[k], field[k + 2], field[k], v)
        third[k] = KEEP * v + wm[k] * (sm[k] + image)

    for p in range(6):
        mid = third[(p + 1) // 2]
        total[p] = v2[p] + jnp.stack([mid[0], mid[0], mid[1], mid[1]])

    lane8 = iota((8, LANES), 1)
    for p in range(4):
        up = total[p + 2, :, pl.ds(8, 8)]
        low = total[p, :, pl.ds(8, 8)]
        v = total[p + 1, :, pl.ds(8, 8)]
        image = fx[p + 1] * up + fx[p] * low
        image = image + fy[p, :, pl.ds(8, 8)] * total[p + 1, :, pl.ds(9, 8)]
        image = image + fy[p, :, pl.ds(7, 8)] * total[p + 1, :, pl.ds(7, 8)]
        zc = fz[p]
        end = jnp.where(lane8 == LANES - 1, 0.0, lane_roll(v[0], -1))
        begin = jnp.where(lane8 == 0, 0.0, lane_roll(zc[3] * v[3], 1))
        below_z = [begin, zc[0] * v[0], zc[1] * v[1], zc[2] * v[2]]
        above_z = [zc[0] * v[1], zc[1] * v[2], zc[2] * v[3], zc[3] * end]
        done = []
        for r in range(4):
            done.append(KEEP * v[r] + w[p, r] * (s[p, r] + image[r] + below_z[r] + above_z[r]))
        for j in range(4):
            index = 32 * j + lane8 // 4
            moved = [pick(done[r], index) for r in range(4)]
            odd = lane8 % 4
            low_pair = jnp.where(odd == 0, moved[0], moved[1])
            high_pair = jnp.where(odd == 2, moved[2], moved[3])
            out_ref[p, :, LANES * j : LANES * (j + 1)] = jnp.where(odd < 2, low_pair, high_pair)


VMEM = pl.BlockSpec(memory_space=pltpu.VMEM)
SMEM = pl.BlockSpec(memory_space=pltpu.SMEM)
HBM = pl.BlockSpec(memory_space=pltpu.HBM)
PARAMS = pltpu.CompilerParams(vmem_limit_bytes=48 * 1024 * 1024)
GX = ("ya", "xa")
GY = ("za", "ca")


def call(kernel, specs, outs, scratch, *args):
    return pl.pallas_call(
        kernel,
        in_specs=specs,
        out_specs=[VMEM] * len(outs),
        out_shape=[jax.ShapeDtypeStruct(shape, F32) for shape in outs],
        scratch_shapes=scratch,
        compiler_params=PARAMS,
    )(*args)


def shifted(value, axis, step):
    count = lax.axis_size(axis)
    if step > 0:
        pairs = [(i, i + step) for i in range(count - step)]
    else:
        pairs = [(i - step, i) for i in range(count + step)]
    return lax.ppermute(value, axis, pairs)


def shards(right_side, labels, conduct_table):
    nx = lax.axis_size(GX)
    ny = lax.axis_size(GY)
    block = lax.axis_size("xa")
    numbers = [lax.axis_index(GX), lax.axis_index(GY), jnp.int32(nx), jnp.int32(ny), lax.axis_index("xa")]
    spot = jnp.stack(numbers).astype(jnp.int32)

    fine = (4, ROWS, LANES)
    mid = (2, ROWS, LANES)
    tile = (4, 8, LANES)

    def room(*shape):
        return pltpu.VMEM(shape, F32)

    own, pairs = call(
        split_kernel, [HBM] * 3, [(4, 2, 4, 8, LANES), (8, LANES)],
        [
            pltpu.SMEM(conduct_table.shape, F32), pltpu.VMEM(labels.shape, jnp.int32), room(*right_side.shape),
            pltpu.SemaphoreType.DMA((3,)),
        ],
        *(pltpu.with_memory_space_constraint(value, pltpu.HBM) for value in (conduct_table, labels, right_side)),
    )
    low = shifted(own, GY, 1)
    high = shifted(own, GY, -1)
    near = (4, NEAR_ROWS, LANES)
    far = (4, FAR_ROWS, LANES)
    wide, up1, down1, up2, down2 = call(
        join_kernel, [VMEM] * 3, [(4, 2) + fine, near, near, far, far], [], low, own, high
    )
    low1 = shifted(up1, GX, 1)
    high1 = shifted(down1, GX, -1)
    low2 = shifted(up2, GX, 2)
    high2 = shifted(down2, GX, -2)

    outs = call(
        up_kernel,
        [SMEM] + [VMEM] * 6,
        [
            (ny, 16, LANES), (2, 16, LANES),
            (5,) + tile, (4,) + fine, (4,) + tile, (4,) + tile, (4,) + tile, (6,) + fine,
            (5,) + mid, (4,) + mid, (4,) + mid, (4,) + mid, (4,) + mid, (4,) + mid,
            (3, ROWS, LANES),
        ],
        [pltpu.VMEM((PLANES,) + fine, jnp.int32), room(PLANES, *fine)]
        + [room(PLANES, *fine)] * 3
        + [room(PLANES, ROWS, LANES)]
        + [room(PLANES, *fine)] * 4
        + [room(8, *mid)] * 3
        + [room(8, ROWS, LANES)]
        + [room(8, *mid)] * 5,
        spot, pairs, low2, low1, wide, high1, high2,
    )
    chunk, ends = outs[:2]
    rows = lax.all_to_all(chunk, GY, 0, 0, tiled=True)
    (planes,) = call(window_kernel, [SMEM, VMEM, VMEM], [(block, 88, LANES)], [room(72, LANES)], spot, rows, ends)
    planes = lax.all_to_all(planes, "xa", 0, 0, tiled=True)
    blocks = [shifted(planes, "ya", 2), shifted(planes, "ya", 1), planes, shifted(planes, "ya", -1), shifted(planes, "ya", -2)]
    (correction,) = call(
        down_kernel,
        [SMEM] + [VMEM] * 19,
        [(4, 8, 4 * LANES)],
        [
            room(4, 5 * block, ROWS, LANES), room(2, 5 * block, ROWS, LANES), room(5 * block, 16, LANES),
            room(6, *mid), room(4, *mid), room(6, *fine),
        ],
        spot, *blocks, rows, *outs[2:],
    )
    return correction


def solution(mesh):
    mesh = Mesh(mesh.devices.reshape(-1, 4, mesh.devices.shape[1] // 2, 2), GX + GY)
    spec = P(GX, GY, None)
    return jax.shard_map(shards, mesh=mesh, in_specs=(spec, spec, P()), out_specs=spec, check_vma=False)
```

```python
import jax
import jax.numpy as jnp
from jax import lax
from jax.experimental import pallas as pl
from jax.experimental.pallas import tpu as pltpu
from jax.sharding import Mesh
from jax.sharding import PartitionSpec as P

F32 = jnp.float32
LANES = 128
ROWS = 24
REACH = 7
PLANES = 4 + 2 * REACH
WINDOW = 8
SPAN = 20
KEEP = 0.2
OMEGA = 0.8


def iota(shape, dim):
    return lax.broadcasted_iota(jnp.int32, shape, dim)


def pick(values, index):
    return jnp.take_along_axis(values, index, axis=1)


def lane_roll(value, shift):
    return pltpu.roll(value, shift % LANES, value.ndim - 1)


def row_roll(value, shift):
    return pltpu.roll(value, shift % value.shape[-2], value.ndim - 2)


def split_kernel(table_hbm, labels_hbm, source_hbm, out_ref, pairs_ref, table_ref, labels_ref, source_ref, done):
    copies = [
        pltpu.make_async_copy(src, dst, done.at[k])
        for k, (src, dst) in enumerate(
            ((table_hbm, table_ref), (labels_hbm, labels_ref), (source_hbm, source_ref)))
    ]
    for copy in copies:
        copy.start()
    for copy in copies:
        copy.wait()
    pairs_ref[...] = pair_table(table_ref)
    lane = iota((8, LANES), 1)
    for plane in range(4):
        labels = labels_ref[plane]
        code = jnp.where(labels == 0, 8.0, jnp.where(labels == 1, 9.0, 11.0)).astype(F32)
        source = source_ref[plane]
        for which, values in enumerate((code, source)):
            parts = [values[:, LANES * j : LANES * (j + 1)] for j in range(4)]
            for residue in range(4):
                index = 4 * (lane % 32) + residue
                moved = [pick(part, index) for part in parts]
                low = jnp.where(lane < 32, moved[0], moved[1])
                high = jnp.where(lane < 96, moved[2], moved[3])
                out_ref[plane, which, residue] = jnp.where(lane < 64, low, high)


def layout(first, last):
    spots = []
    offset = 0
    for which in range(2):
        for distance in range(first, last + 1 - which * (last == REACH)):
            reach = REACH - which - distance
            spots.append((which, distance, 8 - reach, 8 + 2 * reach, offset))
            offset += 8 + 2 * reach
    return spots, offset


NEAR, NEAR_ROWS = layout(1, 4)
FAR, FAR_ROWS = layout(5, REACH)


def join_kernel(low_ref, own_ref, high_ref, all_ref, up1_ref, down1_ref, up2_ref, down2_ref):
    for plane in range(4):
        for which in range(2):
            for residue in range(4):
                for part, ref in enumerate((low_ref, own_ref, high_ref)):
                    all_ref[plane, which, residue, pl.ds(8 * part, 8)] = ref[plane, which, residue]
    for spots, start, up_ref, down_ref in ((NEAR, 1, up1_ref, down1_ref), (FAR, 5, up2_ref, down2_ref)):
        for which, distance, row, rows, offset in spots:
            ahead = distance - start
            for residue in range(4):
                out = pl.ds(offset, rows)
                down_ref[residue, out] = all_ref[ahead, which, residue, pl.ds(row, rows)]
                up_ref[residue, out] = all_ref[3 - ahead, which, residue, pl.ds(row, rows)]


def fine_sum(fx_up, fx_low, fy, fz, v_up, v_low, v):
    lane = iota((ROWS, LANES), 1)
    total = fx_up * v_up + fx_low * v_low
    total = total + fy * row_roll(v, -1) + row_roll(fy * v, 1)
    zv = fz * v
    last = jnp.where(lane == LANES - 1, 0.0, lane_roll(v[0], -1))
    first = jnp.where(lane == 0, 0.0, lane_roll(zv[3], 1))
    lower = [first, fz[0] * v[0], fz[1] * v[1], fz[2] * v[2]]
    upper = [fz[0] * v[1], fz[1] * v[2], fz[2] * v[3], fz[3] * last]
    return total + jnp.stack([lower[r] + upper[r] for r in range(4)])


def middle_sum(fx_up, fx_low, fy, fz, v_up, v_low, v):
    lane = iota((ROWS, LANES), 1)
    total = fx_up * v_up + fx_low * v_low
    total = total + fy * row_roll(v, -2) + row_roll(fy * v, 2)
    last = jnp.where(lane == LANES - 1, 0.0, lane_roll(v[0], -1))
    first = jnp.where(lane == 0, 0.0, lane_roll(fz[1] * v[1], 1))
    return total + jnp.stack([first + fz[0] * v[1], fz[0] * v[0] + fz[1] * last])


def both_rows(value, bit):
    row = iota(value.shape, value.ndim - 2)
    return value + jnp.where((row & bit) == 0, row_roll(value, -bit), row_roll(value, bit))


def upper_row(value, bit):
    row = iota(value.shape, value.ndim - 2)
    return jnp.where((row & bit) != 0, value, row_roll(value, -bit))


def pair_table(table_ref):
    lane = iota((8, LANES), 1)

    def at(*keys):
        hit = lane == keys[0]
        for key in keys[1:]:
            hit = hit | (lane == key)
        return hit

    one = jnp.where(at(8, 16, 17, 19), table_ref[0], jnp.where(at(9, 18, 20), table_ref[1], jnp.where(at(11, 22), table_ref[2], 1.0)))
    two = jnp.where(at(8, 16), table_ref[0], jnp.where(at(9, 17, 18), table_ref[1], jnp.where(at(11, 19, 20, 22), table_ref[2], 1.0)))
    return 2.0 * (one * two) / (one + two)


def up_kernel(
    spot_ref, pairs_ref, low2_ref, low1_ref, own_ref, high1_ref, high2_ref,
    chunk_ref, ends_ref, fx_out, fy_out, fz_out, w_out, s_out, v_out,
    fxm_out, fym_out, fzm_out, wm_out, sm_out, vm_out, root_out,
    code, source, fx, fy, fz, zlow, diag, weight, first, second,
    fxm, fym, fzm, zlowm, diagm, weightm, sourcem, firstm, secondm,
):
    x0 = 4 * spot_ref[0]
    y0 = 8 * spot_ref[1]
    nx = 4 * spot_ref[2]
    ny = 8 * spot_ref[3]
    table = pairs_ref[...]
    blank = jnp.zeros((4, ROWS, LANES), F32)
    for k in range(4):
        code[REACH + k] = own_ref[k, 0].astype(jnp.int32)
        source[REACH + k] = own_ref[k, 1]
    for distance in range(1, REACH + 1):
        for p in (REACH - distance, REACH + 3 + distance):
            code[p] = blank.astype(jnp.int32)
            source[p] = blank
    for spots, low_ref, high_ref in ((NEAR, low1_ref, high1_ref), (FAR, low2_ref, high2_ref)):
        for which, distance, row, rows, offset in spots:
            for p, ref in ((REACH - distance, low_ref), (REACH + 3 + distance, high_ref)):
                for residue in range(4):
                    value = ref[residue, pl.ds(offset, rows)]
                    if which == 0:
                        code[p, residue, pl.ds(row, rows)] = value.astype(jnp.int32)
                    else:
                        source[p, residue, pl.ds(row, rows)] = value

    row = iota((ROWS, LANES), 0)
    lane = iota((ROWS, LANES), 1)
    y = y0 - 8 + row
    rowmask = jnp.where((y >= 0) & (y < ny), 1.0, 0.0)

    def planemask(x):
        return jnp.where((x >= 0) & (x < nx), 1.0, 0.0).astype(F32)

    def look(key):
        flat = key.reshape(-1, LANES)
        parts = [pick(table, flat[8 * k : 8 * k + 8]) for k in range(flat.shape[0] // 8)]
        return jnp.concatenate(parts, axis=0).reshape(key.shape)

    def faces(p, carry):
        here = code[p]
        fx[p] = look(here + code[p + 1])
        fy[p] = look(here + row_roll(here, -1))
        beyond = jnp.where(lane == LANES - 1, 0, lane_roll(here[0], -1))
        after = jnp.stack([here[1], here[2], here[3], beyond])
        fz_here = look(here + after)
        fz[p] = fz_here
        zlow[p] = jnp.where(lane == 0, look(here[0]), lane_roll(fz_here[3], 1))
        return carry

    lax.fori_loop(0, PLANES - 1, faces, 0, unroll=True)

    def start(p, carry):
        fy_here = fy[p]
        fz_here = fz[p]
        lower = jnp.stack([zlow[p], fz_here[0], fz_here[1], fz_here[2]])
        total = fx[p] + fx[p - 1] + fy_here + row_roll(fy_here, 1) + fz_here + lower
        diag[p] = total
        w = (OMEGA * planemask(x0 - REACH + p) * rowmask) / total
        weight[p] = w
        first[p] = w * source[p]
        return carry

    lax.fori_loop(1, PLANES - 1, start, 0, unroll=True)

    def sweep(p, carry):
        v = first[p]
        image = fine_sum(fx[p], fx[p - 1], fy[p], fz[p], first[p + 1], first[p - 1], v)
        second[p] = KEEP * v + weight[p] * (source[p] + image)
        return carry

    lax.fori_loop(2, PLANES - 2, sweep, 0, unroll=True)

    def halves(value):
        return jnp.stack([value[0] + value[1], value[2] + value[3]])

    def residual(p):
        v = second[p]
        image = fine_sum(fx[p], fx[p - 1], fy[p], fz[p], second[p + 1], second[p - 1], v)
        return source[p] - diag[p] * v + image

    def coarse_face(k, carry):
        fxm[k] = both_rows(halves(fx[2 + 2 * k]), 1)
        return carry

    lax.fori_loop(0, 7, coarse_face, 0, unroll=True)

    def middle(k, carry):
        pa = 1 + 2 * k
        pb = 2 + 2 * k
        sm = both_rows(halves(residual(pa) + residual(pb)), 1)
        fym_here = upper_row(halves(fy[pa] + fy[pb]), 1)
        fz_two = fz[pa] + fz[pb]
        fzm_here = both_rows(jnp.stack([fz_two[1], fz_two[3]]), 1)
        zlow_here = both_rows(zlow[pa] + zlow[pb], 1)
        lower = jnp.stack([zlow_here, fzm_here[0]])
        total = fxm[k] + fxm[k - 1] + fym_here + row_roll(fym_here, 2) + fzm_here + lower
        w = (OMEGA * planemask(x0 - REACH + pa) * rowmask) / total
        fym[k] = fym_here
        fzm[k] = fzm_here
        zlowm[k] = zlow_here
        diagm[k] = total
        weightm[k] = w
        sourcem[k] = sm
        firstm[k] = w * sm
        return carry

    lax.fori_loop(1, 7, middle, 0, unroll=True)

    def middle_sweep(k, carry):
        v = firstm[k]
        image = middle_sum(fxm[k], fxm[k - 1], fym[k], fzm[k], firstm[k + 1], firstm[k - 1], v)
        secondm[k] = KEEP * v + weightm[k] * (sourcem[k] + image)
        return carry

    lax.fori_loop(2, 6, middle_sweep, 0, unroll=True)

    coarse_source = jnp.zeros((ROWS, LANES), F32)
    for k in (3, 4):
        v = secondm[k]
        image = middle_sum(fxm[k], fxm[k - 1], fym[k], fzm[k], secondm[k + 1], secondm[k - 1], v)
        left = sourcem[k] - diagm[k] * v + image
        coarse_source = coarse_source + left[0] + left[1]
    coarse_source = both_rows(coarse_source, 2)

    def xface(big):
        value = fxm[2 * big + 4]
        return both_rows(value[0] + value[1], 2)

    xfaces = {big: xface(big) for big in (-2, -1, 0, 1)}
    roots = {}
    keep = None
    for big in (-1, 0, 1):
        ka = 2 * big + 3
        ysum = fym[ka] + fym[ka + 1]
        yface = upper_row(ysum[0] + ysum[1], 2)
        zsum = fzm[ka] + fzm[ka + 1]
        zface = both_rows(zsum[1], 2)
        zbelow = both_rows(zlowm[ka] + zlowm[ka + 1], 2)
        total = xfaces[big] + xfaces[big - 1] + yface + row_roll(yface, 4) + zface + zbelow
        root = lax.rsqrt(total) * (planemask(x0 + 4 * big) * rowmask)
        roots[big] = root
        root_out[big + 1] = root
        if big == 0:
            keep = (yface, zface)
    root = roots[0]
    cx = OMEGA * xfaces[0] * root * roots[1]
    cy = OMEGA * keep[0] * root * row_roll(root, -4)
    cz = OMEGA * keep[1] * root * jnp.where(lane == LANES - 1, 0.0, lane_roll(root, -1))
    lines = []
    for value in (OMEGA * root * coarse_source, cx, cy, cz):
        lines.append(value[8:9])
        lines.append(value[12:13])
    for at_row in (10, 12):
        for k in (3, 4):
            for half in range(2):
                lines.append(secondm[k, half, at_row : at_row + 1])
    chunk = jnp.concatenate(lines, axis=0)
    for peer in range(chunk_ref.shape[0]):
        chunk_ref[peer] = chunk
    for k, other in ((3, 4), (4, 3)):
        lines = [secondm[k, half, 8 + 2 * m : 9 + 2 * m] for half in range(2) for m in range(4)]
        lines += [secondm[other, half, at_row : at_row + 1] for at_row in (6, 16) for half in range(2)]
        lines += [root[at_row : at_row + 1] for at_row in (4, 16)]
        lines += [jnp.zeros((2, LANES), F32)]
        ends_ref[k - 3] = jnp.concatenate(lines, axis=0)

    own_rows = pl.ds(8, 8)
    for k in range(5):
        fx_out[k] = fx[REACH - 1 + k, :, own_rows]
        fxm_out[k] = fxm[1 + k]
    for k in range(4):
        p = REACH + k
        fy_out[k] = fy[p]
        fz_out[k] = fz[p, :, own_rows]
        w_out[k] = weight[p, :, own_rows]
        s_out[k] = source[p, :, own_rows]
        fym_out[k] = fym[2 + k]
        fzm_out[k] = fzm[2 + k]
        wm_out[k] = weightm[2 + k]
        sm_out[k] = sourcem[2 + k]
        vm_out[k] = secondm[2 + k]
    for k in range(6):
        v_out[k] = second[REACH - 1 + k]


def window_kernel(spot_ref, got_ref, ends_ref, other_ref, out_ref, chunk):
    place = spot_ref[4]
    core = spot_ref[5]
    base = spot_ref[1] - core
    count = got_ref.shape[0]
    for step in range(SPAN // 2):
        block = base + (step - 4)
        inside = jnp.where((block >= 0) & (block < count), 1.0, 0.0).astype(F32)
        value = got_ref[jnp.clip(block, 0, count - 1), pl.ds(0, 8)] * inside
        for which in range(4):
            chunk[pl.ds(SPAN * which + 2 * step, 2)] = value[2 * which : 2 * which + 2]
    body = chunk[...]
    size = out_ref.shape[0]
    first = (core == 0).astype(F32)
    for peer in range(size):
        out_ref[peer, pl.ds(0, 4 * SPAN)] = body
        ahead = (lax.rem(peer - place + size, size) == 1).astype(F32)
        mine = ends_ref[0] * ahead + ends_ref[1] * (1.0 - ahead)
        other = other_ref[0] * ahead + other_ref[1] * (1.0 - ahead)
        out_ref[peer, pl.ds(4 * SPAN, 16)] = mine * first + other * (1.0 - first)
        out_ref[peer, pl.ds(4 * SPAN + 16, 16)] = other * first + mine * (1.0 - first)


def down_kernel(
    spot_ref, took1_ref, took2_ref, mid_ref, gave1_ref, gave2_ref, rows_ref, fx, fy, fz, w, s, v2,
    fxm, fym, fzm, wm, sm, vm, root,
    out_ref,
    parts, state, ends, field, third, total,
):
    mine_y = spot_ref[1]
    place = spot_ref[4]
    count_y = rows_ref.shape[0]
    width = 2 * WINDOW + 1
    lane = iota((ROWS, LANES), 1)
    row = iota((ROWS, LANES), 0)

    lower_core = spot_ref[5] == 0
    block = mid_ref.shape[0]
    sources = (
        (took2_ref, gave2_ref), (took1_ref, gave1_ref), (mid_ref, None), (gave1_ref, took1_ref), (gave2_ref, took2_ref)
    )
    for number, (one, two) in enumerate(sources):
        for plane in range(block):
            at = number * block + plane

            def read(first, rows):
                value = one[plane, pl.ds(first, rows)]
                if two is not None:
                    value = jnp.where(lower_core, value, two[plane, pl.ds(first, rows)])
                return value

            for which in range(4):
                value = jnp.where(row < SPAN, read(SPAN * which, ROWS), 0.0)
                parts[which, at] = value
                if which == 0:
                    state[0, at] = value
            ends[at] = jnp.where(lower_core, read(4 * SPAN, 16), read(4 * SPAN + 16, 16))

    for turn in range(1, WINDOW):
        old = (turn - 1) % 2
        new = turn % 2
        for step in range(turn, width - turn):
            here = place + step
            v = state[old, here]
            cy = parts[2, here]
            cz = parts[3, here]
            value = KEEP * v + parts[0, here]
            value = value + parts[1, here] * state[old, here + 1] + parts[1, here - 1] * state[old, here - 1]
            value = value + cy * row_roll(v, -1) + row_roll(cy * v, 1)
            value = value + cz * lane_roll(v, -1) + lane_roll(cz * v, 1)
            state[new, here] = value

    def swap_rows(value, line, first, stop):
        return jnp.where((row >= first) & (row < stop), jnp.broadcast_to(line, (ROWS, LANES)), value)

    def corners(value, at):
        halves = []
        for half in range(2):
            part = swap_rows(value[half], ends[at, pl.ds(8 + half, 1)], 6, 8)
            halves.append(swap_rows(part, ends[at, pl.ds(10 + half, 1)], 16, 18))
        return jnp.stack(halves)

    last = (WINDOW - 1) % 2
    spread = []
    for big in range(3):
        value = state[last, place + WINDOW - 1 + big]
        picked = jnp.zeros((ROWS, LANES), F32)
        for k in range(4):
            line = jnp.where(lower_core, value[7 + k : 8 + k], value[9 + k : 10 + k])
            line = jnp.broadcast_to(line, (ROWS, LANES))
            picked = jnp.where((row >= 4 + 4 * k) & (row < 8 + 4 * k), line, picked)
        scale = root[big]
        if big != 1:
            beside = place + WINDOW - 1 + big
            scale = swap_rows(scale, ends[beside, pl.ds(12, 1)], 4, 8)
            scale = swap_rows(scale, ends[beside, pl.ds(13, 1)], 16, 20)
        spread.append(picked * scale)

    def line_block(at):
        halves = []
        for half in range(2):
            rows = []
            for m in range(4):
                line = ends[at, pl.ds(4 * half + m, 1)]
                rows += [line, line]
            pad = jnp.zeros((8, LANES), F32)
            halves.append(jnp.concatenate([pad] + [jnp.concatenate(rows, axis=0)] + [pad], axis=0))
        return jnp.stack(halves)

    field[0] = line_block(place + WINDOW - 1) + spread[0]
    field[5] = line_block(place + WINDOW + 1) + spread[2]
    field[1] = corners(vm[0], place + WINDOW - 1) + spread[0]
    field[4] = corners(vm[3], place + WINDOW + 1) + spread[2]
    left = jnp.where(mine_y > 0, 1.0, 0.0).astype(F32)
    right = jnp.where(mine_y < count_y - 1, 1.0, 0.0).astype(F32)
    left_spot = jnp.maximum(mine_y - 1, 0)
    right_spot = jnp.minimum(mine_y + 1, count_y - 1)
    for k in range(2):
        halves = []
        for half in range(2):
            value = vm[1 + k, half]
            lower = rows_ref[left_spot, pl.ds(12 + 2 * k + half, 1)] * left
            upper = rows_ref[right_spot, pl.ds(8 + 2 * k + half, 1)] * right
            halves.append(swap_rows(swap_rows(value, lower, 4, 6), upper, 18, 20))
        field[2 + k] = jnp.stack(halves) + spread[1]

    for k in range(4):
        v = field[k + 1]
        image = middle_sum(fxm[k + 1], fxm[k], fym[k], fzm[k], field[k + 2], field[k], v)
        third[k] = KEEP * v + wm[k] * (sm[k] + image)

    for p in range(6):
        mid = third[(p + 1) // 2]
        total[p] = v2[p] + jnp.stack([mid[0], mid[0], mid[1], mid[1]])

    lane8 = iota((8, LANES), 1)
    for p in range(4):
        up = total[p + 2, :, pl.ds(8, 8)]
        low = total[p, :, pl.ds(8, 8)]
        v = total[p + 1, :, pl.ds(8, 8)]
        image = fx[p + 1] * up + fx[p] * low
        image = image + fy[p, :, pl.ds(8, 8)] * total[p + 1, :, pl.ds(9, 8)]
        image = image + fy[p, :, pl.ds(7, 8)] * total[p + 1, :, pl.ds(7, 8)]
        zc = fz[p]
        end = jnp.where(lane8 == LANES - 1, 0.0, lane_roll(v[0], -1))
        begin = jnp.where(lane8 == 0, 0.0, lane_roll(zc[3] * v[3], 1))
        below_z = [begin, zc[0] * v[0], zc[1] * v[1], zc[2] * v[2]]
        above_z = [zc[0] * v[1], zc[1] * v[2], zc[2] * v[3], zc[3] * end]
        done = []
        for r in range(4):
            done.append(KEEP * v[r] + w[p, r] * (s[p, r] + image[r] + below_z[r] + above_z[r]))
        for j in range(4):
            index = 32 * j + lane8 // 4
            moved = [pick(done[r], index) for r in range(4)]
            odd = lane8 % 4
            low_pair = jnp.where(odd == 0, moved[0], moved[1])
            high_pair = jnp.where(odd == 2, moved[2], moved[3])
            out_ref[p, :, LANES * j : LANES * (j + 1)] = jnp.where(odd < 2, low_pair, high_pair)


VMEM = pl.BlockSpec(memory_space=pltpu.VMEM)
SMEM = pl.BlockSpec(memory_space=pltpu.SMEM)
HBM = pl.BlockSpec(memory_space=pltpu.HBM)
PARAMS = pltpu.CompilerParams(vmem_limit_bytes=48 * 1024 * 1024)
GX = ("ya", "xa")
GY = ("za", "ca")


def call(kernel, specs, outs, scratch, *args):
    return pl.pallas_call(
        kernel,
        in_specs=specs,
        out_specs=[VMEM] * len(outs),
        out_shape=[jax.ShapeDtypeStruct(shape, F32) for shape in outs],
        scratch_shapes=scratch,
        compiler_params=PARAMS,
    )(*args)


def shifted(value, axis, step):
    count = lax.axis_size(axis)
    if step > 0:
        pairs = [(i, i + step) for i in range(count - step)]
    else:
        pairs = [(i - step, i) for i in range(count + step)]
    return lax.ppermute(value, axis, pairs)


def parted(value, step):
    pairs = []
    for i in range(lax.axis_size("ya") - step):
        pairs.append((2 * i, 2 * (i + step)))
        pairs.append((2 * (i + step) + 1, 2 * i + 1))
    return lax.ppermute(value, ("ya", "ca"), pairs)


def swapped(value):
    return lax.ppermute(value, "ca", [(0, 1), (1, 0)])


def shards(right_side, labels, conduct_table):
    nx = lax.axis_size(GX)
    ny = lax.axis_size(GY)
    block = lax.axis_size("xa")
    numbers = [lax.axis_index(GX), lax.axis_index(GY), jnp.int32(nx), jnp.int32(ny), lax.axis_index("xa"), lax.axis_index("ca")]
    spot = jnp.stack(numbers).astype(jnp.int32)

    fine = (4, ROWS, LANES)
    mid = (2, ROWS, LANES)
    tile = (4, 8, LANES)

    def room(*shape):
        return pltpu.VMEM(shape, F32)

    own, pairs = call(
        split_kernel, [HBM] * 3, [(4, 2, 4, 8, LANES), (8, LANES)],
        [
            pltpu.SMEM(conduct_table.shape, F32), pltpu.VMEM(labels.shape, jnp.int32), room(*right_side.shape),
            pltpu.SemaphoreType.DMA((3,)),
        ],
        *(pltpu.with_memory_space_constraint(value, pltpu.HBM) for value in (conduct_table, labels, right_side)),
    )
    low = shifted(own, GY, 1)
    high = shifted(own, GY, -1)
    near = (4, NEAR_ROWS, LANES)
    far = (4, FAR_ROWS, LANES)
    wide, up1, down1, up2, down2 = call(
        join_kernel, [VMEM] * 3, [(4, 2) + fine, near, near, far, far], [], low, own, high
    )
    low1 = shifted(up1, GX, 1)
    high1 = shifted(down1, GX, -1)
    low2 = shifted(up2, GX, 2)
    high2 = shifted(down2, GX, -2)

    outs = call(
        up_kernel,
        [SMEM] + [VMEM] * 6,
        [
            (ny, 16, LANES), (2, 16, LANES),
            (5,) + tile, (4,) + fine, (4,) + tile, (4,) + tile, (4,) + tile, (6,) + fine,
            (5,) + mid, (4,) + mid, (4,) + mid, (4,) + mid, (4,) + mid, (4,) + mid,
            (3, ROWS, LANES),
        ],
        [pltpu.VMEM((PLANES,) + fine, jnp.int32), room(PLANES, *fine)]
        + [room(PLANES, *fine)] * 3
        + [room(PLANES, ROWS, LANES)]
        + [room(PLANES, *fine)] * 4
        + [room(8, *mid)] * 3
        + [room(8, ROWS, LANES)]
        + [room(8, *mid)] * 5,
        spot, pairs, low2, low1, wide, high1, high2,
    )
    chunk, ends = outs[:2]
    rows = lax.all_to_all(chunk, GY, 0, 0, tiled=True)
    other = swapped(ends)
    window = (block, 4 * SPAN + 32, LANES)
    (planes,) = call(
        window_kernel, [SMEM] + [VMEM] * 3, [window], [room(4 * SPAN, LANES)], spot, rows, ends, other
    )
    planes = lax.all_to_all(planes, "xa", 0, 0, tiled=True)
    took1 = parted(planes, 1)
    took2 = parted(planes, 2)
    blocks = [took1, took2, planes, swapped(took1), swapped(took2)]
    (correction,) = call(
        down_kernel,
        [SMEM] + [VMEM] * 19,
        [(4, 8, 4 * LANES)],
        [
            room(4, 5 * block, ROWS, LANES), room(2, 5 * block, ROWS, LANES), room(5 * block, 16, LANES),
            room(6, *mid), room(4, *mid), room(6, *fine),
        ],
        spot, *blocks, rows, *outs[2:],
    )
    return correction


def solution(mesh):
    mesh = Mesh(mesh.devices.reshape(-1, 4, mesh.devices.shape[1] // 2, 2), GX + GY)
    spec = P(GX, GY, None)
    return jax.shard_map(shards, mesh=mesh, in_specs=(spec, spec, P()), out_specs=spec, check_vma=False)
```

```python
import jax
import jax.numpy as jnp
from jax import lax
from jax.experimental import pallas as pl
from jax.experimental.pallas import tpu as pltpu
from jax.sharding import Mesh
from jax.sharding import PartitionSpec as P

F32 = jnp.float32
LANES = 128
ROWS = 24
REACH = 7
PLANES = 4 + 2 * REACH
WINDOW = 8
SPAN = 20
CORE = 12
KEEP = 0.2
OMEGA = 0.8


def iota(shape, dim):
    return lax.broadcasted_iota(jnp.int32, shape, dim)


def pick(values, index):
    return jnp.take_along_axis(values, index, axis=1)


def lane_roll(value, shift):
    return pltpu.roll(value, shift % LANES, value.ndim - 1)


def row_roll(value, shift):
    return pltpu.roll(value, shift % value.shape[-2], value.ndim - 2)


def split_kernel(table_hbm, labels_hbm, source_hbm, out_ref, pairs_ref, table_ref, labels_ref, source_ref, done):
    copies = [
        pltpu.make_async_copy(src, dst, done.at[k])
        for k, (src, dst) in enumerate(
            ((table_hbm, table_ref), (labels_hbm, labels_ref), (source_hbm, source_ref)))
    ]
    for copy in copies:
        copy.start()
    for copy in copies:
        copy.wait()
    pairs_ref[...] = pair_table(table_ref)
    lane = iota((8, LANES), 1)
    for plane in range(4):
        labels = labels_ref[plane]
        code = jnp.where(labels == 0, 8.0, jnp.where(labels == 1, 9.0, 11.0)).astype(F32)
        source = source_ref[plane]
        for which, values in enumerate((code, source)):
            parts = [values[:, LANES * j : LANES * (j + 1)] for j in range(4)]
            for residue in range(4):
                index = 4 * (lane % 32) + residue
                moved = [pick(part, index) for part in parts]
                low = jnp.where(lane < 32, moved[0], moved[1])
                high = jnp.where(lane < 96, moved[2], moved[3])
                out_ref[plane, which, residue] = jnp.where(lane < 64, low, high)


def layout(first, last):
    spots = []
    offset = 0
    for which in range(2):
        for distance in range(first, last + 1 - which * (last == REACH)):
            reach = REACH - which - distance
            spots.append((which, distance, 8 - reach, 8 + 2 * reach, offset))
            offset += 8 + 2 * reach
    return spots, offset


NEAR, NEAR_ROWS = layout(1, 4)
FAR, FAR_ROWS = layout(5, REACH)


def join_kernel(low_ref, own_ref, high_ref, all_ref, up1_ref, down1_ref, up2_ref, down2_ref):
    for plane in range(4):
        for which in range(2):
            for residue in range(4):
                for part, ref in enumerate((low_ref, own_ref, high_ref)):
                    all_ref[plane, which, residue, pl.ds(8 * part, 8)] = ref[plane, which, residue]
    for spots, start, up_ref, down_ref in ((NEAR, 1, up1_ref, down1_ref), (FAR, 5, up2_ref, down2_ref)):
        for which, distance, row, rows, offset in spots:
            ahead = distance - start
            for residue in range(4):
                out = pl.ds(offset, rows)
                down_ref[residue, out] = all_ref[ahead, which, residue, pl.ds(row, rows)]
                up_ref[residue, out] = all_ref[3 - ahead, which, residue, pl.ds(row, rows)]


def fine_sum(fx_up, fx_low, fy, fz, v_up, v_low, v):
    lane = iota((ROWS, LANES), 1)
    total = fx_up * v_up + fx_low * v_low
    total = total + fy * row_roll(v, -1) + row_roll(fy * v, 1)
    zv = fz * v
    last = jnp.where(lane == LANES - 1, 0.0, lane_roll(v[0], -1))
    first = jnp.where(lane == 0, 0.0, lane_roll(zv[3], 1))
    lower = [first, fz[0] * v[0], fz[1] * v[1], fz[2] * v[2]]
    upper = [fz[0] * v[1], fz[1] * v[2], fz[2] * v[3], fz[3] * last]
    return total + jnp.stack([lower[r] + upper[r] for r in range(4)])


def middle_sum(fx_up, fx_low, fy, fz, v_up, v_low, v):
    lane = iota((ROWS, LANES), 1)
    total = fx_up * v_up + fx_low * v_low
    total = total + fy * row_roll(v, -2) + row_roll(fy * v, 2)
    last = jnp.where(lane == LANES - 1, 0.0, lane_roll(v[0], -1))
    first = jnp.where(lane == 0, 0.0, lane_roll(fz[1] * v[1], 1))
    return total + jnp.stack([first + fz[0] * v[1], fz[0] * v[0] + fz[1] * last])


def both_rows(value, bit):
    row = iota(value.shape, value.ndim - 2)
    return value + jnp.where((row & bit) == 0, row_roll(value, -bit), row_roll(value, bit))


def upper_row(value, bit):
    row = iota(value.shape, value.ndim - 2)
    return jnp.where((row & bit) != 0, value, row_roll(value, -bit))


def pair_table(table_ref):
    lane = iota((8, LANES), 1)

    def at(*keys):
        hit = lane == keys[0]
        for key in keys[1:]:
            hit = hit | (lane == key)
        return hit

    one = jnp.where(at(8, 16, 17, 19), table_ref[0], jnp.where(at(9, 18, 20), table_ref[1], jnp.where(at(11, 22), table_ref[2], 1.0)))
    two = jnp.where(at(8, 16), table_ref[0], jnp.where(at(9, 17, 18), table_ref[1], jnp.where(at(11, 19, 20, 22), table_ref[2], 1.0)))
    return 2.0 * (one * two) / (one + two)


def up_kernel(
    spot_ref, pairs_ref, low2_ref, low1_ref, own_ref, high1_ref, high2_ref,
    chunk_ref, ends_ref, fx_out, fy_out, fz_out, w_out, s_out, v_out,
    fxm_out, fym_out, fzm_out, wm_out, sm_out, vm_out, root_out,
    code, source, fx, fy, fz, zlow, diag, weight, first, second,
    fxm, fym, fzm, zlowm, diagm, weightm, sourcem, firstm, secondm,
):
    x0 = 4 * spot_ref[0]
    y0 = 8 * spot_ref[1]
    nx = 4 * spot_ref[2]
    ny = 8 * spot_ref[3]
    table = pairs_ref[...]
    blank = jnp.zeros((4, ROWS, LANES), F32)
    for k in range(4):
        code[REACH + k] = own_ref[k, 0].astype(jnp.int32)
        source[REACH + k] = own_ref[k, 1]
    for distance in range(1, REACH + 1):
        for p in (REACH - distance, REACH + 3 + distance):
            code[p] = blank.astype(jnp.int32)
            source[p] = blank
    for spots, low_ref, high_ref in ((NEAR, low1_ref, high1_ref), (FAR, low2_ref, high2_ref)):
        for which, distance, row, rows, offset in spots:
            for p, ref in ((REACH - distance, low_ref), (REACH + 3 + distance, high_ref)):
                for residue in range(4):
                    value = ref[residue, pl.ds(offset, rows)]
                    if which == 0:
                        code[p, residue, pl.ds(row, rows)] = value.astype(jnp.int32)
                    else:
                        source[p, residue, pl.ds(row, rows)] = value

    row = iota((ROWS, LANES), 0)
    lane = iota((ROWS, LANES), 1)
    y = y0 - 8 + row
    rowmask = jnp.where((y >= 0) & (y < ny), 1.0, 0.0)

    def planemask(x):
        return jnp.where((x >= 0) & (x < nx), 1.0, 0.0).astype(F32)

    def look(key):
        flat = key.reshape(-1, LANES)
        parts = [pick(table, flat[8 * k : 8 * k + 8]) for k in range(flat.shape[0] // 8)]
        return jnp.concatenate(parts, axis=0).reshape(key.shape)

    def faces(p, carry):
        here = code[p]
        fx[p] = look(here + code[p + 1])
        fy[p] = look(here + row_roll(here, -1))
        beyond = jnp.where(lane == LANES - 1, 0, lane_roll(here[0], -1))
        after = jnp.stack([here[1], here[2], here[3], beyond])
        fz_here = look(here + after)
        fz[p] = fz_here
        zlow[p] = jnp.where(lane == 0, look(here[0]), lane_roll(fz_here[3], 1))
        return carry

    lax.fori_loop(0, PLANES - 1, faces, 0, unroll=True)

    def start(p, carry):
        fy_here = fy[p]
        fz_here = fz[p]
        lower = jnp.stack([zlow[p], fz_here[0], fz_here[1], fz_here[2]])
        total = fx[p] + fx[p - 1] + fy_here + row_roll(fy_here, 1) + fz_here + lower
        diag[p] = total
        w = (OMEGA * planemask(x0 - REACH + p) * rowmask) / total
        weight[p] = w
        first[p] = w * source[p]
        return carry

    lax.fori_loop(1, PLANES - 1, start, 0, unroll=True)

    def sweep(p, carry):
        v = first[p]
        image = fine_sum(fx[p], fx[p - 1], fy[p], fz[p], first[p + 1], first[p - 1], v)
        second[p] = KEEP * v + weight[p] * (source[p] + image)
        return carry

    lax.fori_loop(2, PLANES - 2, sweep, 0, unroll=True)

    def halves(value):
        return jnp.stack([value[0] + value[1], value[2] + value[3]])

    def residual(p):
        v = second[p]
        image = fine_sum(fx[p], fx[p - 1], fy[p], fz[p], second[p + 1], second[p - 1], v)
        return source[p] - diag[p] * v + image

    def coarse_face(k, carry):
        fxm[k] = both_rows(halves(fx[2 + 2 * k]), 1)
        return carry

    lax.fori_loop(0, 7, coarse_face, 0, unroll=True)

    def middle(k, carry):
        pa = 1 + 2 * k
        pb = 2 + 2 * k
        sm = both_rows(halves(residual(pa) + residual(pb)), 1)
        fym_here = upper_row(halves(fy[pa] + fy[pb]), 1)
        fz_two = fz[pa] + fz[pb]
        fzm_here = both_rows(jnp.stack([fz_two[1], fz_two[3]]), 1)
        zlow_here = both_rows(zlow[pa] + zlow[pb], 1)
        lower = jnp.stack([zlow_here, fzm_here[0]])
        total = fxm[k] + fxm[k - 1] + fym_here + row_roll(fym_here, 2) + fzm_here + lower
        w = (OMEGA * planemask(x0 - REACH + pa) * rowmask) / total
        fym[k] = fym_here
        fzm[k] = fzm_here
        zlowm[k] = zlow_here
        diagm[k] = total
        weightm[k] = w
        sourcem[k] = sm
        firstm[k] = w * sm
        return carry

    lax.fori_loop(1, 7, middle, 0, unroll=True)

    def middle_sweep(k, carry):
        v = firstm[k]
        image = middle_sum(fxm[k], fxm[k - 1], fym[k], fzm[k], firstm[k + 1], firstm[k - 1], v)
        secondm[k] = KEEP * v + weightm[k] * (sourcem[k] + image)
        return carry

    lax.fori_loop(2, 6, middle_sweep, 0, unroll=True)

    coarse_source = jnp.zeros((ROWS, LANES), F32)
    for k in (3, 4):
        v = secondm[k]
        image = middle_sum(fxm[k], fxm[k - 1], fym[k], fzm[k], secondm[k + 1], secondm[k - 1], v)
        left = sourcem[k] - diagm[k] * v + image
        coarse_source = coarse_source + left[0] + left[1]
    coarse_source = both_rows(coarse_source, 2)

    def xface(big):
        value = fxm[2 * big + 4]
        return both_rows(value[0] + value[1], 2)

    xfaces = {big: xface(big) for big in (-2, -1, 0, 1)}
    roots = {}
    keep = None
    for big in (-1, 0, 1):
        ka = 2 * big + 3
        ysum = fym[ka] + fym[ka + 1]
        yface = upper_row(ysum[0] + ysum[1], 2)
        zsum = fzm[ka] + fzm[ka + 1]
        zface = both_rows(zsum[1], 2)
        zbelow = both_rows(zlowm[ka] + zlowm[ka + 1], 2)
        total = xfaces[big] + xfaces[big - 1] + yface + row_roll(yface, 4) + zface + zbelow
        root = lax.rsqrt(total) * (planemask(x0 + 4 * big) * rowmask)
        roots[big] = root
        root_out[big + 1] = root
        if big == 0:
            keep = (yface, zface)
    root = roots[0]
    cx = OMEGA * xfaces[0] * root * roots[1]
    cy = OMEGA * keep[0] * root * row_roll(root, -4)
    cz = OMEGA * keep[1] * root * jnp.where(lane == LANES - 1, 0.0, lane_roll(root, -1))
    lines = []
    for value in (OMEGA * root * coarse_source, cx, cy, cz):
        lines.append(value[8:9])
        lines.append(value[12:13])
    for at_row in (10, 12):
        for k in (3, 4):
            for half in range(2):
                lines.append(secondm[k, half, at_row : at_row + 1])
    chunk = jnp.concatenate(lines, axis=0)
    for peer in range(chunk_ref.shape[0]):
        chunk_ref[peer] = chunk
    for k, other in ((3, 4), (4, 3)):
        lines = [secondm[k, half, 8 + 2 * m : 9 + 2 * m] for half in range(2) for m in range(4)]
        lines += [secondm[other, half, at_row : at_row + 1] for at_row in (6, 16) for half in range(2)]
        lines += [root[at_row : at_row + 1] for at_row in (4, 16)]
        lines += [jnp.zeros((2, LANES), F32)]
        ends_ref[k - 3] = jnp.concatenate(lines, axis=0)

    own_rows = pl.ds(8, 8)
    for k in range(5):
        fx_out[k] = fx[REACH - 1 + k, :, own_rows]
        fxm_out[k] = fxm[1 + k]
    for k in range(4):
        p = REACH + k
        fy_out[k] = fy[p]
        fz_out[k] = fz[p, :, own_rows]
        w_out[k] = weight[p, :, own_rows]
        s_out[k] = source[p, :, own_rows]
        fym_out[k] = fym[2 + k]
        fzm_out[k] = fzm[2 + k]
        wm_out[k] = weightm[2 + k]
        sm_out[k] = sourcem[2 + k]
        vm_out[k] = secondm[2 + k]
    for k in range(6):
        v_out[k] = second[REACH - 1 + k]


def window_kernel(spot_ref, got_ref, ends_ref, other_ref, out_ref, chunk):
    place = spot_ref[4]
    core = spot_ref[5]
    base = spot_ref[1] - core
    count = got_ref.shape[0]
    for step in range(SPAN // 2):
        block = base + (step - 4)
        inside = jnp.where((block >= 0) & (block < count), 1.0, 0.0).astype(F32)
        value = got_ref[jnp.clip(block, 0, count - 1), pl.ds(0, 8)] * inside
        for which in range(4):
            if 2 <= step < 8:
                at = CORE * which + 2 * step - 4
            else:
                at = 4 * CORE + (SPAN - CORE) * which + (2 * step if step < 2 else 2 * step - CORE)
            chunk[pl.ds(at, 2)] = value[2 * which : 2 * which + 2]
    body = chunk[...]
    size = out_ref.shape[0]
    first = (core == 0).astype(F32)
    for peer in range(size):
        out_ref[peer, pl.ds(0, 4 * SPAN)] = body
        ahead = (lax.rem(peer - place + size, size) == 1).astype(F32)
        mine = ends_ref[0] * ahead + ends_ref[1] * (1.0 - ahead)
        other = other_ref[0] * ahead + other_ref[1] * (1.0 - ahead)
        out_ref[peer, pl.ds(4 * SPAN, 16)] = mine * first + other * (1.0 - first)
        out_ref[peer, pl.ds(4 * SPAN + 16, 16)] = other * first + mine * (1.0 - first)


def down_kernel(
    spot_ref, took1_ref, took2_ref, mid_ref, gave_ref, rows_ref, fx, fy, fz, w, s, v2,
    fxm, fym, fzm, wm, sm, vm, root,
    out_ref,
    parts, state, ends, field, third, total,
):
    mine_y = spot_ref[1]
    place = spot_ref[4]
    count_y = rows_ref.shape[0]
    width = 2 * WINDOW + 1
    lane = iota((ROWS, LANES), 1)
    row = iota((ROWS, LANES), 0)

    lower_core = spot_ref[5] == 0
    block = mid_ref.shape[0]
    gave1_ref = gave_ref.at[:, pl.ds(0, 4 * SPAN + 32)]
    gave2_ref = gave_ref.at[:, pl.ds(4 * SPAN + 32, 4 * CORE)]
    sources = (
        (took2_ref, gave2_ref), (took1_ref, gave1_ref), (mid_ref, None), (gave1_ref, took1_ref), (gave2_ref, took2_ref)
    )
    for number, (one, two) in enumerate(sources):
        for plane in range(block):
            at = number * block + plane

            def read(first, rows):
                value = one[plane, pl.ds(first, rows)]
                if two is not None:
                    value = jnp.where(lower_core, value, two[plane, pl.ds(first, rows)])
                return value

            blank = jnp.zeros((4, LANES), F32)
            for which in range(4):
                below = above = blank
                if 0 < number < 4:
                    outer = read(4 * CORE + (SPAN - CORE) * which, SPAN - CORE)
                    below, above = outer[:4], outer[4:]
                value = jnp.concatenate([below, read(CORE * which, CORE), above, blank], axis=0)
                parts[which, at] = value
                if which == 0:
                    state[0, at] = value
            if 0 < number < 4:
                ends[at] = jnp.where(lower_core, read(4 * SPAN, 16), read(4 * SPAN + 16, 16))

    for turn in range(1, WINDOW):
        old = (turn - 1) % 2
        new = turn % 2
        for step in range(turn, width - turn):
            here = place + step
            v = state[old, here]
            cy = parts[2, here]
            cz = parts[3, here]
            value = KEEP * v + parts[0, here]
            value = value + parts[1, here] * state[old, here + 1] + parts[1, here - 1] * state[old, here - 1]
            value = value + cy * row_roll(v, -1) + row_roll(cy * v, 1)
            value = value + cz * lane_roll(v, -1) + lane_roll(cz * v, 1)
            state[new, here] = value

    def swap_rows(value, line, first, stop):
        return jnp.where((row >= first) & (row < stop), jnp.broadcast_to(line, (ROWS, LANES)), value)

    def corners(value, at):
        halves = []
        for half in range(2):
            part = swap_rows(value[half], ends[at, pl.ds(8 + half, 1)], 6, 8)
            halves.append(swap_rows(part, ends[at, pl.ds(10 + half, 1)], 16, 18))
        return jnp.stack(halves)

    last = (WINDOW - 1) % 2
    spread = []
    for big in range(3):
        value = state[last, place + WINDOW - 1 + big]
        picked = jnp.zeros((ROWS, LANES), F32)
        for k in range(4):
            line = jnp.where(lower_core, value[7 + k : 8 + k], value[9 + k : 10 + k])
            line = jnp.broadcast_to(line, (ROWS, LANES))
            picked = jnp.where((row >= 4 + 4 * k) & (row < 8 + 4 * k), line, picked)
        scale = root[big]
        if big != 1:
            beside = place + WINDOW - 1 + big
            scale = swap_rows(scale, ends[beside, pl.ds(12, 1)], 4, 8)
            scale = swap_rows(scale, ends[beside, pl.ds(13, 1)], 16, 20)
        spread.append(picked * scale)

    def line_block(at):
        halves = []
        for half in range(2):
            rows = []
            for m in range(4):
                line = ends[at, pl.ds(4 * half + m, 1)]
                rows += [line, line]
            pad = jnp.zeros((8, LANES), F32)
            halves.append(jnp.concatenate([pad] + [jnp.concatenate(rows, axis=0)] + [pad], axis=0))
        return jnp.stack(halves)

    field[0] = line_block(place + WINDOW - 1) + spread[0]
    field[5] = line_block(place + WINDOW + 1) + spread[2]
    field[1] = corners(vm[0], place + WINDOW - 1) + spread[0]
    field[4] = corners(vm[3], place + WINDOW + 1) + spread[2]
    left = jnp.where(mine_y > 0, 1.0, 0.0).astype(F32)
    right = jnp.where(mine_y < count_y - 1, 1.0, 0.0).astype(F32)
    left_spot = jnp.maximum(mine_y - 1, 0)
    right_spot = jnp.minimum(mine_y + 1, count_y - 1)
    for k in range(2):
        halves = []
        for half in range(2):
            value = vm[1 + k, half]
            lower = rows_ref[left_spot, pl.ds(12 + 2 * k + half, 1)] * left
            upper = rows_ref[right_spot, pl.ds(8 + 2 * k + half, 1)] * right
            halves.append(swap_rows(swap_rows(value, lower, 4, 6), upper, 18, 20))
        field[2 + k] = jnp.stack(halves) + spread[1]

    for k in range(4):
        v = field[k + 1]
        image = middle_sum(fxm[k + 1], fxm[k], fym[k], fzm[k], field[k + 2], field[k], v)
        third[k] = KEEP * v + wm[k] * (sm[k] + image)

    for p in range(6):
        mid = third[(p + 1) // 2]
        total[p] = v2[p] + jnp.stack([mid[0], mid[0], mid[1], mid[1]])

    lane8 = iota((8, LANES), 1)
    for p in range(4):
        up = total[p + 2, :, pl.ds(8, 8)]
        low = total[p, :, pl.ds(8, 8)]
        v = total[p + 1, :, pl.ds(8, 8)]
        image = fx[p + 1] * up + fx[p] * low
        image = image + fy[p, :, pl.ds(8, 8)] * total[p + 1, :, pl.ds(9, 8)]
        image = image + fy[p, :, pl.ds(7, 8)] * total[p + 1, :, pl.ds(7, 8)]
        zc = fz[p]
        end = jnp.where(lane8 == LANES - 1, 0.0, lane_roll(v[0], -1))
        begin = jnp.where(lane8 == 0, 0.0, lane_roll(zc[3] * v[3], 1))
        below_z = [begin, zc[0] * v[0], zc[1] * v[1], zc[2] * v[2]]
        above_z = [zc[0] * v[1], zc[1] * v[2], zc[2] * v[3], zc[3] * end]
        done = []
        for r in range(4):
            done.append(KEEP * v[r] + w[p, r] * (s[p, r] + image[r] + below_z[r] + above_z[r]))
        for j in range(4):
            index = 32 * j + lane8 // 4
            moved = [pick(done[r], index) for r in range(4)]
            odd = lane8 % 4
            low_pair = jnp.where(odd == 0, moved[0], moved[1])
            high_pair = jnp.where(odd == 2, moved[2], moved[3])
            out_ref[p, :, LANES * j : LANES * (j + 1)] = jnp.where(odd < 2, low_pair, high_pair)


VMEM = pl.BlockSpec(memory_space=pltpu.VMEM)
SMEM = pl.BlockSpec(memory_space=pltpu.SMEM)
HBM = pl.BlockSpec(memory_space=pltpu.HBM)
PARAMS = pltpu.CompilerParams(vmem_limit_bytes=48 * 1024 * 1024)
GX = ("ya", "xa")
GY = ("za", "ca")


def call(kernel, specs, outs, scratch, *args):
    return pl.pallas_call(
        kernel,
        in_specs=specs,
        out_specs=[VMEM] * len(outs),
        out_shape=[jax.ShapeDtypeStruct(shape, F32) for shape in outs],
        scratch_shapes=scratch,
        compiler_params=PARAMS,
    )(*args)


def shifted(value, axis, step):
    count = lax.axis_size(axis)
    if step > 0:
        pairs = [(i, i + step) for i in range(count - step)]
    else:
        pairs = [(i - step, i) for i in range(count + step)]
    return lax.ppermute(value, axis, pairs)


def parted(value, step):
    pairs = []
    for i in range(lax.axis_size("ya") - step):
        pairs.append((2 * i, 2 * (i + step)))
        pairs.append((2 * (i + step) + 1, 2 * i + 1))
    return lax.ppermute(value, ("ya", "ca"), pairs)


def swapped(value):
    return lax.ppermute(value, "ca", [(0, 1), (1, 0)])


def shards(right_side, labels, conduct_table):
    nx = lax.axis_size(GX)
    ny = lax.axis_size(GY)
    block = lax.axis_size("xa")
    numbers = [lax.axis_index(GX), lax.axis_index(GY), jnp.int32(nx), jnp.int32(ny), lax.axis_index("xa"), lax.axis_index("ca")]
    spot = jnp.stack(numbers).astype(jnp.int32)

    fine = (4, ROWS, LANES)
    mid = (2, ROWS, LANES)
    tile = (4, 8, LANES)

    def room(*shape):
        return pltpu.VMEM(shape, F32)

    own, pairs = call(
        split_kernel, [HBM] * 3, [(4, 2, 4, 8, LANES), (8, LANES)],
        [
            pltpu.SMEM(conduct_table.shape, F32), pltpu.VMEM(labels.shape, jnp.int32), room(*right_side.shape),
            pltpu.SemaphoreType.DMA((3,)),
        ],
        *(pltpu.with_memory_space_constraint(value, pltpu.HBM) for value in (conduct_table, labels, right_side)),
    )
    low = shifted(own, GY, 1)
    high = shifted(own, GY, -1)
    near = (4, NEAR_ROWS, LANES)
    far = (4, FAR_ROWS, LANES)
    wide, up1, down1, up2, down2 = call(
        join_kernel, [VMEM] * 3, [(4, 2) + fine, near, near, far, far], [], low, own, high
    )
    low1 = shifted(up1, GX, 1)
    high1 = shifted(down1, GX, -1)
    low2 = shifted(up2, GX, 2)
    high2 = shifted(down2, GX, -2)

    outs = call(
        up_kernel,
        [SMEM] + [VMEM] * 6,
        [
            (ny, 16, LANES), (2, 16, LANES),
            (5,) + tile, (4,) + fine, (4,) + tile, (4,) + tile, (4,) + tile, (6,) + fine,
            (5,) + mid, (4,) + mid, (4,) + mid, (4,) + mid, (4,) + mid, (4,) + mid,
            (3, ROWS, LANES),
        ],
        [pltpu.VMEM((PLANES,) + fine, jnp.int32), room(PLANES, *fine)]
        + [room(PLANES, *fine)] * 3
        + [room(PLANES, ROWS, LANES)]
        + [room(PLANES, *fine)] * 4
        + [room(8, *mid)] * 3
        + [room(8, ROWS, LANES)]
        + [room(8, *mid)] * 5,
        spot, pairs, low2, low1, wide, high1, high2,
    )
    chunk, ends = outs[:2]
    rows = lax.all_to_all(chunk, GY, 0, 0, tiled=True)
    other = swapped(ends)
    window = (block, 4 * SPAN + 32, LANES)
    (planes,) = call(
        window_kernel, [SMEM] + [VMEM] * 3, [window], [room(4 * SPAN, LANES)], spot, rows, ends, other
    )
    planes = lax.all_to_all(planes, "xa", 0, 0, tiled=True)
    planes, middle_rows = lax.optimization_barrier((planes, planes[:, : 4 * CORE]))
    took1 = parted(planes, 1)
    took2 = parted(middle_rows, 2)
    gave = swapped(jnp.concatenate([took1, took2], axis=1))
    blocks = [took1, took2, planes, gave]
    (correction,) = call(
        down_kernel,
        [SMEM] + [VMEM] * 18,
        [(4, 8, 4 * LANES)],
        [
            room(4, 5 * block, ROWS, LANES), room(2, 5 * block, ROWS, LANES), room(5 * block, 16, LANES),
            room(6, *mid), room(4, *mid), room(6, *fine),
        ],
        spot, *blocks, rows, *outs[2:],
    )
    return correction


def solution(mesh):
    mesh = Mesh(mesh.devices.reshape(-1, 4, mesh.devices.shape[1] // 2, 2), GX + GY)
    spec = P(GX, GY, None)
    return jax.shard_map(shards, mesh=mesh, in_specs=(spec, spec, P()), out_specs=spec, check_vma=False)
```

```python
import jax
import jax.numpy as jnp
from jax import lax
from jax.experimental import pallas as pl
from jax.experimental.pallas import tpu as pltpu
from jax.sharding import Mesh
from jax.sharding import PartitionSpec as P

F32 = jnp.float32
LANES = 128
ROWS = 24
REACH = 7
PLANES = 4 + 2 * REACH
WINDOW = 8
SPAN = 20
CORE = 12
KEEP = 0.2
OMEGA = 0.8


def iota(shape, dim):
    return lax.broadcasted_iota(jnp.int32, shape, dim)


def pick(values, index):
    return jnp.take_along_axis(values, index, axis=1)


def lane_roll(value, shift):
    return pltpu.roll(value, shift % LANES, value.ndim - 1)


def row_roll(value, shift):
    return pltpu.roll(value, shift % value.shape[-2], value.ndim - 2)


def split_kernel(table_hbm, labels_hbm, source_hbm, out_ref, pairs_ref, table_ref, labels_ref, source_ref, done):
    copies = [
        pltpu.make_async_copy(src, dst, done.at[k])
        for k, (src, dst) in enumerate(
            ((table_hbm, table_ref), (labels_hbm, labels_ref), (source_hbm, source_ref)))
    ]
    for copy in copies:
        copy.start()
    for copy in copies:
        copy.wait()
    pairs_ref[...] = pair_table(table_ref)
    lane = iota((8, LANES), 1)
    for plane in range(4):
        labels = labels_ref[plane]
        code = jnp.where(labels == 0, 8.0, jnp.where(labels == 1, 9.0, 11.0)).astype(F32)
        source = source_ref[plane]
        for which, values in enumerate((code, source)):
            parts = [values[:, LANES * j : LANES * (j + 1)] for j in range(4)]
            for residue in range(4):
                index = 4 * (lane % 32) + residue
                moved = [pick(part, index) for part in parts]
                low = jnp.where(lane < 32, moved[0], moved[1])
                high = jnp.where(lane < 96, moved[2], moved[3])
                out_ref[plane, which, residue] = jnp.where(lane < 64, low, high)


def layout(first, last):
    spots = []
    offset = 0
    for which in range(2):
        for distance in range(first, last + 1 - which * (last == REACH)):
            reach = REACH - which - distance
            spots.append((which, distance, 8 - reach, 8 + 2 * reach, offset))
            offset += 8 + 2 * reach
    return spots, offset


NEAR, NEAR_ROWS = layout(1, 4)
FAR, FAR_ROWS = layout(5, REACH)


def join_kernel(low_ref, own_ref, high_ref, all_ref, up1_ref, down1_ref, up2_ref, down2_ref):
    for plane in range(4):
        for which in range(2):
            for residue in range(4):
                for part, ref in enumerate((low_ref, own_ref, high_ref)):
                    all_ref[plane, which, residue, pl.ds(8 * part, 8)] = ref[plane, which, residue]
    for spots, start, up_ref, down_ref in ((NEAR, 1, up1_ref, down1_ref), (FAR, 5, up2_ref, down2_ref)):
        for which, distance, row, rows, offset in spots:
            ahead = distance - start
            for residue in range(4):
                out = pl.ds(offset, rows)
                down_ref[residue, out] = all_ref[ahead, which, residue, pl.ds(row, rows)]
                up_ref[residue, out] = all_ref[3 - ahead, which, residue, pl.ds(row, rows)]


def middle_sum(fx_up, fx_low, fy, fz, v_up, v_low, v):
    lane = iota((ROWS, LANES), 1)
    total = fx_up * v_up + fx_low * v_low
    total = total + fy * row_roll(v, -2) + row_roll(fy * v, 2)
    last = jnp.where(lane == LANES - 1, 0.0, lane_roll(v[0], -1))
    first = jnp.where(lane == 0, 0.0, lane_roll(fz[1] * v[1], 1))
    return total + jnp.stack([first + fz[0] * v[1], fz[0] * v[0] + fz[1] * last])


def both_rows(value, bit):
    row = iota(value.shape, value.ndim - 2)
    return value + jnp.where((row & bit) == 0, row_roll(value, -bit), row_roll(value, bit))


def upper_row(value, bit):
    row = iota(value.shape, value.ndim - 2)
    return jnp.where((row & bit) != 0, value, row_roll(value, -bit))


def pair_table(table_ref):
    lane = iota((8, LANES), 1)

    def at(*keys):
        hit = lane == keys[0]
        for key in keys[1:]:
            hit = hit | (lane == key)
        return hit

    one = jnp.where(at(8, 16, 17, 19), table_ref[0], jnp.where(at(9, 18, 20), table_ref[1], jnp.where(at(11, 22), table_ref[2], 1.0)))
    two = jnp.where(at(8, 16), table_ref[0], jnp.where(at(9, 17, 18), table_ref[1], jnp.where(at(11, 19, 20, 22), table_ref[2], 1.0)))
    return 2.0 * (one * two) / (one + two)


def up_kernel(
    spot_ref, pairs_ref, low2_ref, low1_ref, own_ref, high1_ref, high2_ref,
    chunk_ref, ends_ref, fx_out, fy_out, fz_out, w_out, s_out, v_out,
    fxm_out, fym_out, fzm_out, wm_out, sm_out, vm_out, root_out,
    code, source, fx, fy, fz, zlow, diag, weight, first, second,
    fxm, fym, fzm, zlowm, diagm, weightm, sourcem, firstm, secondm,
):
    x0 = 4 * spot_ref[0]
    y0 = 8 * spot_ref[1]
    nx = 4 * spot_ref[2]
    ny = 8 * spot_ref[3]
    table = pairs_ref[...]
    blank = jnp.zeros((4, ROWS, LANES), F32)
    for k in range(4):
        code[REACH + k] = own_ref[k, 0].astype(jnp.int32)
        source[REACH + k] = own_ref[k, 1]
    for distance in range(1, REACH + 1):
        for p in (REACH - distance, REACH + 3 + distance):
            code[p] = blank.astype(jnp.int32)
            source[p] = blank
    for spots, low_ref, high_ref in ((NEAR, low1_ref, high1_ref), (FAR, low2_ref, high2_ref)):
        for which, distance, row, rows, offset in spots:
            for p, ref in ((REACH - distance, low_ref), (REACH + 3 + distance, high_ref)):
                for residue in range(4):
                    value = ref[residue, pl.ds(offset, rows)]
                    if which == 0:
                        code[p, residue, pl.ds(row, rows)] = value.astype(jnp.int32)
                    else:
                        source[p, residue, pl.ds(row, rows)] = value

    row = iota((ROWS, LANES), 0)
    lane = iota((ROWS, LANES), 1)
    y = y0 - 8 + row
    rowmask = jnp.where((y >= 0) & (y < ny), 1.0, 0.0)

    def planemask(x):
        return jnp.where((x >= 0) & (x < nx), 1.0, 0.0).astype(F32)

    def look(key):
        flat = key.reshape(-1, LANES)
        parts = [pick(table, flat[8 * k : 8 * k + 8]) for k in range(flat.shape[0] // 8)]
        return jnp.concatenate(parts, axis=0).reshape(key.shape)

    def faces(p, carry):
        here = [code[p, r] for r in range(4)]
        after = here[1:] + [jnp.where(lane == LANES - 1, 0, lane_roll(here[0], -1))]
        for r in range(4):
            fx[p, r] = look(here[r] + code[p + 1, r])
            fy[p, r] = look(here[r] + row_roll(here[r], -1))
            across = look(here[r] + after[r])
            fz[p, r] = across
        zlow[p] = jnp.where(lane == 0, look(here[0]), lane_roll(across, 1))
        return carry

    lax.fori_loop(0, PLANES - 1, faces, 0, unroll=True)

    def start(p, carry):
        mask = (OMEGA * planemask(x0 - REACH + p)) * rowmask
        lower = zlow[p]
        for r in range(4):
            fy_here = fy[p, r]
            upper = fz[p, r]
            total = fx[p, r] + fx[p - 1, r] + fy_here + row_roll(fy_here, 1) + upper + lower
            lower = upper
            diag[p, r] = total
            w = mask / total
            weight[p, r] = w
            first[p, r] = w * source[p, r]
        return carry

    lax.fori_loop(1, PLANES - 1, start, 0, unroll=True)

    def image(field, p):
        v = [field[p, r] for r in range(4)]
        along = [fz[p, r] * v[r] for r in range(4)]
        below = [jnp.where(lane == 0, 0.0, lane_roll(along[3], 1))] + along[:3]
        above = v[1:] + [jnp.where(lane == LANES - 1, 0.0, lane_roll(v[0], -1))]
        sums = []
        for r in range(4):
            fy_here = fy[p, r]
            total = fx[p, r] * field[p + 1, r] + fx[p - 1, r] * field[p - 1, r]
            total = total + fy_here * row_roll(v[r], -1) + row_roll(fy_here * v[r], 1)
            sums.append(total + (below[r] + fz[p, r] * above[r]))
        return v, sums

    def sweep(p, carry):
        v, sums = image(first, p)
        for r in range(4):
            second[p, r] = KEEP * v[r] + weight[p, r] * (source[p, r] + sums[r])
        return carry

    lax.fori_loop(2, PLANES - 2, sweep, 0, unroll=True)

    def halves(value):
        return jnp.stack([value[0] + value[1], value[2] + value[3]])

    def residual(p):
        v, sums = image(second, p)
        return jnp.stack([source[p, r] - diag[p, r] * v[r] + sums[r] for r in range(4)])

    def coarse_face(k, carry):
        fxm[k] = both_rows(halves(fx[2 + 2 * k]), 1)
        return carry

    lax.fori_loop(0, 7, coarse_face, 0, unroll=True)

    def middle(k, carry):
        pa = 1 + 2 * k
        pb = 2 + 2 * k
        sm = both_rows(halves(residual(pa) + residual(pb)), 1)
        fym_here = upper_row(halves(fy[pa] + fy[pb]), 1)
        fz_two = fz[pa] + fz[pb]
        fzm_here = both_rows(jnp.stack([fz_two[1], fz_two[3]]), 1)
        zlow_here = both_rows(zlow[pa] + zlow[pb], 1)
        lower = jnp.stack([zlow_here, fzm_here[0]])
        total = fxm[k] + fxm[k - 1] + fym_here + row_roll(fym_here, 2) + fzm_here + lower
        w = (OMEGA * planemask(x0 - REACH + pa) * rowmask) / total
        fym[k] = fym_here
        fzm[k] = fzm_here
        zlowm[k] = zlow_here
        diagm[k] = total
        weightm[k] = w
        sourcem[k] = sm
        firstm[k] = w * sm
        return carry

    lax.fori_loop(1, 7, middle, 0, unroll=True)

    def middle_sweep(k, carry):
        v = firstm[k]
        near = middle_sum(fxm[k], fxm[k - 1], fym[k], fzm[k], firstm[k + 1], firstm[k - 1], v)
        secondm[k] = KEEP * v + weightm[k] * (sourcem[k] + near)
        return carry

    lax.fori_loop(2, 6, middle_sweep, 0, unroll=True)

    coarse_source = jnp.zeros((ROWS, LANES), F32)
    for k in (3, 4):
        v = secondm[k]
        near = middle_sum(fxm[k], fxm[k - 1], fym[k], fzm[k], secondm[k + 1], secondm[k - 1], v)
        left = sourcem[k] - diagm[k] * v + near
        coarse_source = coarse_source + left[0] + left[1]
    coarse_source = both_rows(coarse_source, 2)

    def xface(big):
        value = fxm[2 * big + 4]
        return both_rows(value[0] + value[1], 2)

    xfaces = {big: xface(big) for big in (-2, -1, 0, 1)}
    roots = {}
    keep = None
    for big in (-1, 0, 1):
        ka = 2 * big + 3
        ysum = fym[ka] + fym[ka + 1]
        yface = upper_row(ysum[0] + ysum[1], 2)
        zsum = fzm[ka] + fzm[ka + 1]
        zface = both_rows(zsum[1], 2)
        zbelow = both_rows(zlowm[ka] + zlowm[ka + 1], 2)
        total = xfaces[big] + xfaces[big - 1] + yface + row_roll(yface, 4) + zface + zbelow
        root = lax.rsqrt(total) * (planemask(x0 + 4 * big) * rowmask)
        roots[big] = root
        root_out[big + 1] = root
        if big == 0:
            keep = (yface, zface)
    root = roots[0]
    cx = OMEGA * xfaces[0] * root * roots[1]
    cy = OMEGA * keep[0] * root * row_roll(root, -4)
    cz = OMEGA * keep[1] * root * jnp.where(lane == LANES - 1, 0.0, lane_roll(root, -1))
    lines = []
    for value in (OMEGA * root * coarse_source, cx, cy, cz):
        lines.append(value[8:9])
        lines.append(value[12:13])
    for at_row in (10, 12):
        for k in (3, 4):
            for half in range(2):
                lines.append(secondm[k, half, at_row : at_row + 1])
    chunk = jnp.concatenate(lines, axis=0)
    for peer in range(chunk_ref.shape[0]):
        chunk_ref[peer] = chunk
    for k, other in ((3, 4), (4, 3)):
        lines = [secondm[k, half, 8 + 2 * m : 9 + 2 * m] for half in range(2) for m in range(4)]
        lines += [secondm[other, half, at_row : at_row + 1] for at_row in (6, 16) for half in range(2)]
        lines += [root[at_row : at_row + 1] for at_row in (4, 16)]
        lines += [jnp.zeros((2, LANES), F32)]
        ends_ref[k - 3] = jnp.concatenate(lines, axis=0)

    own_rows = pl.ds(8, 8)
    for k in range(5):
        fx_out[k] = fx[REACH - 1 + k, :, own_rows]
        fxm_out[k] = fxm[1 + k]
    for k in range(4):
        p = REACH + k
        fy_out[k] = fy[p]
        fz_out[k] = fz[p, :, own_rows]
        w_out[k] = weight[p, :, own_rows]
        s_out[k] = source[p, :, own_rows]
        fym_out[k] = fym[2 + k]
        fzm_out[k] = fzm[2 + k]
        wm_out[k] = weightm[2 + k]
        sm_out[k] = sourcem[2 + k]
        vm_out[k] = secondm[2 + k]
    for k in range(6):
        v_out[k] = second[REACH - 1 + k]


def window_kernel(spot_ref, got_ref, ends_ref, other_ref, out_ref, chunk):
    place = spot_ref[4]
    core = spot_ref[5]
    base = spot_ref[1] - core
    count = got_ref.shape[0]
    for step in range(SPAN // 2):
        block = base + (step - 4)
        inside = jnp.where((block >= 0) & (block < count), 1.0, 0.0).astype(F32)
        value = got_ref[jnp.clip(block, 0, count - 1), pl.ds(0, 8)] * inside
        for which in range(4):
            if 2 <= step < 8:
                at = CORE * which + 2 * step - 4
            else:
                at = 4 * CORE + (SPAN - CORE) * which + (2 * step if step < 2 else 2 * step - CORE)
            chunk[pl.ds(at, 2)] = value[2 * which : 2 * which + 2]
    body = chunk[...]
    size = out_ref.shape[0]
    first = (core == 0).astype(F32)
    for peer in range(size):
        out_ref[peer, pl.ds(0, 4 * SPAN)] = body
        ahead = (lax.rem(peer - place + size, size) == 1).astype(F32)
        mine = ends_ref[0] * ahead + ends_ref[1] * (1.0 - ahead)
        other = other_ref[0] * ahead + other_ref[1] * (1.0 - ahead)
        out_ref[peer, pl.ds(4 * SPAN, 16)] = mine * first + other * (1.0 - first)
        out_ref[peer, pl.ds(4 * SPAN + 16, 16)] = other * first + mine * (1.0 - first)


def down_kernel(
    spot_ref, took1_ref, took2_ref, mid_ref, gave_ref, rows_ref, fx, fy, fz, w, s, v2,
    fxm, fym, fzm, wm, sm, vm, root,
    out_ref,
    parts, state, ends, field, third, total,
):
    mine_y = spot_ref[1]
    place = spot_ref[4]
    count_y = rows_ref.shape[0]
    width = 2 * WINDOW + 1
    lane = iota((ROWS, LANES), 1)
    row = iota((ROWS, LANES), 0)

    lower_core = spot_ref[5] == 0
    block = mid_ref.shape[0]
    gave1_ref = gave_ref.at[:, pl.ds(0, 4 * SPAN + 32)]
    gave2_ref = gave_ref.at[:, pl.ds(4 * SPAN + 32, 4 * CORE)]
    sources = (
        (took2_ref, gave2_ref), (took1_ref, gave1_ref), (mid_ref, None), (gave1_ref, took1_ref), (gave2_ref, took2_ref)
    )
    for number, (one, two) in enumerate(sources):
        for plane in range(block):
            at = number * block + plane

            def read(first, rows):
                value = one[plane, pl.ds(first, rows)]
                if two is not None:
                    value = jnp.where(lower_core, value, two[plane, pl.ds(first, rows)])
                return value

            blank = jnp.zeros((4, LANES), F32)
            for which in range(4):
                below = above = blank
                if 0 < number < 4:
                    outer = read(4 * CORE + (SPAN - CORE) * which, SPAN - CORE)
                    below, above = outer[:4], outer[4:]
                value = jnp.concatenate([below, read(CORE * which, CORE), above, blank], axis=0)
                parts[which, at] = value
                if which == 0:
                    state[0, at] = value
            if 0 < number < 4:
                ends[at] = jnp.where(lower_core, read(4 * SPAN, 16), read(4 * SPAN + 16, 16))

    for turn in range(1, WINDOW):
        old = (turn - 1) % 2
        new = turn % 2
        for step in range(turn, width - turn):
            here = place + step
            v = state[old, here]
            cy = parts[2, here]
            cz = parts[3, here]
            value = KEEP * v + parts[0, here]
            value = value + parts[1, here] * state[old, here + 1] + parts[1, here - 1] * state[old, here - 1]
            value = value + cy * row_roll(v, -1) + row_roll(cy * v, 1)
            value = value + cz * lane_roll(v, -1) + lane_roll(cz * v, 1)
            state[new, here] = value

    def swap_rows(value, line, first, stop):
        return jnp.where((row >= first) & (row < stop), jnp.broadcast_to(line, (ROWS, LANES)), value)

    def corners(value, at):
        halves = []
        for half in range(2):
            part = swap_rows(value[half], ends[at, pl.ds(8 + half, 1)], 6, 8)
            halves.append(swap_rows(part, ends[at, pl.ds(10 + half, 1)], 16, 18))
        return jnp.stack(halves)

    last = (WINDOW - 1) % 2
    spread = []
    for big in range(3):
        value = state[last, place + WINDOW - 1 + big]
        picked = jnp.zeros((ROWS, LANES), F32)
        for k in range(4):
            line = jnp.where(lower_core, value[7 + k : 8 + k], value[9 + k : 10 + k])
            line = jnp.broadcast_to(line, (ROWS, LANES))
            picked = jnp.where((row >= 4 + 4 * k) & (row < 8 + 4 * k), line, picked)
        scale = root[big]
        if big != 1:
            beside = place + WINDOW - 1 + big
            scale = swap_rows(scale, ends[beside, pl.ds(12, 1)], 4, 8)
            scale = swap_rows(scale, ends[beside, pl.ds(13, 1)], 16, 20)
        spread.append(picked * scale)

    def line_block(at):
        halves = []
        for half in range(2):
            rows = []
            for m in range(4):
                line = ends[at, pl.ds(4 * half + m, 1)]
                rows += [line, line]
            pad = jnp.zeros((8, LANES), F32)
            halves.append(jnp.concatenate([pad] + [jnp.concatenate(rows, axis=0)] + [pad], axis=0))
        return jnp.stack(halves)

    field[0] = line_block(place + WINDOW - 1) + spread[0]
    field[5] = line_block(place + WINDOW + 1) + spread[2]
    field[1] = corners(vm[0], place + WINDOW - 1) + spread[0]
    field[4] = corners(vm[3], place + WINDOW + 1) + spread[2]
    left = jnp.where(mine_y > 0, 1.0, 0.0).astype(F32)
    right = jnp.where(mine_y < count_y - 1, 1.0, 0.0).astype(F32)
    left_spot = jnp.maximum(mine_y - 1, 0)
    right_spot = jnp.minimum(mine_y + 1, count_y - 1)
    for k in range(2):
        halves = []
        for half in range(2):
            value = vm[1 + k, half]
            lower = rows_ref[left_spot, pl.ds(12 + 2 * k + half, 1)] * left
            upper = rows_ref[right_spot, pl.ds(8 + 2 * k + half, 1)] * right
            halves.append(swap_rows(swap_rows(value, lower, 4, 6), upper, 18, 20))
        field[2 + k] = jnp.stack(halves) + spread[1]

    for k in range(4):
        v = field[k + 1]
        image = middle_sum(fxm[k + 1], fxm[k], fym[k], fzm[k], field[k + 2], field[k], v)
        third[k] = KEEP * v + wm[k] * (sm[k] + image)

    for p in range(6):
        mid = third[(p + 1) // 2]
        total[p] = v2[p] + jnp.stack([mid[0], mid[0], mid[1], mid[1]])

    lane8 = iota((8, LANES), 1)
    for p in range(4):
        up = total[p + 2, :, pl.ds(8, 8)]
        low = total[p, :, pl.ds(8, 8)]
        v = total[p + 1, :, pl.ds(8, 8)]
        image = fx[p + 1] * up + fx[p] * low
        image = image + fy[p, :, pl.ds(8, 8)] * total[p + 1, :, pl.ds(9, 8)]
        image = image + fy[p, :, pl.ds(7, 8)] * total[p + 1, :, pl.ds(7, 8)]
        zc = fz[p]
        end = jnp.where(lane8 == LANES - 1, 0.0, lane_roll(v[0], -1))
        begin = jnp.where(lane8 == 0, 0.0, lane_roll(zc[3] * v[3], 1))
        below_z = [begin, zc[0] * v[0], zc[1] * v[1], zc[2] * v[2]]
        above_z = [zc[0] * v[1], zc[1] * v[2], zc[2] * v[3], zc[3] * end]
        done = []
        for r in range(4):
            done.append(KEEP * v[r] + w[p, r] * (s[p, r] + image[r] + below_z[r] + above_z[r]))
        for j in range(4):
            index = 32 * j + lane8 // 4
            moved = [pick(done[r], index) for r in range(4)]
            odd = lane8 % 4
            low_pair = jnp.where(odd == 0, moved[0], moved[1])
            high_pair = jnp.where(odd == 2, moved[2], moved[3])
            out_ref[p, :, LANES * j : LANES * (j + 1)] = jnp.where(odd < 2, low_pair, high_pair)


VMEM = pl.BlockSpec(memory_space=pltpu.VMEM)
SMEM = pl.BlockSpec(memory_space=pltpu.SMEM)
HBM = pl.BlockSpec(memory_space=pltpu.HBM)
PARAMS = pltpu.CompilerParams(vmem_limit_bytes=48 * 1024 * 1024)
GX = ("ya", "xa")
GY = ("za", "ca")


def call(kernel, specs, outs, scratch, *args):
    return pl.pallas_call(
        kernel,
        in_specs=specs,
        out_specs=[VMEM] * len(outs),
        out_shape=[jax.ShapeDtypeStruct(shape, F32) for shape in outs],
        scratch_shapes=scratch,
        compiler_params=PARAMS,
    )(*args)


def shifted(value, axis, step):
    count = lax.axis_size(axis)
    if step > 0:
        pairs = [(i, i + step) for i in range(count - step)]
    else:
        pairs = [(i - step, i) for i in range(count + step)]
    return lax.ppermute(value, axis, pairs)


def parted(value, step):
    pairs = []
    for i in range(lax.axis_size("ya") - step):
        pairs.append((2 * i, 2 * (i + step)))
        pairs.append((2 * (i + step) + 1, 2 * i + 1))
    return lax.ppermute(value, ("ya", "ca"), pairs)


def swapped(value):
    return lax.ppermute(value, "ca", [(0, 1), (1, 0)])


def shards(right_side, labels, conduct_table):
    nx = lax.axis_size(GX)
    ny = lax.axis_size(GY)
    block = lax.axis_size("xa")
    numbers = [lax.axis_index(GX), lax.axis_index(GY), jnp.int32(nx), jnp.int32(ny), lax.axis_index("xa"), lax.axis_index("ca")]
    spot = jnp.stack(numbers).astype(jnp.int32)

    fine = (4, ROWS, LANES)
    mid = (2, ROWS, LANES)
    tile = (4, 8, LANES)

    def room(*shape):
        return pltpu.VMEM(shape, F32)

    own, pairs = call(
        split_kernel, [HBM] * 3, [(4, 2, 4, 8, LANES), (8, LANES)],
        [
            pltpu.SMEM(conduct_table.shape, F32), pltpu.VMEM(labels.shape, jnp.int32), room(*right_side.shape),
            pltpu.SemaphoreType.DMA((3,)),
        ],
        *(pltpu.with_memory_space_constraint(value, pltpu.HBM) for value in (conduct_table, labels, right_side)),
    )
    low = shifted(own, GY, 1)
    high = shifted(own, GY, -1)
    near = (4, NEAR_ROWS, LANES)
    far = (4, FAR_ROWS, LANES)
    wide, up1, down1, up2, down2 = call(
        join_kernel, [VMEM] * 3, [(4, 2) + fine, near, near, far, far], [], low, own, high
    )
    low1 = shifted(up1, GX, 1)
    high1 = shifted(down1, GX, -1)
    low2 = shifted(up2, GX, 2)
    high2 = shifted(down2, GX, -2)

    outs = call(
        up_kernel,
        [SMEM] + [VMEM] * 6,
        [
            (ny, 16, LANES), (2, 16, LANES),
            (5,) + tile, (4,) + fine, (4,) + tile, (4,) + tile, (4,) + tile, (6,) + fine,
            (5,) + mid, (4,) + mid, (4,) + mid, (4,) + mid, (4,) + mid, (4,) + mid,
            (3, ROWS, LANES),
        ],
        [pltpu.VMEM((PLANES,) + fine, jnp.int32), room(PLANES, *fine)]
        + [room(PLANES, *fine)] * 3
        + [room(PLANES, ROWS, LANES)]
        + [room(PLANES, *fine)] * 4
        + [room(8, *mid)] * 3
        + [room(8, ROWS, LANES)]
        + [room(8, *mid)] * 5,
        spot, pairs, low2, low1, wide, high1, high2,
    )
    chunk, ends = outs[:2]
    rows = lax.all_to_all(chunk, GY, 0, 0, tiled=True)
    other = swapped(ends)
    window = (block, 4 * SPAN + 32, LANES)
    (planes,) = call(
        window_kernel, [SMEM] + [VMEM] * 3, [window], [room(4 * SPAN, LANES)], spot, rows, ends, other
    )
    planes = lax.all_to_all(planes, "xa", 0, 0, tiled=True)
    planes, middle_rows = lax.optimization_barrier((planes, planes[:, : 4 * CORE]))
    took1 = parted(planes, 1)
    took2 = parted(middle_rows, 2)
    gave = swapped(jnp.concatenate([took1, took2], axis=1))
    blocks = [took1, took2, planes, gave]
    (correction,) = call(
        down_kernel,
        [SMEM] + [VMEM] * 18,
        [(4, 8, 4 * LANES)],
        [
            room(4, 5 * block, ROWS, LANES), room(2, 5 * block, ROWS, LANES), room(5 * block, 16, LANES),
            room(6, *mid), room(4, *mid), room(6, *fine),
        ],
        spot, *blocks, rows, *outs[2:],
    )
    return correction


def solution(mesh):
    mesh = Mesh(mesh.devices.reshape(-1, 4, mesh.devices.shape[1] // 2, 2), GX + GY)
    spec = P(GX, GY, None)
    return jax.shard_map(shards, mesh=mesh, in_specs=(spec, spec, P()), out_specs=spec, check_vma=False)
```

```python
import jax
import jax.numpy as jnp
from jax import lax
from jax.experimental import pallas as pl
from jax.experimental.pallas import tpu as pltpu
from jax.sharding import Mesh
from jax.sharding import PartitionSpec as P

F32 = jnp.float32
LANES = 128
ROWS = 24
REACH = 7
PLANES = 4 + 2 * REACH
WINDOW = 8
SPAN = 20
CORE = 12
KEEP = 0.2
OMEGA = 0.8


def iota(shape, dim):
    return lax.broadcasted_iota(jnp.int32, shape, dim)


def pick(values, index):
    return jnp.take_along_axis(values, index, axis=1)


def lane_roll(value, shift):
    return pltpu.roll(value, shift % LANES, value.ndim - 1)


def row_roll(value, shift):
    return pltpu.roll(value, shift % value.shape[-2], value.ndim - 2)


def split_kernel(table_hbm, labels_hbm, source_hbm, out_ref, pairs_ref, table_ref, labels_ref, source_ref, done):
    copies = [
        pltpu.make_async_copy(src, dst, done.at[k])
        for k, (src, dst) in enumerate(
            ((table_hbm, table_ref), (labels_hbm, labels_ref), (source_hbm, source_ref)))
    ]
    for copy in copies:
        copy.start()
    for copy in copies:
        copy.wait()
    pairs_ref[...] = pair_table(table_ref)
    lane = iota((8, LANES), 1)
    for plane in range(4):
        labels = labels_ref[plane]
        code = jnp.where(labels == 0, 8.0, jnp.where(labels == 1, 9.0, 11.0)).astype(F32)
        source = source_ref[plane]
        for which, values in enumerate((code, source)):
            parts = [values[:, LANES * j : LANES * (j + 1)] for j in range(4)]
            for residue in range(4):
                index = 4 * (lane % 32) + residue
                moved = [pick(part, index) for part in parts]
                low = jnp.where(lane < 32, moved[0], moved[1])
                high = jnp.where(lane < 96, moved[2], moved[3])
                out_ref[plane, which, residue] = jnp.where(lane < 64, low, high)


def layout(first, last):
    spots = []
    offset = 0
    for which in range(2):
        for distance in range(first, last + 1 - which * (last == REACH)):
            reach = REACH - which - distance
            spots.append((which, distance, 8 - reach, 8 + 2 * reach, offset))
            offset += 8 + 2 * reach
    return spots, offset


NEAR, NEAR_ROWS = layout(1, 4)
FAR, FAR_ROWS = layout(5, REACH)


def join_kernel(low_ref, own_ref, high_ref, all_ref, up1_ref, down1_ref, up2_ref, down2_ref):
    for plane in range(4):
        for which in range(2):
            for residue in range(4):
                for part, ref in enumerate((low_ref, own_ref, high_ref)):
                    all_ref[plane, which, residue, pl.ds(8 * part, 8)] = ref[plane, which, residue]
    for spots, start, up_ref, down_ref in ((NEAR, 1, up1_ref, down1_ref), (FAR, 5, up2_ref, down2_ref)):
        for which, distance, row, rows, offset in spots:
            ahead = distance - start
            for residue in range(4):
                out = pl.ds(offset, rows)
                down_ref[residue, out] = all_ref[ahead, which, residue, pl.ds(row, rows)]
                up_ref[residue, out] = all_ref[3 - ahead, which, residue, pl.ds(row, rows)]


def middle_sum(fx_up, fx_low, fy, fz, v_up, v_low, v):
    lane = iota((ROWS, LANES), 1)
    total = fx_up * v_up + fx_low * v_low
    total = total + fy * row_roll(v, -2) + row_roll(fy * v, 2)
    last = jnp.where(lane == LANES - 1, 0.0, lane_roll(v[0], -1))
    first = jnp.where(lane == 0, 0.0, lane_roll(fz[1] * v[1], 1))
    return total + jnp.stack([first + fz[0] * v[1], fz[0] * v[0] + fz[1] * last])


def both_rows(value, bit):
    row = iota(value.shape, value.ndim - 2)
    return value + jnp.where((row & bit) == 0, row_roll(value, -bit), row_roll(value, bit))


def upper_row(value, bit):
    row = iota(value.shape, value.ndim - 2)
    return jnp.where((row & bit) != 0, value, row_roll(value, -bit))


def pair_table(table_ref):
    lane = iota((8, LANES), 1)

    def at(*keys):
        hit = lane == keys[0]
        for key in keys[1:]:
            hit = hit | (lane == key)
        return hit

    one = jnp.where(at(8, 16, 17, 19), table_ref[0], jnp.where(at(9, 18, 20), table_ref[1], jnp.where(at(11, 22), table_ref[2], 1.0)))
    two = jnp.where(at(8, 16), table_ref[0], jnp.where(at(9, 17, 18), table_ref[1], jnp.where(at(11, 19, 20, 22), table_ref[2], 1.0)))
    return 2.0 * (one * two) / (one + two)


def up_kernel(
    spot_ref, pairs_ref, low2_ref, low1_ref, own_ref, high1_ref, high2_ref,
    chunk_ref, ends_ref, edge_ref, fx_out, fy_out, fz_out, w_out, s_out, v_out,
    fxm_out, fym_out, fzm_out, wm_out, sm_out, vm_out, root_out,
    code, source, fx, fy, fz, zlow, diag, weight, first, second,
    fxm, fym, fzm, zlowm, diagm, weightm, sourcem, firstm, secondm,
):
    x0 = 4 * spot_ref[0]
    y0 = 8 * spot_ref[1]
    nx = 4 * spot_ref[2]
    ny = 8 * spot_ref[3]
    table = pairs_ref[...]
    blank = jnp.zeros((4, ROWS, LANES), F32)

    def in_grid(value, row):
        y = y0 - 8 + row + iota(value.shape, value.ndim - 2)
        return jnp.where((y >= 0) & (y < ny), value.astype(jnp.int32), 0)

    for k in range(4):
        code[REACH + k] = in_grid(own_ref[k, 0], 0)
        source[REACH + k] = own_ref[k, 1]
    for distance in range(1, REACH + 1):
        for p in (REACH - distance, REACH + 3 + distance):
            code[p] = blank.astype(jnp.int32)
            source[p] = blank
    for spots, low_ref, high_ref in ((NEAR, low1_ref, high1_ref), (FAR, low2_ref, high2_ref)):
        for which, distance, row, rows, offset in spots:
            for p, ref in ((REACH - distance, low_ref), (REACH + 3 + distance, high_ref)):
                for residue in range(4):
                    value = ref[residue, pl.ds(offset, rows)]
                    if which == 0:
                        code[p, residue, pl.ds(row, rows)] = in_grid(value, row)
                    else:
                        source[p, residue, pl.ds(row, rows)] = value

    row = iota((ROWS, LANES), 0)
    lane = iota((ROWS, LANES), 1)
    y = y0 - 8 + row
    rowmask = jnp.where((y >= 0) & (y < ny), 1.0, 0.0)

    def planemask(x):
        return jnp.where((x >= 0) & (x < nx), 1.0, 0.0).astype(F32)

    def look(key):
        flat = key.reshape(-1, LANES)
        parts = [pick(table, flat[8 * k : 8 * k + 8]) for k in range(flat.shape[0] // 8)]
        return jnp.concatenate(parts, axis=0).reshape(key.shape)

    def faces(p, carry):
        here = [code[p, r] for r in range(4)]
        after = here[1:] + [jnp.where(lane == LANES - 1, 0, lane_roll(here[0], -1))]
        for r in range(4):
            fx[p, r] = look(here[r] + code[p + 1, r])
            fy[p, r] = look(here[r] + row_roll(here[r], -1))
            across = look(here[r] + after[r])
            fz[p, r] = across
        zlow[p] = jnp.where(lane == 0, look(here[0]), lane_roll(across, 1))
        return carry

    lax.fori_loop(0, PLANES - 1, faces, 0, unroll=True)

    def start(p, carry):
        mask = (OMEGA * planemask(x0 - REACH + p)) * rowmask
        lower = zlow[p]
        for r in range(4):
            fy_here = fy[p, r]
            upper = fz[p, r]
            total = fx[p, r] + fx[p - 1, r] + fy_here + row_roll(fy_here, 1) + upper + lower
            lower = upper
            diag[p, r] = total
            w = mask / total
            weight[p, r] = w
            first[p, r] = w * source[p, r]
        return carry

    lax.fori_loop(1, PLANES - 1, start, 0, unroll=True)

    def image(field, p):
        v = [field[p, r] for r in range(4)]
        along = [fz[p, r] * v[r] for r in range(4)]
        below = [jnp.where(lane == 0, 0.0, lane_roll(along[3], 1))] + along[:3]
        above = v[1:] + [jnp.where(lane == LANES - 1, 0.0, lane_roll(v[0], -1))]
        sums = []
        for r in range(4):
            fy_here = fy[p, r]
            total = fx[p, r] * field[p + 1, r] + fx[p - 1, r] * field[p - 1, r]
            total = total + fy_here * row_roll(v[r], -1) + row_roll(fy_here * v[r], 1)
            sums.append(total + (below[r] + fz[p, r] * above[r]))
        return v, sums

    def sweep(p, carry):
        v, sums = image(first, p)
        for r in range(4):
            second[p, r] = KEEP * v[r] + weight[p, r] * (source[p, r] + sums[r])
        return carry

    lax.fori_loop(2, PLANES - 2, sweep, 0, unroll=True)

    def halves(value):
        return jnp.stack([value[0] + value[1], value[2] + value[3]])

    def residual(p):
        v, sums = image(second, p)
        return jnp.stack([source[p, r] - diag[p, r] * v[r] + sums[r] for r in range(4)])

    def coarse_face(k, carry):
        fxm[k] = both_rows(halves(fx[2 + 2 * k]), 1)
        return carry

    lax.fori_loop(0, 7, coarse_face, 0, unroll=True)

    def middle(k, carry):
        pa = 1 + 2 * k
        pb = 2 + 2 * k
        sm = both_rows(halves(residual(pa) + residual(pb)), 1)
        fym_here = upper_row(halves(fy[pa] + fy[pb]), 1)
        fz_two = fz[pa] + fz[pb]
        fzm_here = both_rows(jnp.stack([fz_two[1], fz_two[3]]), 1)
        zlow_here = both_rows(zlow[pa] + zlow[pb], 1)
        lower = jnp.stack([zlow_here, fzm_here[0]])
        total = fxm[k] + fxm[k - 1] + fym_here + row_roll(fym_here, 2) + fzm_here + lower
        w = (OMEGA * planemask(x0 - REACH + pa) * rowmask) / total
        fym[k] = fym_here
        fzm[k] = fzm_here
        zlowm[k] = zlow_here
        diagm[k] = total
        weightm[k] = w
        sourcem[k] = sm
        firstm[k] = w * sm
        return carry

    lax.fori_loop(1, 7, middle, 0, unroll=True)

    def middle_sweep(k, carry):
        v = firstm[k]
        near = middle_sum(fxm[k], fxm[k - 1], fym[k], fzm[k], firstm[k + 1], firstm[k - 1], v)
        secondm[k] = KEEP * v + weightm[k] * (sourcem[k] + near)
        return carry

    lax.fori_loop(2, 6, middle_sweep, 0, unroll=True)

    coarse_source = jnp.zeros((ROWS, LANES), F32)
    for k in (3, 4):
        v = secondm[k]
        near = middle_sum(fxm[k], fxm[k - 1], fym[k], fzm[k], secondm[k + 1], secondm[k - 1], v)
        left = sourcem[k] - diagm[k] * v + near
        coarse_source = coarse_source + left[0] + left[1]
    coarse_source = both_rows(coarse_source, 2)

    def xface(big):
        value = fxm[2 * big + 4]
        return both_rows(value[0] + value[1], 2)

    xfaces = {big: xface(big) for big in (-2, -1, 0, 1)}
    roots = {}
    keep = None
    for big in (-1, 0, 1):
        ka = 2 * big + 3
        ysum = fym[ka] + fym[ka + 1]
        yface = upper_row(ysum[0] + ysum[1], 2)
        zsum = fzm[ka] + fzm[ka + 1]
        zface = both_rows(zsum[1], 2)
        zbelow = both_rows(zlowm[ka] + zlowm[ka + 1], 2)
        total = xfaces[big] + xfaces[big - 1] + yface + row_roll(yface, 4) + zface + zbelow
        root = lax.rsqrt(total) * (planemask(x0 + 4 * big) * rowmask)
        roots[big] = root
        root_out[big + 1] = root
        if big == 0:
            keep = (yface, zface)
    root = roots[0]
    cx = OMEGA * xfaces[0] * root * roots[1]
    cy = OMEGA * keep[0] * root * row_roll(root, -4)
    cz = OMEGA * keep[1] * root * jnp.where(lane == LANES - 1, 0.0, lane_roll(root, -1))
    lines = []
    for value in (OMEGA * root * coarse_source, cx, cy, cz):
        lines.append(value[8:9])
        lines.append(value[12:13])
    chunk = jnp.concatenate(lines, axis=0)
    for peer in range(chunk_ref.shape[0]):
        chunk_ref[peer] = chunk
    first_core = spot_ref[5] == 0

    def edges(sibling):
        rows = []
        for k in (3, 4):
            for half in range(2):
                low = secondm[k, half, 10:11]
                high = secondm[k, half, 12:13]
                rows.append(jnp.where(first_core == sibling, high, low))
        return rows

    edge_ref[...] = jnp.concatenate(edges(False) + [jnp.zeros((4, LANES), F32)], axis=0)
    inside_chip = edges(True)
    for k, other in ((3, 4), (4, 3)):
        lines = [secondm[k, half, 8 + 2 * m : 9 + 2 * m] for half in range(2) for m in range(4)]
        lines += [secondm[other, half, at_row : at_row + 1] for at_row in (6, 16) for half in range(2)]
        lines += [root[at_row : at_row + 1] for at_row in (4, 16)]
        lines += inside_chip[2 * (k - 3) : 2 * (k - 2)]
        ends_ref[k - 3] = jnp.concatenate(lines, axis=0)

    own_rows = pl.ds(8, 8)
    for k in range(5):
        fx_out[k] = fx[REACH - 1 + k, :, own_rows]
        fxm_out[k] = fxm[1 + k]
    for k in range(4):
        p = REACH + k
        fy_out[k] = fy[p]
        fz_out[k] = fz[p, :, own_rows]
        w_out[k] = weight[p, :, own_rows]
        s_out[k] = source[p, :, own_rows]
        fym_out[k] = fym[2 + k]
        fzm_out[k] = fzm[2 + k]
        wm_out[k] = weightm[2 + k]
        sm_out[k] = sourcem[2 + k]
        vm_out[k] = secondm[2 + k]
    for k in range(6):
        v_out[k] = second[REACH - 1 + k]


def window_kernel(spot_ref, got_ref, ends_ref, other_ref, out_ref, chunk):
    place = spot_ref[4]
    core = spot_ref[5]
    base = spot_ref[1] - core
    count = got_ref.shape[0]
    for step in range(SPAN // 2):
        block = base + (step - 4)
        inside = jnp.where((block >= 0) & (block < count), 1.0, 0.0).astype(F32)
        value = got_ref[jnp.clip(block, 0, count - 1), pl.ds(0, 8)] * inside
        for which in range(4):
            if 2 <= step < 8:
                at = CORE * which + 2 * step - 4
            else:
                at = 4 * CORE + (SPAN - CORE) * which + (2 * step if step < 2 else 2 * step - CORE)
            chunk[pl.ds(at, 2)] = value[2 * which : 2 * which + 2]
    body = chunk[...]
    size = out_ref.shape[0]
    first = (core == 0).astype(F32)
    for peer in range(size):
        out_ref[peer, pl.ds(0, 4 * SPAN)] = body
        ahead = (lax.rem(peer - place + size, size) == 1).astype(F32)
        mine = ends_ref[0] * ahead + ends_ref[1] * (1.0 - ahead)
        other = other_ref[0] * ahead + other_ref[1] * (1.0 - ahead)
        out_ref[peer, pl.ds(4 * SPAN, 16)] = mine * first + other * (1.0 - first)
        out_ref[peer, pl.ds(4 * SPAN + 16, 16)] = other * first + mine * (1.0 - first)


def down_kernel(
    spot_ref, took1_ref, took2_ref, mid_ref, gave_ref, other_ref, edge_ref, fx, fy, fz, w, s, v2,
    fxm, fym, fzm, wm, sm, vm, root,
    out_ref,
    parts, state, ends, field, third, total,
):
    place = spot_ref[4]
    width = 2 * WINDOW + 1
    lane = iota((ROWS, LANES), 1)
    row = iota((ROWS, LANES), 0)

    lower_core = spot_ref[5] == 0
    block = mid_ref.shape[0]
    gave1_ref = gave_ref.at[:, pl.ds(0, 4 * SPAN + 32)]
    gave2_ref = gave_ref.at[:, pl.ds(4 * SPAN + 32, 4 * CORE)]
    sources = (
        (took2_ref, gave2_ref), (took1_ref, gave1_ref), (mid_ref, None), (gave1_ref, took1_ref), (gave2_ref, took2_ref)
    )
    for number, (one, two) in enumerate(sources):
        for plane in range(block):
            at = number * block + plane

            def read(first, rows):
                value = one[plane, pl.ds(first, rows)]
                if two is not None:
                    value = jnp.where(lower_core, value, two[plane, pl.ds(first, rows)])
                return value

            blank = jnp.zeros((4, LANES), F32)
            for which in range(4):
                below = above = blank
                if 0 < number < 4:
                    outer = read(4 * CORE + (SPAN - CORE) * which, SPAN - CORE)
                    below, above = outer[:4], outer[4:]
                value = jnp.concatenate([below, read(CORE * which, CORE), above, blank], axis=0)
                parts[which, at] = value
                if which == 0:
                    state[0, at] = value
            if 0 < number < 4:
                ends[at] = jnp.where(lower_core, read(4 * SPAN, 16), read(4 * SPAN + 16, 16))

    for turn in range(1, WINDOW):
        old = (turn - 1) % 2
        new = turn % 2
        for step in range(turn, width - turn):
            here = place + step
            v = state[old, here]
            cy = parts[2, here]
            cz = parts[3, here]
            value = KEEP * v + parts[0, here]
            value = value + parts[1, here] * state[old, here + 1] + parts[1, here - 1] * state[old, here - 1]
            value = value + cy * row_roll(v, -1) + row_roll(cy * v, 1)
            value = value + cz * lane_roll(v, -1) + lane_roll(cz * v, 1)
            state[new, here] = value

    def swap_rows(value, line, first, stop):
        return jnp.where((row >= first) & (row < stop), jnp.broadcast_to(line, (ROWS, LANES)), value)

    def corners(value, at):
        halves = []
        for half in range(2):
            part = swap_rows(value[half], ends[at, pl.ds(8 + half, 1)], 6, 8)
            halves.append(swap_rows(part, ends[at, pl.ds(10 + half, 1)], 16, 18))
        return jnp.stack(halves)

    last = (WINDOW - 1) % 2
    spread = []
    for big in range(3):
        value = state[last, place + WINDOW - 1 + big]
        picked = jnp.zeros((ROWS, LANES), F32)
        for k in range(4):
            line = jnp.where(lower_core, value[7 + k : 8 + k], value[9 + k : 10 + k])
            line = jnp.broadcast_to(line, (ROWS, LANES))
            picked = jnp.where((row >= 4 + 4 * k) & (row < 8 + 4 * k), line, picked)
        scale = root[big]
        if big != 1:
            beside = place + WINDOW - 1 + big
            scale = swap_rows(scale, ends[beside, pl.ds(12, 1)], 4, 8)
            scale = swap_rows(scale, ends[beside, pl.ds(13, 1)], 16, 20)
        spread.append(picked * scale)

    def line_block(at):
        halves = []
        for half in range(2):
            rows = []
            for m in range(4):
                line = ends[at, pl.ds(4 * half + m, 1)]
                rows += [line, line]
            pad = jnp.zeros((8, LANES), F32)
            halves.append(jnp.concatenate([pad] + [jnp.concatenate(rows, axis=0)] + [pad], axis=0))
        return jnp.stack(halves)

    field[0] = line_block(place + WINDOW - 1) + spread[0]
    field[5] = line_block(place + WINDOW + 1) + spread[2]
    field[1] = corners(vm[0], place + WINDOW - 1) + spread[0]
    field[4] = corners(vm[3], place + WINDOW + 1) + spread[2]
    for k in range(2):
        halves = []
        for half in range(2):
            value = vm[1 + k, half]
            sibling = other_ref[k, pl.ds(14 + half, 1)]
            beyond = edge_ref[pl.ds(2 * k + half, 1)]
            lower = jnp.where(lower_core, beyond, sibling)
            upper = jnp.where(lower_core, sibling, beyond)
            halves.append(swap_rows(swap_rows(value, lower, 4, 6), upper, 18, 20))
        field[2 + k] = jnp.stack(halves) + spread[1]

    for k in range(4):
        v = field[k + 1]
        image = middle_sum(fxm[k + 1], fxm[k], fym[k], fzm[k], field[k + 2], field[k], v)
        third[k] = KEEP * v + wm[k] * (sm[k] + image)

    for p in range(6):
        mid = third[(p + 1) // 2]
        total[p] = v2[p] + jnp.stack([mid[0], mid[0], mid[1], mid[1]])

    lane8 = iota((8, LANES), 1)
    for p in range(4):
        up = total[p + 2, :, pl.ds(8, 8)]
        low = total[p, :, pl.ds(8, 8)]
        v = total[p + 1, :, pl.ds(8, 8)]
        image = fx[p + 1] * up + fx[p] * low
        image = image + fy[p, :, pl.ds(8, 8)] * total[p + 1, :, pl.ds(9, 8)]
        image = image + fy[p, :, pl.ds(7, 8)] * total[p + 1, :, pl.ds(7, 8)]
        zc = fz[p]
        end = jnp.where(lane8 == LANES - 1, 0.0, lane_roll(v[0], -1))
        begin = jnp.where(lane8 == 0, 0.0, lane_roll(zc[3] * v[3], 1))
        below_z = [begin, zc[0] * v[0], zc[1] * v[1], zc[2] * v[2]]
        above_z = [zc[0] * v[1], zc[1] * v[2], zc[2] * v[3], zc[3] * end]
        done = []
        for r in range(4):
            done.append(KEEP * v[r] + w[p, r] * (s[p, r] + image[r] + below_z[r] + above_z[r]))
        for j in range(4):
            index = 32 * j + lane8 // 4
            moved = [pick(done[r], index) for r in range(4)]
            odd = lane8 % 4
            low_pair = jnp.where(odd == 0, moved[0], moved[1])
            high_pair = jnp.where(odd == 2, moved[2], moved[3])
            out_ref[p, :, LANES * j : LANES * (j + 1)] = jnp.where(odd < 2, low_pair, high_pair)


VMEM = pl.BlockSpec(memory_space=pltpu.VMEM)
SMEM = pl.BlockSpec(memory_space=pltpu.SMEM)
HBM = pl.BlockSpec(memory_space=pltpu.HBM)
PARAMS = pltpu.CompilerParams(vmem_limit_bytes=48 * 1024 * 1024)
GX = ("ya", "xa")
GY = ("za", "ca")


def call(kernel, specs, outs, scratch, *args):
    return pl.pallas_call(
        kernel,
        in_specs=specs,
        out_specs=[VMEM] * len(outs),
        out_shape=[jax.ShapeDtypeStruct(shape, F32) for shape in outs],
        scratch_shapes=scratch,
        compiler_params=PARAMS,
    )(*args)


def shifted(value, axis, step):
    count = lax.axis_size(axis)
    if step > 0:
        pairs = [(i, i + step) for i in range(count - step)]
    else:
        pairs = [(i - step, i) for i in range(count + step)]
    return lax.ppermute(value, axis, pairs)


def parted(value, step):
    pairs = []
    for i in range(lax.axis_size("ya") - step):
        pairs.append((2 * i, 2 * (i + step)))
        pairs.append((2 * (i + step) + 1, 2 * i + 1))
    return lax.ppermute(value, ("ya", "ca"), pairs)


def shifted_chip(value):
    pairs = []
    for i in range(lax.axis_size("za") - 1):
        pairs.append((2 * i + 1, 2 * i + 2))
        pairs.append((2 * i + 2, 2 * i + 1))
    return lax.ppermute(value, GY, pairs)


def swapped(value):
    return lax.ppermute(value, "ca", [(0, 1), (1, 0)])


def shards(right_side, labels, conduct_table):
    nx = lax.axis_size(GX)
    ny = lax.axis_size(GY)
    block = lax.axis_size("xa")
    numbers = [lax.axis_index(GX), lax.axis_index(GY), jnp.int32(nx), jnp.int32(ny), lax.axis_index("xa"), lax.axis_index("ca")]
    spot = jnp.stack(numbers).astype(jnp.int32)

    fine = (4, ROWS, LANES)
    mid = (2, ROWS, LANES)
    tile = (4, 8, LANES)

    def room(*shape):
        return pltpu.VMEM(shape, F32)

    own, pairs = call(
        split_kernel, [HBM] * 3, [(4, 2, 4, 8, LANES), (8, LANES)],
        [
            pltpu.SMEM(conduct_table.shape, F32), pltpu.VMEM(labels.shape, jnp.int32), room(*right_side.shape),
            pltpu.SemaphoreType.DMA((3,)),
        ],
        *(pltpu.with_memory_space_constraint(value, pltpu.HBM) for value in (conduct_table, labels, right_side)),
    )
    ring = [(i, (i + 1) % ny) for i in range(ny)]
    low = lax.ppermute(own, GY, ring)
    high = lax.ppermute(own, GY, [(b, a) for a, b in ring])
    near = (4, NEAR_ROWS, LANES)
    far = (4, FAR_ROWS, LANES)
    wide, up1, down1, up2, down2 = call(
        join_kernel, [VMEM] * 3, [(4, 2) + fine, near, near, far, far], [], low, own, high
    )
    low1 = shifted(up1, GX, 1)
    high1 = shifted(down1, GX, -1)
    low2 = shifted(up2, GX, 2)
    high2 = shifted(down2, GX, -2)

    outs = call(
        up_kernel,
        [SMEM] + [VMEM] * 6,
        [
            (ny, 8, LANES), (2, 16, LANES), (8, LANES),
            (5,) + tile, (4,) + fine, (4,) + tile, (4,) + tile, (4,) + tile, (6,) + fine,
            (5,) + mid, (4,) + mid, (4,) + mid, (4,) + mid, (4,) + mid, (4,) + mid,
            (3, ROWS, LANES),
        ],
        [pltpu.VMEM((PLANES,) + fine, jnp.int32), room(PLANES, *fine)]
        + [room(PLANES, *fine)] * 3
        + [room(PLANES, ROWS, LANES)]
        + [room(PLANES, *fine)] * 4
        + [room(8, *mid)] * 3
        + [room(8, ROWS, LANES)]
        + [room(8, *mid)] * 5,
        spot, pairs, low2, low1, wide, high1, high2,
    )
    chunk, ends, edge = outs[:3]
    rows = lax.all_to_all(chunk, GY, 0, 0, tiled=True)
    other = swapped(ends)
    window = (block, 4 * SPAN + 32, LANES)
    (planes,) = call(
        window_kernel, [SMEM] + [VMEM] * 3, [window], [room(4 * SPAN, LANES)], spot, rows, ends, other
    )
    planes = lax.all_to_all(planes, "xa", 0, 0, tiled=True)
    planes, middle_rows = lax.optimization_barrier((planes, planes[:, : 4 * CORE]))
    took1 = parted(planes, 1)
    took2 = parted(middle_rows, 2)
    took1, took2, edge = lax.optimization_barrier((took1, took2, shifted_chip(edge)))
    gave = swapped(jnp.concatenate([took1, took2], axis=1))
    blocks = [took1, took2, planes, gave]
    (correction,) = call(
        down_kernel,
        [SMEM] + [VMEM] * 19,
        [(4, 8, 4 * LANES)],
        [
            room(4, 5 * block, ROWS, LANES), room(2, 5 * block, ROWS, LANES), room(5 * block, 16, LANES),
            room(6, *mid), room(4, *mid), room(6, *fine),
        ],
        spot, *blocks, other, edge, *outs[3:],
    )
    return correction


def solution(mesh):
    mesh = Mesh(mesh.devices.reshape(-1, 4, mesh.devices.shape[1] // 2, 2), GX + GY)
    spec = P(GX, GY, None)
    return jax.shard_map(shards, mesh=mesh, in_specs=(spec, spec, P()), out_specs=spec, check_vma=False)
```

```python
import jax
import jax.numpy as jnp
from jax import lax
from jax.experimental import pallas as pl
from jax.experimental.pallas import tpu as pltpu
from jax.sharding import Mesh
from jax.sharding import PartitionSpec as P

F32 = jnp.float32
LANES = 128
ROWS = 24
REACH = 7
PLANES = 4 + 2 * REACH
WINDOW = 8
SPAN = 20
CORE = 12
KEEP = 0.2
OMEGA = 0.8


def iota(shape, dim):
    return lax.broadcasted_iota(jnp.int32, shape, dim)


def pick(values, index):
    return jnp.take_along_axis(values, index, axis=1)


def lane_roll(value, shift):
    return pltpu.roll(value, shift % LANES, value.ndim - 1)


def row_roll(value, shift):
    return pltpu.roll(value, shift % value.shape[-2], value.ndim - 2)


def split_kernel(table_hbm, labels_hbm, source_hbm, out_ref, pairs_ref, table_ref, labels_ref, source_ref, done):
    copies = [
        pltpu.make_async_copy(src, dst, done.at[k])
        for k, (src, dst) in enumerate(
            ((table_hbm, table_ref), (labels_hbm, labels_ref), (source_hbm, source_ref)))
    ]
    for copy in copies:
        copy.start()
    for copy in copies:
        copy.wait()
    pairs_ref[...] = pair_table(table_ref)
    lane = iota((8, LANES), 1)
    for plane in range(4):
        labels = labels_ref[plane]
        code = jnp.where(labels == 0, 8.0, jnp.where(labels == 1, 9.0, 11.0)).astype(F32)
        source = source_ref[plane]
        for which, values in enumerate((code, source)):
            parts = [values[:, LANES * j : LANES * (j + 1)] for j in range(4)]
            for residue in range(4):
                index = 4 * (lane % 32) + residue
                moved = [pick(part, index) for part in parts]
                low = jnp.where(lane < 32, moved[0], moved[1])
                high = jnp.where(lane < 96, moved[2], moved[3])
                out_ref[plane, which, residue] = jnp.where(lane < 64, low, high)


def layout(first, last):
    spots = []
    offset = 0
    for which in range(2):
        for distance in range(first, last + 1 - which * (last == REACH)):
            reach = REACH - which - distance
            spots.append((which, distance, 8 - reach, 8 + 2 * reach, offset))
            offset += 8 + 2 * reach
    return spots, offset


NEAR, NEAR_ROWS = layout(1, 4)
FAR, FAR_ROWS = layout(5, REACH)


def join_kernel(low_ref, own_ref, high_ref, all_ref, up1_ref, down1_ref, up2_ref, down2_ref):
    for plane in range(4):
        for which in range(2):
            for residue in range(4):
                for part, ref in enumerate((low_ref, own_ref, high_ref)):
                    all_ref[plane, which, residue, pl.ds(8 * part, 8)] = ref[plane, which, residue]
    for spots, start, up_ref, down_ref in ((NEAR, 1, up1_ref, down1_ref), (FAR, 5, up2_ref, down2_ref)):
        for which, distance, row, rows, offset in spots:
            ahead = distance - start
            for residue in range(4):
                out = pl.ds(offset, rows)
                down_ref[residue, out] = all_ref[ahead, which, residue, pl.ds(row, rows)]
                up_ref[residue, out] = all_ref[3 - ahead, which, residue, pl.ds(row, rows)]


def middle_sum(fx_up, fx_low, fy, fz, v_up, v_low, v):
    lane = iota((ROWS, LANES), 1)
    total = fx_up * v_up + fx_low * v_low
    total = total + fy * row_roll(v, -2) + row_roll(fy * v, 2)
    last = jnp.where(lane == LANES - 1, 0.0, lane_roll(v[0], -1))
    first = jnp.where(lane == 0, 0.0, lane_roll(fz[1] * v[1], 1))
    return total + jnp.stack([first + fz[0] * v[1], fz[0] * v[0] + fz[1] * last])


def both_rows(value, bit):
    row = iota(value.shape, value.ndim - 2)
    return value + jnp.where((row & bit) == 0, row_roll(value, -bit), row_roll(value, bit))


def upper_row(value, bit):
    row = iota(value.shape, value.ndim - 2)
    return jnp.where((row & bit) != 0, value, row_roll(value, -bit))


def pair_table(table_ref):
    lane = iota((8, LANES), 1)

    def at(*keys):
        hit = lane == keys[0]
        for key in keys[1:]:
            hit = hit | (lane == key)
        return hit

    one = jnp.where(at(8, 16, 17, 19), table_ref[0], jnp.where(at(9, 18, 20), table_ref[1], jnp.where(at(11, 22), table_ref[2], 1.0)))
    two = jnp.where(at(8, 16), table_ref[0], jnp.where(at(9, 17, 18), table_ref[1], jnp.where(at(11, 19, 20, 22), table_ref[2], 1.0)))
    return 2.0 * (one * two) / (one + two)


def up_kernel(
    spot_ref, pairs_ref, low2_ref, low1_ref, own_ref, high1_ref, high2_ref,
    chunk_ref, ends_ref, edge_ref, fx_out, fy_out, fz_out, w_out, s_out, v_out,
    fxm_out, fym_out, fzm_out, wm_out, sm_out, vm_out, root_out,
    code, source, fx, fy, fz, zlow, diag, weight, first, second,
    fxm, fym, fzm, zlowm, diagm, weightm, sourcem, firstm, secondm,
):
    x0 = 4 * spot_ref[0]
    y0 = 8 * spot_ref[1]
    nx = 4 * spot_ref[2]
    ny = 8 * spot_ref[3]
    table = pairs_ref[...]
    blank = jnp.zeros((4, ROWS, LANES), F32)

    def in_grid(value, row):
        y = y0 - 8 + row + iota(value.shape, value.ndim - 2)
        return jnp.where((y >= 0) & (y < ny), value.astype(jnp.int32), 0)

    for k in range(4):
        code[REACH + k] = in_grid(own_ref[k, 0], 0)
        source[REACH + k] = own_ref[k, 1]
    for distance in range(1, REACH + 1):
        for p in (REACH - distance, REACH + 3 + distance):
            code[p] = blank.astype(jnp.int32)
            source[p] = blank
    for spots, low_ref, high_ref in ((NEAR, low1_ref, high1_ref), (FAR, low2_ref, high2_ref)):
        for which, distance, row, rows, offset in spots:
            for p, ref in ((REACH - distance, low_ref), (REACH + 3 + distance, high_ref)):
                for residue in range(4):
                    value = ref[residue, pl.ds(offset, rows)]
                    if which == 0:
                        code[p, residue, pl.ds(row, rows)] = in_grid(value, row)
                    else:
                        source[p, residue, pl.ds(row, rows)] = value

    row = iota((ROWS, LANES), 0)
    lane = iota((ROWS, LANES), 1)
    y = y0 - 8 + row
    rowmask = jnp.where((y >= 0) & (y < ny), 1.0, 0.0)

    def planemask(x):
        return jnp.where((x >= 0) & (x < nx), 1.0, 0.0).astype(F32)

    def look(key):
        flat = key.reshape(-1, LANES)
        parts = [pick(table, flat[8 * k : 8 * k + 8]) for k in range(flat.shape[0] // 8)]
        return jnp.concatenate(parts, axis=0).reshape(key.shape)

    def faces(p, carry):
        here = [code[p, r] for r in range(4)]
        after = here[1:] + [jnp.where(lane == LANES - 1, 0, lane_roll(here[0], -1))]
        for r in range(4):
            fx[p, r] = look(here[r] + code[p + 1, r])
            fy[p, r] = look(here[r] + row_roll(here[r], -1))
            across = look(here[r] + after[r])
            fz[p, r] = across
        zlow[p] = jnp.where(lane == 0, look(here[0]), lane_roll(across, 1))
        return carry

    lax.fori_loop(0, PLANES - 1, faces, 0, unroll=True)

    def start(p, carry):
        mask = (OMEGA * planemask(x0 - REACH + p)) * rowmask
        lower = zlow[p]
        for r in range(4):
            fy_here = fy[p, r]
            upper = fz[p, r]
            total = fx[p, r] + fx[p - 1, r] + fy_here + row_roll(fy_here, 1) + upper + lower
            lower = upper
            diag[p, r] = total
            w = mask / total
            weight[p, r] = w
            first[p, r] = w * source[p, r]
        return carry

    lax.fori_loop(1, PLANES - 1, start, 0, unroll=True)

    def image(field, p):
        v = [field[p, r] for r in range(4)]
        along = [fz[p, r] * v[r] for r in range(4)]
        below = [jnp.where(lane == 0, 0.0, lane_roll(along[3], 1))] + along[:3]
        above = v[1:] + [jnp.where(lane == LANES - 1, 0.0, lane_roll(v[0], -1))]
        sums = []
        for r in range(4):
            fy_here = fy[p, r]
            total = fx[p, r] * field[p + 1, r] + fx[p - 1, r] * field[p - 1, r]
            total = total + fy_here * row_roll(v[r], -1) + row_roll(fy_here * v[r], 1)
            sums.append(total + (below[r] + fz[p, r] * above[r]))
        return v, sums

    def sweep(p, carry):
        v, sums = image(first, p)
        for r in range(4):
            second[p, r] = KEEP * v[r] + weight[p, r] * (source[p, r] + sums[r])
        return carry

    lax.fori_loop(2, PLANES - 2, sweep, 0, unroll=True)

    def halves(value):
        return jnp.stack([value[0] + value[1], value[2] + value[3]])

    def residual(p):
        v, sums = image(second, p)
        return jnp.stack([source[p, r] - diag[p, r] * v[r] + sums[r] for r in range(4)])

    def coarse_face(k, carry):
        fxm[k] = both_rows(halves(fx[2 + 2 * k]), 1)
        return carry

    lax.fori_loop(0, 7, coarse_face, 0, unroll=True)

    def middle(k, carry):
        pa = 1 + 2 * k
        pb = 2 + 2 * k
        sm = both_rows(halves(residual(pa) + residual(pb)), 1)
        fym_here = upper_row(halves(fy[pa] + fy[pb]), 1)
        fz_two = fz[pa] + fz[pb]
        fzm_here = both_rows(jnp.stack([fz_two[1], fz_two[3]]), 1)
        zlow_here = both_rows(zlow[pa] + zlow[pb], 1)
        lower = jnp.stack([zlow_here, fzm_here[0]])
        total = fxm[k] + fxm[k - 1] + fym_here + row_roll(fym_here, 2) + fzm_here + lower
        w = (OMEGA * planemask(x0 - REACH + pa) * rowmask) / total
        fym[k] = fym_here
        fzm[k] = fzm_here
        zlowm[k] = zlow_here
        diagm[k] = total
        weightm[k] = w
        sourcem[k] = sm
        firstm[k] = w * sm
        return carry

    lax.fori_loop(1, 7, middle, 0, unroll=True)

    def middle_sweep(k, carry):
        v = firstm[k]
        near = middle_sum(fxm[k], fxm[k - 1], fym[k], fzm[k], firstm[k + 1], firstm[k - 1], v)
        secondm[k] = KEEP * v + weightm[k] * (sourcem[k] + near)
        return carry

    lax.fori_loop(2, 6, middle_sweep, 0, unroll=True)

    coarse_source = jnp.zeros((ROWS, LANES), F32)
    for k in (3, 4):
        v = secondm[k]
        near = middle_sum(fxm[k], fxm[k - 1], fym[k], fzm[k], secondm[k + 1], secondm[k - 1], v)
        left = sourcem[k] - diagm[k] * v + near
        coarse_source = coarse_source + left[0] + left[1]
    coarse_source = both_rows(coarse_source, 2)

    def xface(big):
        value = fxm[2 * big + 4]
        return both_rows(value[0] + value[1], 2)

    xfaces = {big: xface(big) for big in (-2, -1, 0, 1)}
    roots = {}
    keep = None
    for big in (-1, 0, 1):
        ka = 2 * big + 3
        ysum = fym[ka] + fym[ka + 1]
        yface = upper_row(ysum[0] + ysum[1], 2)
        zsum = fzm[ka] + fzm[ka + 1]
        zface = both_rows(zsum[1], 2)
        zbelow = both_rows(zlowm[ka] + zlowm[ka + 1], 2)
        total = xfaces[big] + xfaces[big - 1] + yface + row_roll(yface, 4) + zface + zbelow
        root = lax.rsqrt(total) * (planemask(x0 + 4 * big) * rowmask)
        roots[big] = root
        root_out[big + 1] = root
        if big == 0:
            keep = (yface, zface)
    root = roots[0]
    cx = OMEGA * xfaces[0] * root * roots[1]
    cy = OMEGA * keep[0] * root * row_roll(root, -4)
    cz = OMEGA * keep[1] * root * jnp.where(lane == LANES - 1, 0.0, lane_roll(root, -1))
    lines = []
    for value in (OMEGA * root * coarse_source, cx, cy, cz):
        lines.append(value[8:9])
        lines.append(value[12:13])
    chunk = jnp.concatenate(lines, axis=0)
    for peer in range(chunk_ref.shape[0]):
        chunk_ref[peer] = chunk
    first_core = spot_ref[5] == 0

    def edges(sibling):
        rows = []
        for k in (3, 4):
            for half in range(2):
                low = secondm[k, half, 10:11]
                high = secondm[k, half, 12:13]
                rows.append(jnp.where(first_core == sibling, high, low))
        return rows

    edge_ref[...] = jnp.concatenate(edges(False) + [jnp.zeros((4, LANES), F32)], axis=0)
    inside_chip = edges(True)
    for k, other in ((3, 4), (4, 3)):
        lines = [secondm[k, half, 8 + 2 * m : 9 + 2 * m] for half in range(2) for m in range(4)]
        lines += [secondm[other, half, at_row : at_row + 1] for at_row in (6, 16) for half in range(2)]
        lines += [root[at_row : at_row + 1] for at_row in (4, 16)]
        lines += inside_chip[2 * (k - 3) : 2 * (k - 2)]
        ends_ref[k - 3] = jnp.concatenate(lines, axis=0)

    own_rows = pl.ds(8, 8)
    for k in range(5):
        fx_out[k] = fx[REACH - 1 + k, :, own_rows]
        fxm_out[k] = fxm[1 + k]
    for k in range(4):
        p = REACH + k
        fy_out[k] = fy[p]
        fz_out[k] = fz[p, :, own_rows]
        w_out[k] = weight[p, :, own_rows]
        s_out[k] = source[p, :, own_rows]
        fym_out[k] = fym[2 + k]
        fzm_out[k] = fzm[2 + k]
        wm_out[k] = weightm[2 + k]
        sm_out[k] = sourcem[2 + k]
        vm_out[k] = secondm[2 + k]
    for k in range(6):
        v_out[k] = second[REACH - 1 + k]


def window_kernel(spot_ref, got_ref, ends_ref, other_ref, out_ref, chunk):
    place = spot_ref[4]
    core = spot_ref[5]
    base = spot_ref[1] - core
    count = got_ref.shape[0]
    for step in range(SPAN // 2):
        block = base + (step - 4)
        inside = jnp.where((block >= 0) & (block < count), 1.0, 0.0).astype(F32)
        value = got_ref[jnp.clip(block, 0, count - 1), pl.ds(0, 8)] * inside
        for which in range(4):
            if 2 <= step < 8:
                at = CORE * which + 2 * step - 4
            else:
                at = 4 * CORE + (SPAN - CORE) * which + (2 * step if step < 2 else 2 * step - CORE)
            chunk[pl.ds(at, 2)] = value[2 * which : 2 * which + 2]
    body = chunk[...]
    size = out_ref.shape[0]
    first = (core == 0).astype(F32)
    for peer in range(size):
        out_ref[peer, pl.ds(0, 4 * SPAN)] = body
        ahead = (lax.rem(peer - place + size, size) == 1).astype(F32)
        mine = ends_ref[0] * ahead + ends_ref[1] * (1.0 - ahead)
        other = other_ref[0] * ahead + other_ref[1] * (1.0 - ahead)
        out_ref[peer, pl.ds(4 * SPAN, 16)] = mine * first + other * (1.0 - first)
        out_ref[peer, pl.ds(4 * SPAN + 16, 16)] = other * first + mine * (1.0 - first)


def down_kernel(
    spot_ref, took1_ref, took2_ref, mid_ref, gave_ref, other_ref, edge_ref, fx, fy, fz, w, s, v2,
    fxm, fym, fzm, wm, sm, vm, root,
    out_ref,
    parts, state, ends, field, third, total,
):
    place = spot_ref[4]
    width = 2 * WINDOW + 1
    lane = iota((ROWS, LANES), 1)
    row = iota((ROWS, LANES), 0)

    lower_core = spot_ref[5] == 0
    block = mid_ref.shape[0]
    gave1_ref = gave_ref.at[:, pl.ds(0, 4 * SPAN + 32)]
    gave2_ref = gave_ref.at[:, pl.ds(4 * SPAN + 32, 4 * CORE)]
    sources = (
        (took2_ref, gave2_ref), (took1_ref, gave1_ref), (mid_ref, None), (gave1_ref, took1_ref), (gave2_ref, took2_ref)
    )
    for number, (one, two) in enumerate(sources):
        for plane in range(block):
            at = number * block + plane

            def read(first, rows):
                value = one[plane, pl.ds(first, rows)]
                if two is not None:
                    value = jnp.where(lower_core, value, two[plane, pl.ds(first, rows)])
                return value

            blank = jnp.zeros((4, LANES), F32)
            for which in range(4):
                below = above = blank
                if 0 < number < 4:
                    outer = read(4 * CORE + (SPAN - CORE) * which, SPAN - CORE)
                    below, above = outer[:4], outer[4:]
                value = jnp.concatenate([below, read(CORE * which, CORE), above, blank], axis=0)
                parts[which, at] = value
                if which == 0:
                    state[0, at] = value
            if 0 < number < 4:
                ends[at] = jnp.where(lower_core, read(4 * SPAN, 16), read(4 * SPAN + 16, 16))

    for turn in range(1, WINDOW):
        old = (turn - 1) % 2
        new = turn % 2
        for step in range(turn, width - turn):
            here = place + step
            v = state[old, here]
            cy = parts[2, here]
            cz = parts[3, here]
            value = KEEP * v + parts[0, here]
            value = value + parts[1, here] * state[old, here + 1] + parts[1, here - 1] * state[old, here - 1]
            value = value + cy * row_roll(v, -1) + row_roll(cy * v, 1)
            value = value + cz * lane_roll(v, -1) + lane_roll(cz * v, 1)
            state[new, here] = value

    def swap_rows(value, line, first, stop):
        return jnp.where((row >= first) & (row < stop), jnp.broadcast_to(line, (ROWS, LANES)), value)

    def corners(value, at):
        halves = []
        for half in range(2):
            part = swap_rows(value[half], ends[at, pl.ds(8 + half, 1)], 6, 8)
            halves.append(swap_rows(part, ends[at, pl.ds(10 + half, 1)], 16, 18))
        return jnp.stack(halves)

    last = (WINDOW - 1) % 2
    spread = []
    for big in range(3):
        value = state[last, place + WINDOW - 1 + big]
        picked = jnp.zeros((ROWS, LANES), F32)
        for k in range(4):
            line = jnp.where(lower_core, value[7 + k : 8 + k], value[9 + k : 10 + k])
            line = jnp.broadcast_to(line, (ROWS, LANES))
            picked = jnp.where((row >= 4 + 4 * k) & (row < 8 + 4 * k), line, picked)
        scale = root[big]
        if big != 1:
            beside = place + WINDOW - 1 + big
            scale = swap_rows(scale, ends[beside, pl.ds(12, 1)], 4, 8)
            scale = swap_rows(scale, ends[beside, pl.ds(13, 1)], 16, 20)
        spread.append(picked * scale)

    def line_block(at):
        halves = []
        for half in range(2):
            rows = []
            for m in range(4):
                line = ends[at, pl.ds(4 * half + m, 1)]
                rows += [line, line]
            pad = jnp.zeros((8, LANES), F32)
            halves.append(jnp.concatenate([pad] + [jnp.concatenate(rows, axis=0)] + [pad], axis=0))
        return jnp.stack(halves)

    field[0] = line_block(place + WINDOW - 1) + spread[0]
    field[5] = line_block(place + WINDOW + 1) + spread[2]
    field[1] = corners(vm[0], place + WINDOW - 1) + spread[0]
    field[4] = corners(vm[3], place + WINDOW + 1) + spread[2]
    for k in range(2):
        halves = []
        for half in range(2):
            value = vm[1 + k, half]
            sibling = other_ref[k, pl.ds(14 + half, 1)]
            beyond = edge_ref[pl.ds(2 * k + half, 1)]
            lower = jnp.where(lower_core, beyond, sibling)
            upper = jnp.where(lower_core, sibling, beyond)
            halves.append(swap_rows(swap_rows(value, lower, 4, 6), upper, 18, 20))
        field[2 + k] = jnp.stack(halves) + spread[1]

    for k in range(4):
        v = field[k + 1]
        image = middle_sum(fxm[k + 1], fxm[k], fym[k], fzm[k], field[k + 2], field[k], v)
        third[k] = KEEP * v + wm[k] * (sm[k] + image)

    for p in range(6):
        mid = third[(p + 1) // 2]
        total[p] = v2[p] + jnp.stack([mid[0], mid[0], mid[1], mid[1]])

    lane8 = iota((8, LANES), 1)
    for p in range(4):
        up = total[p + 2, :, pl.ds(8, 8)]
        low = total[p, :, pl.ds(8, 8)]
        v = total[p + 1, :, pl.ds(8, 8)]
        image = fx[p + 1] * up + fx[p] * low
        image = image + fy[p, :, pl.ds(8, 8)] * total[p + 1, :, pl.ds(9, 8)]
        image = image + fy[p, :, pl.ds(7, 8)] * total[p + 1, :, pl.ds(7, 8)]
        zc = fz[p]
        end = jnp.where(lane8 == LANES - 1, 0.0, lane_roll(v[0], -1))
        begin = jnp.where(lane8 == 0, 0.0, lane_roll(zc[3] * v[3], 1))
        below_z = [begin, zc[0] * v[0], zc[1] * v[1], zc[2] * v[2]]
        above_z = [zc[0] * v[1], zc[1] * v[2], zc[2] * v[3], zc[3] * end]
        done = []
        for r in range(4):
            done.append(KEEP * v[r] + w[p, r] * (s[p, r] + image[r] + below_z[r] + above_z[r]))
        for j in range(4):
            index = 32 * j + lane8 // 4
            moved = [pick(done[r], index) for r in range(4)]
            odd = lane8 % 4
            low_pair = jnp.where(odd == 0, moved[0], moved[1])
            high_pair = jnp.where(odd == 2, moved[2], moved[3])
            out_ref[p, :, LANES * j : LANES * (j + 1)] = jnp.where(odd < 2, low_pair, high_pair)


VMEM = pl.BlockSpec(memory_space=pltpu.VMEM)
SMEM = pl.BlockSpec(memory_space=pltpu.SMEM)
HBM = pl.BlockSpec(memory_space=pltpu.HBM)
PARAMS = pltpu.CompilerParams(vmem_limit_bytes=48 * 1024 * 1024)
GX = ("ya", "xa")
GY = ("za", "ca")


def call(kernel, specs, outs, scratch, *args):
    return pl.pallas_call(
        kernel,
        in_specs=specs,
        out_specs=[VMEM] * len(outs),
        out_shape=[jax.ShapeDtypeStruct(shape, F32) for shape in outs],
        scratch_shapes=scratch,
        compiler_params=PARAMS,
    )(*args)


def shifted(value, axis, step):
    count = lax.axis_size(axis)
    if step > 0:
        pairs = [(i, i + step) for i in range(count - step)]
    else:
        pairs = [(i - step, i) for i in range(count + step)]
    return lax.ppermute(value, axis, pairs)


def parted(value, step):
    pairs = []
    for i in range(lax.axis_size("ya") - step):
        pairs.append((2 * i, 2 * (i + step)))
        pairs.append((2 * (i + step) + 1, 2 * i + 1))
    return lax.ppermute(value, ("ya", "ca"), pairs)


def shifted_chip(value):
    count = lax.axis_size(GY)
    ring = [(i, (i + 1) % count) for i in range(count)]
    low = lax.ppermute(value, GY, ring)
    high = lax.ppermute(value, GY, [(b, a) for a, b in ring])
    place = lax.axis_index(GY)
    kept = jnp.where(lax.axis_index("ca") == 0, low, high)
    return jnp.where((place > 0) & (place < count - 1), kept, 0.0)


def swapped(value):
    return lax.ppermute(value, "ca", [(0, 1), (1, 0)])


def shards(right_side, labels, conduct_table):
    nx = lax.axis_size(GX)
    ny = lax.axis_size(GY)
    block = lax.axis_size("xa")
    numbers = [lax.axis_index(GX), lax.axis_index(GY), jnp.int32(nx), jnp.int32(ny), lax.axis_index("xa"), lax.axis_index("ca")]
    spot = jnp.stack(numbers).astype(jnp.int32)

    fine = (4, ROWS, LANES)
    mid = (2, ROWS, LANES)
    tile = (4, 8, LANES)

    def room(*shape):
        return pltpu.VMEM(shape, F32)

    own, pairs = call(
        split_kernel, [HBM] * 3, [(4, 2, 4, 8, LANES), (8, LANES)],
        [
            pltpu.SMEM(conduct_table.shape, F32), pltpu.VMEM(labels.shape, jnp.int32), room(*right_side.shape),
            pltpu.SemaphoreType.DMA((3,)),
        ],
        *(pltpu.with_memory_space_constraint(value, pltpu.HBM) for value in (conduct_table, labels, right_side)),
    )
    ring = [(i, (i + 1) % ny) for i in range(ny)]
    low = lax.ppermute(own, GY, ring)
    high = lax.ppermute(own, GY, [(b, a) for a, b in ring])
    near = (4, NEAR_ROWS, LANES)
    far = (4, FAR_ROWS, LANES)
    wide, up1, down1, up2, down2 = call(
        join_kernel, [VMEM] * 3, [(4, 2) + fine, near, near, far, far], [], low, own, high
    )
    low1 = shifted(up1, GX, 1)
    high1 = shifted(down1, GX, -1)
    low2 = shifted(up2, GX, 2)
    high2 = shifted(down2, GX, -2)

    outs = call(
        up_kernel,
        [SMEM] + [VMEM] * 6,
        [
            (ny, 8, LANES), (2, 16, LANES), (8, LANES),
            (5,) + tile, (4,) + fine, (4,) + tile, (4,) + tile, (4,) + tile, (6,) + fine,
            (5,) + mid, (4,) + mid, (4,) + mid, (4,) + mid, (4,) + mid, (4,) + mid,
            (3, ROWS, LANES),
        ],
        [pltpu.VMEM((PLANES,) + fine, jnp.int32), room(PLANES, *fine)]
        + [room(PLANES, *fine)] * 3
        + [room(PLANES, ROWS, LANES)]
        + [room(PLANES, *fine)] * 4
        + [room(8, *mid)] * 3
        + [room(8, ROWS, LANES)]
        + [room(8, *mid)] * 5,
        spot, pairs, low2, low1, wide, high1, high2,
    )
    chunk, ends, edge = outs[:3]
    rows = lax.all_to_all(chunk, GY, 0, 0, tiled=True)
    other = swapped(ends)
    window = (block, 4 * SPAN + 32, LANES)
    (planes,) = call(
        window_kernel, [SMEM] + [VMEM] * 3, [window], [room(4 * SPAN, LANES)], spot, rows, ends, other
    )
    planes = lax.all_to_all(planes, "xa", 0, 0, tiled=True)
    planes, middle_rows = lax.optimization_barrier((planes, planes[:, : 4 * CORE]))
    took1 = parted(planes, 1)
    took2 = parted(middle_rows, 2)
    took1, took2, edge = lax.optimization_barrier((took1, took2, shifted_chip(edge)))
    gave = swapped(jnp.concatenate([took1, took2], axis=1))
    blocks = [took1, took2, planes, gave]
    (correction,) = call(
        down_kernel,
        [SMEM] + [VMEM] * 19,
        [(4, 8, 4 * LANES)],
        [
            room(4, 5 * block, ROWS, LANES), room(2, 5 * block, ROWS, LANES), room(5 * block, 16, LANES),
            room(6, *mid), room(4, *mid), room(6, *fine),
        ],
        spot, *blocks, other, edge, *outs[3:],
    )
    return correction


def solution(mesh):
    mesh = Mesh(mesh.devices.reshape(-1, 4, mesh.devices.shape[1] // 2, 2), GX + GY)
    spec = P(GX, GY, None)
    return jax.shard_map(shards, mesh=mesh, in_specs=(spec, spec, P()), out_specs=spec, check_vma=False)
```
